32 devices in a mesh: dp: 16 (over z, y, x), scale: 2 (over core).
Axes of the slice: x: 2, y: 2, z: 4, core: 2. Of those that a mesh axis runs over, the one named last changes fastest.
Arguments:
- noise_maps: bfloat16 [32, 256, 256], P(('dp', 'scale')), may hold values from -6 to 6
- dataset_lowres_images: bfloat16 [64, 3, 1024], P(('dp', 'scale')), may hold values from -1 to 1
- dataset_highres_images: bfloat16 [32, 3, 4096], P(('dp', 'scale')), may hold values from -1 to 1
- occupied_mask: int32 [32, 4], P(('dp', 'scale')), may hold values from 0 to 1, as said below
- shift_amounts: int32 [32, 4, 2], P(('dp', 'scale')), may hold values from -4 to 4
- mirror_indicator: int32 [32, 4], P(('dp', 'scale')), may hold values 0 or 1
- erase_box_corner: int32 [32, 4, 2], P(('dp', 'scale')), may hold values from 0 to 16
- update_ordinal: int32 [1], replicated, may hold values from 2 to 20
- fixed_backbone_params: bfloat16 [240544], P(('dp', 'scale'))
- singular_estimate_dirs: float32 [960], replicated, may hold values from -6 to 6
- maker_weight_arrays: float32 [9699328], P(('dp', 'scale'))
- maker_mean_estimate: float32 [9699328], P(('dp', 'scale')), may hold values from -0.0034179688 to 0.0034179688
- maker_variance_estimate: float32 [9699328], P(('dp', 'scale')), may hold values from 4.8828124e-08 to 1.953125e-07
- judge_weight_arrays: float32 [348160], P(('dp', 'scale'))
- judge_mean_estimate: float32 [348160], P(('dp', 'scale')), may hold values from -0.00390625 to 0.00390625
- judge_variance_estimate: float32 [348160], P(('dp', 'scale')), may hold values from 7.6293944e-08 to 3.0517577e-07
- output_weight_rows: float32 [2496], replicated
- output_mean_estimate: float32 [2496], replicated, may hold values from -0.046875 to 0.046875
- output_variance_estimate: float32 [2496], replicated, may hold values from 2e-06 to 8e-06
Outputs:
- gen_new: float32 [9699328], P(('dp', 'scale'))
- gen_first_new: float32 [9699328], P(('dp', 'scale'))
- gen_second_new: float32 [9699328], P(('dp', 'scale'))
- crit_new: float32 [348160], P(('dp', 'scale'))
- crit_first_new: float32 [348160], P(('dp', 'scale'))
- crit_second_new: float32 [348160], P(('dp', 'scale'))
- head_new: float32 [2496], replicated
- head_first_new: float32 [2496], replicated
- head_second_new: float32 [2496], replicated
- losses: float32 [2], replicated
- power_new: float32 [960], replicated
The draws below stay inside these ranges and needn't reach their ends.
Inputs may be any that keep to these rules, and one draw needn't show every extreme that they name: `occupied_mask`: each device holds 1 generated slots, then 2 small and 1 large real slots; the first generated slot and the first small real slot of every device are live.
All inputs are finite; a program needn't handle non-finite values. No bound on the sum of `mirror_indicator` on one device may be relied on, other than what follows from the above.
Results may differ from the reference program's by a relative error of at most 0.00085.
The reference program's roundings to bfloat16 on the way count: a program that leaves them out, or rounds other values in their place, can miss the bound.
Values may be sent and summed in bfloat16 or wider, within the bound.
No kernel may reach another device: no remote copies, remote signals or barrier semaphores. Data moves between devices by JAX's collectives and lax.ppermute only.
A program may use at most 256 MiB of HBM per device.

```python
import math
import jax
import jax.numpy as jnp
from jax import lax

S = 32
SYNTH_IMAGES = 1
TRUE_LOW_RES = 2
REAL_L = 1
Z = 256
GIN = 1024
GOUT = 512
C1 = 24
C2 = 40
C3 = 112
C4 = 320
K1 = 64
K2 = 128
K3 = 256
K4 = 512
SLOTS = 4
UNITS = 960
GPAR = 9699328
DPAR = 348160
HEADS = 2496
FROZEN = 240544
DEVICES = 32


def segment_scales(total, lengths, factors):
    places = jnp.arange(total)
    scales = jnp.full((total,), 1.0, jnp.float32)
    bound_low = 0
    for length, factor in zip(lengths, factors):
        inside = (places >= bound_low) & (places < bound_low + length)
        scales = jnp.where(inside, jnp.float32(factor), scales)
        bound_low = bound_low + length
    return scales


def draw_occupied_mask(key, part):
    coins = jax.random.randint(key, (DEVICES, SLOTS), 0, 2)
    places = jnp.arange(SLOTS)
    forced = (places == 0) | (places == SYNTH_IMAGES)
    return jnp.where(forced[None, :], 1, coins).astype(jnp.int32)


def draw_maker_weight_arrays(key, part):
    values = jax.random.normal(key, (GPAR,), jnp.float32)
    return values * segment_scales(GPAR, [Z * GIN, 9 * GIN * 2 * GOUT], [Z ** (-0.5), (9 * GIN) ** (-0.5)])


def draw_judge_weight_arrays(key, part):
    values = jax.random.normal(key, (DPAR,), jnp.float32)
    return values * segment_scales(DPAR, [K1 * K1, K2 * K2, K3 * K3, K4 * K4], [K1 ** (-0.5), K2 ** (-0.5), K3 ** (-0.5), K4 ** (-0.5)])


def draw_output_weight_rows(key, part):
    values = jax.random.normal(key, (HEADS,), jnp.float32)
    return values * segment_scales(HEADS, [UNITS, 3 * GOUT], [1.0, 3.0 * GOUT ** (-0.5)])


def draw_fixed_backbone_params(key, part):
    values = jax.random.normal(key, (FROZEN,), jnp.float32)
    lengths = [3 * C1, C1 * C2, C2 * C3, C3 * C4, C1 * K1, C2 * K2, C3 * K3, C4 * K4]
    factors = [3 ** (-0.5), C1 ** (-0.5), C2 ** (-0.5), C3 ** (-0.5), C1 ** (-0.5), C2 ** (-0.5), C3 ** (-0.5), C4 ** (-0.5)]
    return (values * segment_scales(FROZEN, lengths, factors)).astype(jnp.bfloat16)


def set_ends(array, own_key, low, largest):
    shape = array.shape
    index_at = [jax.random.randint(jax.random.fold_in(own_key, axis), (), 0, shape[axis]) for axis in range(len(shape))]
    array = array.at[tuple(index_at)].set(low)
    longest = shape.index(max(shape))
    index_at[longest] = (index_at[longest] + 1) % shape[longest]
    return array.at[tuple(index_at)].set(largest)


def steps_of(rng, shape, shards, least, top_value):
    level, own = 1.0, jax.random.fold_in(rng, 6)
    for position, blocks in shards:
        steps = jnp.exp(jax.random.uniform(jax.random.fold_in(own, position), (blocks,), jnp.float32, least / len(shards), top_value / len(shards)))
        level = level * jnp.repeat(steps, shape[position] // blocks).reshape([-1 if axis == position else 1 for axis in range(len(shape))])
    return level


def scatter_about(rng, shape, scale, most, split=(), held_as=jnp.bfloat16):
    loudness = steps_of(rng, shape, split, -0.22, 0.18) if split else 1.0
    entries = jax.random.normal(rng, shape, jnp.float32) * scale * loudness
    return jnp.minimum(jnp.maximum(entries, -most), most).astype(held_as)


def setup_inputs(seed: int = 0) -> dict:
    seeds = jax.random.split(jax.random.key(seed), 20)
    return {
        "noise_maps": scatter_about(seeds[0], (DEVICES * SYNTH_IMAGES, Z, S * S // 4), 1.0, 6.0, ((0, 32),)),
        "dataset_lowres_images": jnp.clip(jax.random.uniform(seeds[1], (DEVICES * TRUE_LOW_RES, 3, S * S), jnp.float32, -1.0, 1.0) * steps_of(seeds[1], (DEVICES * TRUE_LOW_RES, 3, S * S), ((0, 32),), -0.4, 0.0), -1.0, 1.0).astype(jnp.bfloat16),
        "dataset_highres_images": jnp.clip(jax.random.uniform(seeds[2], (DEVICES * REAL_L, 3, 4 * S * S), jnp.float32, -1.0, 1.0) * steps_of(seeds[2], (DEVICES * REAL_L, 3, 4 * S * S), ((0, 32),), -0.4, 0.0), -1.0, 1.0).astype(jnp.bfloat16),
        "occupied_mask": draw_occupied_mask(jax.random.fold_in(seeds[19], 71), 0),
        "shift_amounts": set_ends(jax.random.randint(seeds[4], (DEVICES, SLOTS, 2), 0 - S // 8, S // 8 + 1), jax.random.fold_in(seeds[4], 1), 0 - S // 8, (S // 8 + 1) - 1).astype(jnp.int32),
        "mirror_indicator": set_ends((jax.random.randint(seeds[5], (DEVICES, SLOTS), 0, 2) < 1).astype(jnp.int32), jax.random.fold_in(seeds[5], 1), 0, 1),
        "erase_box_corner": set_ends(jax.random.randint(seeds[6], (DEVICES, SLOTS, 2), 0, S // 2 + 1), jax.random.fold_in(seeds[6], 1), 0, (S // 2 + 1) - 1).astype(jnp.int32),
        "update_ordinal": jax.random.randint(seeds[7], (1,), 2, 21).astype(jnp.int32),
        "fixed_backbone_params": draw_fixed_backbone_params(jax.random.fold_in(seeds[19], 71), 0),
        "singular_estimate_dirs": scatter_about(seeds[9], (UNITS,), 1.0, 6.0, (), jnp.float32),
        "maker_weight_arrays": draw_maker_weight_arrays(jax.random.fold_in(seeds[19], 71), 0),
        "maker_mean_estimate": scatter_about(seeds[11], (GPAR,), (0.04 / (S * (SYNTH_IMAGES * DEVICES) ** 0.5)), 0.0034179688, ((0, 32),), jnp.float32),
        "maker_variance_estimate": jnp.clip(jnp.exp(math.log(1.9531249506599124e-07) - 1.3862944 * jax.random.uniform(seeds[12], (GPAR,), jnp.float32) ** steps_of(seeds[12], (GPAR,), ((0, 32),), -0.2, 0.2)), 4.882812376649781e-08, 1.9531249506599124e-07),
        "judge_weight_arrays": draw_judge_weight_arrays(jax.random.fold_in(seeds[19], 71), 0),
        "judge_mean_estimate": scatter_about(seeds[14], (DPAR,), (0.1 / (S * (SLOTS * DEVICES) ** 0.5)), 0.00390625, ((0, 32),), jnp.float32),
        "judge_variance_estimate": jnp.clip(jnp.exp(math.log(3.0517577442878974e-07) - 1.3862944 * jax.random.uniform(seeds[15], (DPAR,), jnp.float32) ** steps_of(seeds[15], (DPAR,), ((0, 32),), -0.2, 0.2)), 7.629394360719743e-08, 3.0517577442878974e-07),
        "output_weight_rows": draw_output_weight_rows(jax.random.fold_in(seeds[19], 71), 0),
        "output_mean_estimate": scatter_about(seeds[17], (HEADS,), 0.003, 0.046875, (), jnp.float32),
        "output_variance_estimate": jnp.clip(jnp.exp(jax.random.uniform(seeds[18], (HEADS,), jnp.float32, math.log(1.9999999949504854e-06), math.log(7.999999979801942e-06))), 1.9999999949504854e-06, 7.999999979801942e-06),
    }


@jax.custom_vjp
def low(v):
    return lax.optimization_barrier(v.astype(jnp.bfloat16)).astype(jnp.float32)

@jax.custom_vjp
def low_back(v):
    return v

def low_keep(v):
    return (low(v), None)

def low_pass(kept, grad):
    return (grad,)

def back_keep(v):
    return (v, None)

def back_low(kept, grad):
    return (low(grad),)
low.defvjp(low_keep, low_pass)
low_back.defvjp(back_keep, back_low)
highest = lax.Precision.HIGHEST
leak_slope = 0.2
learn_rate = 0.03
beta_first = 0.5
beta_second = 0.5
adam_epsilon = 1e-08
weight_decay = 0.0001
norm_epsilon = 1e-06

def product(left_side, right_side):
    return jnp.dot(left_side, right_side, precision=highest, preferred_element_type=jnp.float32)

def carve_flat(flat_array, layouts):
    segments = []
    offset = 0
    for layout in layouts:
        length = 1
        for extent in layout:
            length = length * extent
        segments.append(flat_array[offset:offset + length].reshape(layout))
        offset = offset + length
    return segments

def frozen_layouts():
    return [(3, C1), (C1, C2), (C2, C3), (C3, C4), (C1, K1), (C2, K2), (C3, K3), (C4, K4)]

def critic_layouts():
    return [(K1, K1), (K2, K2), (K3, K3), (K4, K4)]

def vector_layouts():
    return [(K1,), (K2,), (K3,), (K4,)]

def normalize(vector):
    return vector * lax.rsqrt(jnp.sum(vector * vector) + norm_epsilon)

def pooled(feature_map):
    height, breadth = (feature_map.shape[-2], feature_map.shape[-1])
    grouped = feature_map.reshape(feature_map.shape[:-2] + (height // 2, 2, breadth // 2, 2))
    return lax.optimization_barrier(jnp.mean(grouped, axis=(-3, -1)))

def doubled(feature_map):
    return jnp.repeat(jnp.repeat(feature_map, 2, axis=-2), 2, axis=-1)

def shift_stack(feature_map):
    height, breadth = (feature_map.shape[-2], feature_map.shape[-1])
    padding = [(0, 0)] * (feature_map.ndim - 2) + [(1, 1), (1, 1)]
    padded = jnp.pad(feature_map, padding)
    segments = [padded[..., down_at:down_at + height, across_at:across_at + breadth] for down_at in range(3) for across_at in range(3)]
    return jnp.concatenate(segments, axis=0).reshape(9 * feature_map.shape[0], -1)

def augment_tables(shift_pair, flip_flag, corner_pair):
    places = jnp.arange(S, dtype=jnp.int32)
    down_table = (places[:, None] - shift_pair[0] == places[None, :]).astype(jnp.float32)
    moved_at = places - shift_pair[1]
    inside = (moved_at >= 0) & (moved_at < S)
    source = jnp.where(flip_flag == 1, S - 1 - moved_at, moved_at)
    across_table = ((source[:, None] == places[None, :]) & inside[:, None]).astype(jnp.float32)
    rows_in = (places >= corner_pair[0]) & (places < corner_pair[0] + S // 2)
    cols_in = (places >= corner_pair[1]) & (places < corner_pair[1] + S // 2)
    keep_mask = jnp.float32(1.0) - (rows_in[:, None] & cols_in[None, :]).astype(jnp.float32)
    return (down_table, across_table, keep_mask)

def apply_tables(image, tables):
    down_table, across_table, keep_mask = tables
    return jnp.einsum('ij,cjk,lk->cil', down_table, image, across_table, precision=highest) * keep_mask

def critic_logits(image, extract, project, matrices, sigmas, unit_heads):
    feature_map = image
    logits = []
    for section_index in range(4):
        inputs = low(pooled(feature_map))
        channels, height, breadth = inputs.shape
        pre_act = low_back(product(extract[section_index].T, inputs.reshape(channels, height * breadth)))
        active = jax.nn.silu(pre_act)
        features = low_back(product(project[section_index].T, low(active)))
        raw_score = low_back(product(matrices[section_index].T, low(features)))
        scaled = raw_score / sigmas[section_index]
        leaky_out = jnp.where(scaled >= 0, scaled, leak_slope * scaled)
        logits.append(product(unit_heads[section_index][None, :], leaky_out)[0])
        feature_map = active.reshape(active.shape[0], height, breadth)
    return logits

def generate(conv_first, conv_second, rgb_weight, latent):
    pre_hidden = low_back(product(conv_first.T, latent))
    hidden = low(jax.nn.silu(pre_hidden)).reshape(GIN, S // 2, S // 2)
    mixed_pre = low_back(product(conv_second.T, shift_stack(doubled(hidden))))
    gated_out = mixed_pre[:GOUT] * jax.nn.sigmoid(mixed_pre[GOUT:])
    return jnp.tanh(product(rgb_weight.T, gated_out)).reshape(3, S, S)

def adamw_update(master, first, second, grad_full, step_number):
    first_new = beta_first * first + (1.0 - beta_first) * grad_full
    second_new = beta_second * second + (1.0 - beta_second) * grad_full * grad_full
    first_fix = 1.0 - jnp.power(jnp.float32(beta_first), step_number)
    second_fix = 1.0 - jnp.power(jnp.float32(beta_second), step_number)
    update = first_new / first_fix / (jnp.sqrt(second_new / second_fix) + adam_epsilon)
    return (master - learn_rate * (update + weight_decay * master), first_new, second_new)

def reference(noise_maps, dataset_lowres_images, dataset_highres_images, occupied_mask, shift_amounts, mirror_indicator, erase_box_corner, update_ordinal, fixed_backbone_params, singular_estimate_dirs, maker_weight_arrays, maker_mean_estimate, maker_variance_estimate, judge_weight_arrays, judge_mean_estimate, judge_variance_estimate, output_weight_rows, output_mean_estimate, output_variance_estimate):
    image_tiles = (S // 2) ** 2 + (S // 4) ** 2 + (S // 8) ** 2 + (S // 16) ** 2
    occupied_mask_all = occupied_mask.astype(jnp.float32)
    synth_tally = jnp.sum(occupied_mask_all[:, :SYNTH_IMAGES]) * image_tiles
    dataset_tally = jnp.sum(occupied_mask_all[:, SYNTH_IMAGES:]) * image_tiles
    frozen_parts = carve_flat(fixed_backbone_params.astype(jnp.float32), frozen_layouts())
    extract, project = (frozen_parts[:4], frozen_parts[4:])
    crit_round = carve_flat(judge_weight_arrays.astype(jnp.bfloat16).astype(jnp.float32), critic_layouts())
    starts = carve_flat(singular_estimate_dirs, vector_layouts())
    right_vecs, left_vecs, sigmas = ([], [], [])
    for section_index in range(4):
        right_vec = normalize(product(crit_round[section_index], starts[section_index]))
        left_vec = normalize(product(crit_round[section_index].T, right_vec))
        right_vecs.append(right_vec)
        left_vecs.append(left_vec)
        sigmas.append(jnp.dot(left_vec, product(crit_round[section_index].T, right_vec), precision=highest))
    head_parts = carve_flat(output_weight_rows, vector_layouts() + [(GOUT, 3)])
    unit_const = [normalize(segment) for segment in head_parts[:4]]
    all_tables = jax.vmap(augment_tables)(shift_amounts.reshape(-1, 2), mirror_indicator.reshape(-1), erase_box_corner.reshape(-1, 2))

    def select(first_slot, last_slot):
        return tuple((one_table.reshape(DEVICES, SLOTS, S, S)[:, first_slot:last_slot].reshape(-1, S, S) for one_table in all_tables))
    fake_tables = select(0, SYNTH_IMAGES)
    synth_share = (occupied_mask_all[:, :SYNTH_IMAGES] / synth_tally).reshape(-1)

    def gen_term(gen_weights, rgb_weight, latent, tables, weight_one):
        conv_first, conv_second = carve_flat(low(gen_weights), [(Z, GIN), (9 * GIN, 2 * GOUT)])
        image = generate(conv_first, conv_second, rgb_weight, latent)
        logits = critic_logits(apply_tables(image, tables), extract, project, crit_round, sigmas, unit_const)
        loss_part = sum((jnp.sum(jax.nn.softplus(-level_logits)) for level_logits in logits)) * weight_one
        return (loss_part, image)

    def gen_step(carry, inputs):
        latent, down_one, across_one, keep_one, weight_one = inputs
        loss_part, pullback, image = jax.vjp(lambda gen_weights, rgb_weight: gen_term(gen_weights, rgb_weight, latent.astype(jnp.float32), (down_one, across_one, keep_one), weight_one), maker_weight_arrays, head_parts[4], has_aux=True)
        grad_gen, grad_rgb = pullback(jnp.ones((), jnp.float32))
        return ((carry[0] + grad_gen, carry[1] + grad_rgb, carry[2] + loss_part), image)
    gen_start = (jnp.zeros((GPAR,), jnp.float32), jnp.zeros((GOUT, 3), jnp.float32), jnp.zeros((), jnp.float32))
    (grad_gen, grad_rgb, loss_gen), fake_images = lax.scan(gen_step, gen_start, (noise_maps, fake_tables[0], fake_tables[1], fake_tables[2], synth_share))
    small_images = dataset_lowres_images.astype(jnp.float32).reshape(-1, 3, S, S)
    large_images = pooled(dataset_highres_images.astype(jnp.float32).reshape(-1, 3, 2 * S, 2 * S))
    images = jnp.concatenate([fake_images, small_images, large_images], axis=0)
    small_tables = select(SYNTH_IMAGES, SYNTH_IMAGES + TRUE_LOW_RES)
    large_tables = select(SYNTH_IMAGES + TRUE_LOW_RES, SLOTS)
    tables_all = tuple((jnp.concatenate([fake_tables[which], small_tables[which], large_tables[which]], axis=0) for which in range(3)))
    dataset_share_lowres = (occupied_mask_all[:, SYNTH_IMAGES:SYNTH_IMAGES + TRUE_LOW_RES] / dataset_tally).reshape(-1)
    dataset_share_highres = (occupied_mask_all[:, SYNTH_IMAGES + TRUE_LOW_RES:] / dataset_tally).reshape(-1)
    weights_all = jnp.concatenate([synth_share, dataset_share_lowres, dataset_share_highres])
    signs_all = jnp.concatenate([-jnp.ones(synth_share.shape, jnp.float32), jnp.ones(dataset_share_lowres.shape, jnp.float32), jnp.ones(dataset_share_highres.shape, jnp.float32)])

    def disc_term(crit_weights, probe_weights, image, tables, weight_one, sign_one):
        matrices = [low(segment) for segment in carve_flat(crit_weights, critic_layouts())]
        level_sigmas = [jnp.dot(left_vecs[section_index], product(matrices[section_index].T, right_vecs[section_index]), precision=highest) for section_index in range(4)]
        unit_heads = [normalize(segment) for segment in carve_flat(probe_weights, vector_layouts())]
        logits = critic_logits(apply_tables(image, tables), extract, project, matrices, level_sigmas, unit_heads)
        return sum((jnp.sum(jax.nn.relu(1.0 - sign_one * level_logits)) for level_logits in logits)) * weight_one

    def disc_step(carry, inputs):
        image, down_one, across_one, keep_one, weight_one, sign_one = inputs
        loss_part, pullback = jax.vjp(lambda crit_weights, probe_weights: disc_term(crit_weights, probe_weights, image, (down_one, across_one, keep_one), weight_one, sign_one), judge_weight_arrays, output_weight_rows[:UNITS])
        grad_crit, grad_probe = pullback(jnp.ones((), jnp.float32))
        return ((carry[0] + grad_crit, carry[1] + grad_probe, carry[2] + loss_part), None)
    disc_start = (jnp.zeros((DPAR,), jnp.float32), jnp.zeros((UNITS,), jnp.float32), jnp.zeros((), jnp.float32))
    (grad_crit, grad_probe, loss_critic), unused = lax.scan(disc_step, disc_start, (images, tables_all[0], tables_all[1], tables_all[2], weights_all, signs_all))
    step_number = update_ordinal[0].astype(jnp.float32)
    gen_new, gen_first_new, gen_second_new = adamw_update(maker_weight_arrays, maker_mean_estimate, maker_variance_estimate, grad_gen, step_number)
    crit_new, crit_first_new, crit_second_new = adamw_update(judge_weight_arrays, judge_mean_estimate, judge_variance_estimate, grad_crit, step_number)
    grad_heads = jnp.concatenate([grad_probe, grad_rgb.reshape(-1)])
    head_new, head_first_new, head_second_new = adamw_update(output_weight_rows, output_mean_estimate, output_variance_estimate, grad_heads, step_number)
    losses = jnp.stack([loss_gen, loss_critic])
    power_new = jnp.concatenate(left_vecs)
    return (gen_new, gen_first_new, gen_second_new, crit_new, crit_first_new, crit_second_new, head_new, head_first_new, head_second_new, losses, power_new)
```

```python
import functools

import jax
import jax.numpy as jnp
from jax import lax
from jax.experimental import pallas as pl
from jax.experimental.pallas import tpu as pltpu
from jax.sharding import Mesh
from jax.sharding import PartitionSpec as P

S = 32
Z = 256
GIN = 1024
GOUT = 512
CS = (24, 40, 112, 320)
KS = (64, 128, 256, 512)
CP = (128, 128, 128, 384)
KP = (128, 128, 256, 512)
SLOTS = 4
PIX = 256
GROUP = 8
IMAGE_TILES = 340
ROWS_FIRST = 256
TAPS = 9

leak_slope = 0.2
learn_rate = 0.03
beta_first = 0.5
beta_second = 0.5
adam_epsilon = 1e-08
weight_decay = 0.0001
norm_epsilon = 1e-06

f32 = jnp.float32
bf16 = jnp.bfloat16
PLANE = ("y", "x", "c")
EVERY = ("z", "y", "x", "c")
VMEM_LIMIT = 60 * 1024 * 1024

NN = (((1,), (0,)), ((), ()))
NT = (((1,), (1,)), ((), ()))
TN = (((0,), (0,)), ((), ()))


def dot(a, b, dims=NN):
    return lax.dot_general(a, b, dims, preferred_element_type=f32)


def call(kernel, out_shape, *args, scratch=(), smem=(), hbm=(), us=5, name=None):
    vmem = pl.BlockSpec(memory_space=pltpu.VMEM)
    spaces = {i: pl.BlockSpec(memory_space=pltpu.SMEM) for i in smem}
    spaces.update({i: pl.BlockSpec(memory_space=pl.ANY) for i in hbm})
    single = not isinstance(out_shape, (list, tuple))
    return pl.pallas_call(
        kernel,
        out_shape=out_shape,
        in_specs=[spaces.get(i, vmem) for i in range(len(args))],
        out_specs=vmem if single else [vmem] * len(out_shape),
        scratch_shapes=list(scratch),
        compiler_params=pltpu.CompilerParams(vmem_limit_bytes=VMEM_LIMIT),
        cost_estimate=pl.CostEstimate(
            flops=int(us * 1e8), bytes_accessed=int(us * 3e5), transcendentals=0
        ),
        name=name,
    )(*args)


def shape(dims, dtype):
    return jax.ShapeDtypeStruct(dims, dtype)


def split_two(x):
    high = x.astype(bf16)
    return high, (x - high.astype(f32)).astype(bf16)


def split_three(x):
    high = x.astype(bf16)
    rest = x - high.astype(f32)
    middle = rest.astype(bf16)
    return high, middle, (rest - middle.astype(f32)).astype(bf16)


def pack_kernel(w_ref, o_ref):
    rows = o_ref.shape[1]
    low_half = lax.broadcasted_iota(jnp.int32, (rows, 128), 1) < 64
    for j in range(4):
        a = w_ref[pl.ds(j, rows, stride=8), :]
        b = w_ref[pl.ds(j + 4, rows, stride=8), :]
        o_ref[2 * j] = jnp.where(low_half, a, pltpu.roll(b, 64, 1)).astype(bf16)
        o_ref[2 * j + 1] = jnp.where(low_half, pltpu.roll(a, 64, 1), b).astype(bf16)


def adam_kernel(fix_ref, g_ref, p_ref, m_ref, v_ref, po_ref, mo_ref, vo_ref):
    rows = g_ref.shape[1]
    low_half = lax.broadcasted_iota(jnp.int32, (rows, 128), 1) < 64
    for j in range(8):
        a = g_ref[2 * (j % 4)]
        b = g_ref[2 * (j % 4) + 1]
        if j < 4:
            g = jnp.where(low_half, a, pltpu.roll(b, 64, 1))
        else:
            g = jnp.where(low_half, pltpu.roll(a, 64, 1), b)
        at = pl.ds(j, rows, stride=8)
        new, first, second = adamw_update(p_ref[at, :], m_ref[at, :], v_ref[at, :], g, fix_ref[0])
        po_ref[at, :] = new
        mo_ref[at, :] = first
        vo_ref[at, :] = second


def adamw_update(master, first, second, grad, fix):
    first_new = beta_first * first + (1.0 - beta_first) * grad
    second_new = beta_second * second + (1.0 - beta_second) * grad * grad
    update = first_new / fix / (jnp.sqrt(second_new / fix) + adam_epsilon)
    return master - learn_rate * (update + weight_decay * master), first_new, second_new


SLOT_MASK = tuple(((m >> 1) & 1) * 4 + (m & 1) * 2 + (m >> 2) for m in range(GROUP))
SLOT_FIRST = tuple(2 * (m & 1) + ((m >> 1) & 1) for m in range(4))
SLOT_SECOND = tuple(4 + m for m in range(4))
NOISE_MASK = tuple((m & 1) * 4 + ((m >> 1) & 1) * 2 + (m >> 2) for m in range(GROUP))


def pre_kernel(me_ref, noise_ref, w_ref, pre_ref, hid_ref):
    for m in range(GROUP):
        rows = pl.ds(pl.multiple_of((me_ref[0] ^ NOISE_MASK[m]) * PIX, PIX), PIX)
        pre = dot(noise_ref[m], w_ref[...], TN)
        pre_ref[rows, :] = pre
        hid_ref[rows, :] = (pre * jax.nn.sigmoid(pre)).astype(bf16)


def turn_kernel(near_ref, far_ref, o_ref):
    for m in range(GROUP):
        source = near_ref if m < 4 else far_ref
        for part, at in enumerate((SLOT_FIRST[m % 4], SLOT_SECOND[m % 4])):
            o_ref[128 * m : 128 * m + 128, 1024 * part : 1024 * part + 1024] = jnp.transpose(
                source[at]
            )


def pixel_column():
    return lax.broadcasted_iota(jnp.int32, (PIX, 128), 0) & 15


def from_left(x, column):
    return jnp.where(column > 0, pltpu.roll(x, 1, 0), 0.0)


def from_right(x, column):
    return jnp.where(column < 15, pltpu.roll(x, PIX - 1, 0), 0.0)


def from_above(x):
    return jnp.concatenate([jnp.zeros((16, x.shape[1]), x.dtype), x[:-16]], axis=0)


def from_below(x):
    return jnp.concatenate([x[16:], jnp.zeros((16, x.shape[1]), x.dtype)], axis=0)


def block_row(tap, q, half):
    return ROWS_FIRST + tap * GIN + half * GOUT + q * 64


def forward_kernel(*refs):
    me_ref, near_ref, far_ref, color_ref = refs[:4]
    factor_ref, gated_ref, rgb_ref, wide, parts, w_ref, sem = refs[-7:]
    blocks = refs[4:-7]
    chunk = w_ref.shape[0] // 4
    if len(blocks) == 1:
        copy = pltpu.make_async_copy(blocks[0], w_ref, sem)
        copy.start()
        copy.wait()
    else:
        for here in range(4):

            @pl.when(me_ref[1] == here)
            def _():
                for k in range(4):
                    pltpu.make_async_copy(
                        blocks[3 + k - here].at[pl.ds(0, chunk), :],
                        w_ref.at[pl.ds(k * chunk, chunk), :],
                        sem,
                    ).start()

        pltpu.make_async_copy(w_ref, w_ref, sem).wait()
    for m in range(GROUP):
        q = me_ref[0] ^ SLOT_MASK[m]
        for tap in range(TAPS):
            for half in range(2):
                at = m * 128 + half * 64
                row = pl.multiple_of(block_row(tap, q, half), 64)
                wide[at : at + 64, 128 * tap : 128 * tap + 128] = w_ref[pl.ds(row, 64), :]
    wide[:, 128 * TAPS :] = jnp.zeros((GIN, 128), bf16)
    low_half = lax.broadcasted_iota(jnp.int32, (PIX, 128), 1) < 64
    column = pixel_column()
    color_high, color_low = split_two(color_ref[...])
    color = jnp.concatenate([color_high, color_low], axis=0)

    @pl.loop(0, 4)
    def _(pair):
        start = pl.multiple_of(pair * 512, 512)
        local = pl.multiple_of((pair & 1) * 512, 512)
        first = pair < 2
        left = []
        for m in range(GROUP):
            at = jnp.where(first, SLOT_FIRST[m % 4], SLOT_SECOND[m % 4])
            left.append((near_ref if m < 4 else far_ref)[at, pl.ds(local, 512), :])
        left = jnp.concatenate(left, axis=1)
        for k in range(5):
            y = dot(left, wide[:, 256 * k : 256 * k + 256])
            parts[2 * k] = y[:, :128]
            if k < 4:
                parts[2 * k + 1] = y[:, 128:]
        for one in range(2):
            rows = pl.ds(pl.multiple_of(start + one * PIX, PIX), PIX)
            here = slice(one * PIX, one * PIX + PIX)
            cols = []
            for a in range(3):
                y0, y1, y2 = (parts[3 * a + b, here, :] for b in range(3))
                cols.append((from_left(y0, column) + (y1 + y2), (y0 + y1) + from_right(y2, column)))
            for pi in range(2):
                gated = []
                for pj in range(2):
                    if pi == 0:
                        mixed = from_above(cols[0][pj]) + (cols[1][pj] + cols[2][pj])
                    else:
                        mixed = (cols[0][pj] + cols[1][pj]) + from_below(cols[2][pj])
                    turned = pltpu.roll(mixed, 64, 1)
                    gate = jax.nn.sigmoid(jnp.where(low_half, turned, mixed))
                    value = jnp.where(low_half, mixed, turned)
                    gated.append(value * gate)
                    factor_ref[2 * pi + pj, rows, :] = jnp.where(
                        low_half, gate, gated[-1] * (1.0 - gate)
                    )
                both = jnp.where(low_half, gated[0], gated[1])
                gated_ref[pi, rows, :] = both
                high, low = split_two(both)
                rgb = dot(color, jnp.concatenate([high, low], axis=1), NT)
                rgb_ref[2 * pair + one, 16 * pi : 16 * pi + 16, :] = rgb[:16] + rgb[16:]


def tap_sums(parts, column):
    sums = []
    for a in range(3):
        line = []
        for pj in range(2):
            even, odd = parts[pj], parts[2 + pj]
            if a == 0:
                line.append(odd + from_below(even))
            elif a == 1:
                line.append(even + odd)
            else:
                line.append(from_above(odd) + even)
        sums.append(line[1] + from_right(line[0], column))
        sums.append(line[0] + line[1])
        sums.append(from_left(line[1], column) + line[0])
    return sums


def weight_grad_kernel(me_ref, dt_ref, factor_ref, hid_ref, color_ref, g_ref, dm_ref, moved):
    column = pixel_column()
    g_ref[:ROWS_FIRST, :] = jnp.zeros((ROWS_FIRST, 128), f32)

    @pl.loop(0, GROUP)
    def _(b):
        rows = pl.ds(pl.multiple_of(b * PIX, PIX), PIX)
        turned = jnp.transpose(dt_ref[b])
        for phase in range(4):
            pi, pj = phase // 2, phase % 2
            spread = turned[:, 8 * phase : 8 * phase + 1] * color_ref[0:1, :]
            for c in (1, 2):
                spread = spread + turned[:, 8 * phase + c : 8 * phase + c + 1] * color_ref[c : c + 1, :]
            low = (spread * factor_ref[phase, rows, :]).astype(bf16)
            dm_ref[phase, rows, :] = low
            plain = low.astype(f32)
            side = (from_right if pj == 0 else from_left)(plain, column)
            lanes = slice(128 * pj, 128 * pj + 128)
            for k, value in enumerate((plain, side)):
                line = (from_below if pi == 0 else from_above)(value)
                moved[4 * pi + k, rows, lanes] = value.astype(bf16)
                moved[4 * pi + 2 + k, rows, lanes] = line.astype(bf16)

    def column_sums(at):
        plain = dot(hid_ref[...], moved[at])
        side = dot(hid_ref[...], moved[at + 1])
        return (
            plain[:, 128:] + side[:, :128],
            plain[:, :128] + plain[:, 128:],
            side[:, 128:] + plain[:, :128],
        )

    def put(tap, value, add):
        for m in range(GROUP):
            for half in range(2):
                q = me_ref[0] ^ SLOT_MASK[m]
                at = pl.ds(pl.multiple_of(block_row(tap, q, half), 64), 64)
                piece = value[128 * m + 64 * half : 128 * m + 64 * half + 64]
                g_ref[at, :] = g_ref[at, :] + piece if add else piece

    for at, takes in ((0, ((1, False), (2, False))), (4, ((0, False), (1, True)))):
        for b, value in enumerate(column_sums(at)):
            for a, add in takes:
                put(3 * a + b, value, add)
    for at, a in ((2, 0), (6, 2)):
        for b, value in enumerate(column_sums(at)):
            put(3 * a + b, value, True)


def hidden_grad_kernel(dm_ref, wide_ref, dt_ref, gated_ref, keep_ref, send_ref, rgb_ref, sums):
    column = pixel_column()
    rgb_ref[...] = jnp.zeros_like(rgb_ref)

    @pl.loop(0, GROUP)
    def _(b):
        rows = pl.ds(pl.multiple_of(b * PIX, PIX), PIX)
        parts = [dm_ref[phase, rows, :].astype(f32) for phase in range(4)]
        for tap, total in enumerate(tap_sums(parts, column)):
            high, low = split_two(total)
            sums[:PIX, 128 * tap : 128 * tap + 128] = high
            sums[PIX:, 128 * tap : 128 * tap + 128] = low
        for k in range(4):
            out = dot(sums[...], wide_ref[256 * k : 256 * k + 256, : 128 * TAPS], NT)
            out = out[:PIX] + out[PIX:]
            put = keep_ref if k < 2 else send_ref
            put[2 * (k % 2), rows, :] = out[:, :128]
            put[2 * (k % 2) + 1, rows, :] = out[:, 128:]
        for pi in range(2):
            high, low = split_two(dt_ref[b, 16 * pi : 16 * pi + 16, :])
            g_high, g_low = split_two(gated_ref[pi, rows, :])
            left = jnp.concatenate([high, low], axis=0)
            out = dot(left, jnp.concatenate([g_high, g_low], axis=1))
            rgb_ref[...] += out[:16, :128] + (out[:16, 128:] + out[16:, :128])


def first_grad_kernel(me_ref, dh_ref, pre_ref, noise_ref, o_ref):
    o_ref[...] = jnp.zeros_like(o_ref)
    for m in range(GROUP):
        rows = pl.ds(pl.multiple_of((me_ref[0] ^ NOISE_MASK[m]) * PIX, PIX), PIX)
        pre = pre_ref[rows, :]
        gate = jax.nn.sigmoid(pre)
        slope = gate * (1.0 + pre * (1.0 - gate))
        o_ref[...] += dot(noise_ref[m], (slope * dh_ref[rows, :]).astype(bf16))


def row_normalized(row):
    return row * lax.rsqrt(jnp.sum(row * row, axis=1, keepdims=True) + norm_epsilon)


def row_times(row, matrix, dims):
    pieces = jnp.concatenate(
        [jnp.broadcast_to(x.astype(f32), (8, row.shape[1])) for x in split_three(row)], axis=0
    ).astype(bf16)
    out = dot(pieces, matrix, dims)
    return out[0:1] + out[8:9] + out[16:17]


INS = (3,) + CS[:3]
CRIT_AT = (0, 4096, 20480, 86016)


def window(length):
    rows = length // 128 if length % 128 == 0 else -(-(127 + length) // 128)
    return -(-rows // 16) * 16


def prepare_kernel(
    crit_length, frozen_length, small_ref, own_ref, u_ref,
    e1, e2, e3, e4, r1, r2, r3, r4, m1, m2, m3, m4, c1, c2, c3, c4,
    left_ref, sigma_ref, share_ref, crit, frozen, moved, rows_buf,
):
    devices = small_ref.shape[0]
    crit_rows, frozen_rows = window(crit_length), window(frozen_length)
    crit[...] = jnp.zeros_like(crit)
    frozen[...] = jnp.zeros_like(frozen)
    for k in range(devices):
        at = pl.ds((k * crit_length) // 128, crit_rows)
        crit[at, :] += small_ref[k, :crit_rows, :].astype(f32)
        at = pl.ds((k * frozen_length) // 128, frozen_rows)
        frozen[at, :] += small_ref[k, crit_rows : crit_rows + frozen_rows, :].astype(f32)
    live = jnp.zeros((1, 128), f32)
    for k in range(devices):
        at = crit_rows + frozen_rows
        live += small_ref[k, at : at + 16, :].astype(f32)[0:1]
    lane = lax.broadcasted_iota(jnp.int32, (1, 128), 1)
    real = jnp.sum(jnp.where((lane > 0) & (lane < SLOTS), live, 0.0), axis=1, keepdims=True)
    count = jnp.where(lane == 0, live, real) * float(IMAGE_TILES)
    share_ref[...] = jnp.broadcast_to(own_ref[...] / jnp.maximum(count, 1.0), share_ref.shape)

    def lanes_of(x):
        return lax.broadcasted_iota(jnp.int32, x.shape, 1)

    def shifted(a, b, lane_at):
        if lane_at == 0:
            return a
        turn = 128 - lane_at
        return jnp.where(lanes_of(a) < turn, pltpu.roll(a, turn, 1), pltpu.roll(b, turn, 1))

    def halves(x):
        low = lanes_of(x) < 64
        return jnp.where(low, x, 0.0), jnp.where(low, pltpu.roll(x, 64, 1), 0.0)

    def flush(ref, rows):
        ref[...] = rows_buf[: ref.shape[0], :].astype(bf16)
        rows_buf[:rows, :] = jnp.zeros((rows, 128), f32)

    total = frozen.shape[0] - 8
    moved[...] = shifted(frozen[:total, :], frozen[1 : total + 1, :], 8)
    rows_buf[...] = jnp.zeros_like(rows_buf)
    for ref, offset, rows, width in ((e1, 0, INS[0], CS[0]), (e2, 72, INS[1], CS[1])):
        for r in range(rows):
            a, lane_at = divmod(offset + r * width, 128)
            row = shifted(frozen[a : a + 1, :], frozen[a + 1 : a + 2, :], lane_at)
            rows_buf[r : r + 1, :] = jnp.where(lane < width, row, 0.0)
        flush(ref, 32)
    for i in range(8):
        a, lane_at = divmod(112 * i, 128)
        row = shifted(
            moved[pl.ds(8 + a, 5, stride=7), :], moved[pl.ds(9 + a, 5, stride=7), :], lane_at
        )
        rows_buf[pl.ds(i, 5, stride=8), :] = jnp.where(lanes_of(row) < 112, row, 0.0)
    flush(e3, 40)
    five = [moved[pl.ds(43 + k, 56, stride=5), :] for k in range(5)]
    pairs = (
        (five[0], shifted(five[2], five[3], 64)),
        (five[1], shifted(five[3], five[4], 64)),
        (halves(five[2])[0], halves(five[4])[1]),
    )
    e4[...] = jnp.zeros_like(e4)
    for b, (even, odd) in enumerate(pairs):
        rows_buf[pl.ds(0, 56, stride=2), :] = even
        rows_buf[pl.ds(1, 56, stride=2), :] = odd
        e4[:112, 128 * b : 128 * b + 128] = rows_buf[:112, :].astype(bf16)
    rows_buf[...] = jnp.zeros_like(rows_buf)
    even, odd = halves(moved[323:335, :])
    rows_buf[pl.ds(0, 12, stride=2), :] = even
    rows_buf[pl.ds(1, 12, stride=2), :] = odd
    flush(r1, 24)
    rows_buf[:40, :] = moved[335:375, :]
    flush(r2, 40)
    r3[...] = jnp.zeros_like(r3)
    r4[...] = jnp.zeros_like(r4)
    for b in range(2):
        r3[:112, 128 * b : 128 * b + 128] = moved[pl.ds(375 + b, 112, stride=2), :].astype(bf16)
    for b in range(4):
        r4[:320, 128 * b : 128 * b + 128] = moved[pl.ds(599 + b, 320, stride=4), :].astype(bf16)
    even, odd = halves(crit[:32, :])
    rows_buf[pl.ds(0, 32, stride=2), :] = even
    rows_buf[pl.ds(1, 32, stride=2), :] = odd
    flush(m1, 64)
    m2[...] = crit[32:160, :].astype(bf16)
    for b in range(2):
        m3[:, 128 * b : 128 * b + 128] = crit[pl.ds(160 + b, 256, stride=2), :].astype(bf16)
    for b in range(4):
        m4[:, 128 * b : 128 * b + 128] = crit[pl.ds(672 + b, 512, stride=4), :].astype(bf16)

    left_ref[...] = jnp.zeros_like(left_ref)
    sigma_ref[...] = jnp.ones_like(sigma_ref)
    for k, (m_ref, c_ref) in enumerate(((m1, c1), (m2, c2), (m3, c3), (m4, c4))):
        width = KP[k]
        matrix = m_ref[...]
        right = row_normalized(row_times(u_ref[k : k + 1, :width], matrix, NT))
        turned = row_times(right, matrix, NN)
        left = row_normalized(turned)
        left_ref[k : k + 1, :width] = left
        sigma = jnp.sum(left * turned, axis=1, keepdims=True)
        sigma_ref[k : k + 1, :] = jnp.broadcast_to(sigma, (1, 128))
        c_ref[...] = jnp.transpose(jnp.broadcast_to(right, (128, width)))


def wanted_code(scal_ref, slot):
    d = lax.broadcasted_iota(jnp.int32, (1, 1024), 1)

    def bit(k):
        return (d >> k) & 1

    i = bit(9) + 2 * bit(7) + 4 * bit(5) + 8 * bit(3) + 16 * bit(1)
    j = bit(8) + 2 * bit(6) + 4 * bit(4) + 8 * bit(2) + 16 * bit(0)
    down, across, flip, top, side = (scal_ref[slot, k] for k in range(5))
    row = i - down
    moved = j - across
    fine = (row >= 0) & (row < S) & (moved >= 0) & (moved < S)
    source = jnp.where(flip == 1, S - 1 - moved, moved)
    boxed = (i >= top) & (i < top + S // 2) & (j >= side) & (j < side + S // 2)
    return jnp.where(fine & jnp.logical_not(boxed), row * S + source, -1)


def three(x):
    return jnp.concatenate([v.astype(f32) for v in split_three(x)], axis=0).astype(bf16)


def fold(x):
    return x[0:8] + x[8:16] + x[16:24]


def fill_pick(pick, scal_ref, slot, phases):
    want = wanted_code(scal_ref, slot)

    @pl.loop(0, 8)
    def _(k):
        s = lax.broadcasted_iota(jnp.int32, (128, 1024), 0) + k * 128
        if phases:
            at = s & 255
            s = (2 * (at >> 4) + (s >> 9)) * S + 2 * (at & 15) + ((s >> 8) & 1)
        hit = jnp.where(s == want, 1.0, 0.0).astype(bf16)
        pick[pl.ds(pl.multiple_of(k * 128, 128), 128), :] = hit


def augmented(image, pick):
    seen = fold(dot(three(image), pick[...]))
    small = 0.25 * ((seen[:, :256] + seen[:, 256:512]) + (seen[:, 512:768] + seen[:, 768:]))
    return jnp.transpose(small).astype(bf16)


def last_pool(slots):
    row = lax.broadcasted_iota(jnp.int32, (16, 16 * slots), 0)
    col = lax.broadcasted_iota(jnp.int32, (16, 16 * slots), 1)
    pool = jnp.where((row // 4 == col // 16) & (row % 4 == col % 4), 0.25, 0.0)
    return jnp.concatenate([pool.astype(bf16)] * 3, axis=1)


def critic_levels(inputs, slots, extract, project, matrices, head_ref, sigma_ref):
    levels = []
    pool = last_pool(slots)
    for k in range(4):
        count = 16 if k == 3 else (slots * PIX) >> (2 * k)
        width = KP[k]
        pre = dot(inputs, extract[k][...])
        active = pre * jax.nn.sigmoid(pre)
        feat = dot(active.astype(bf16), project[k][...]).astype(bf16)
        raw = dot(feat, matrices[k][...])
        sigma = sigma_ref[k : k + 1, 0:1]
        scaled = raw / sigma
        slope = jnp.where(scaled >= 0, 1.0, leak_slope)
        leaky = scaled * slope
        head = head_ref[k : k + 1, :width]
        scale = lax.rsqrt(jnp.sum(head * head, axis=1, keepdims=True) + norm_epsilon)
        unit = head * scale
        logit = jnp.sum(leaky * unit, axis=1, keepdims=True)
        levels.append((pre, feat, raw, sigma, slope, leaky, head, scale, unit, logit))
        if k < 2:
            blocks = active.reshape(slots, 4, count // (4 * slots), CP[k])
            total = (blocks[:, 0] + blocks[:, 1]) + (blocks[:, 2] + blocks[:, 3])
            inputs = (0.25 * total).reshape(count // 4, CP[k]).astype(bf16)
        elif k == 2:
            inputs = dot(pool, three(active)).astype(bf16)
    return levels


def image_grad_kernel(
    scal_ref,
    share_ref,
    got_ref,
    head_ref,
    sigma_ref,
    e1, e2, e3, e4,
    r1, r2, r3, r4,
    m1, m2, m3, m4,
    dt_ref,
    map_ref,
    pick,
):
    extract, project, matrices = (e1, e2, e3, e4), (r1, r2, r3, r4), (m1, m2, m3, m4)
    fill_pick(pick, scal_ref, 0, True)
    color = got_ref[0]
    for k in range(1, GROUP):
        color = color + got_ref[k]
    color = jnp.tanh(color)
    fake = jnp.concatenate([color[8 * k : 8 * k + 8] for k in range(4)], axis=1)
    first_map = augmented(fake, pick)
    map_ref[...] = first_map
    levels = critic_levels(first_map, 1, extract, project, matrices, head_ref, sigma_ref)
    row = lax.broadcasted_iota(jnp.int32, (16, 16), 0)
    col = lax.broadcasted_iota(jnp.int32, (16, 16), 1)
    spread = jnp.where((col < 4) & (row % 4 == col), 0.25, 0.0)
    spread = jnp.concatenate([spread.astype(bf16)] * 3, axis=1)
    carry = None
    for k in (3, 2, 1, 0):
        pre, feat, raw, sigma, slope, leaky, head, scale, unit, logit = levels[k]
        dlogit = -share_ref[0:1, 0:1] * jax.nn.sigmoid(-logit)
        if k == 3:
            dlogit = jnp.where(lax.broadcasted_iota(jnp.int32, (16, 1), 0) < 4, dlogit, 0.0)
        dscaled = dlogit * unit * slope
        dfeat = dot((dscaled / sigma).astype(bf16), matrices[k][...], NT).astype(bf16)
        dactive = dot(dfeat, project[k][...], NT)
        if carry is not None:
            dactive = dactive + carry
        gate = jax.nn.sigmoid(pre)
        dpre = (gate * (1.0 + pre * (1.0 - gate)) * dactive).astype(bf16)
        dinput = dot(dpre, extract[k][...], NT)
        if k == 3:
            carry = dot(spread, three(dinput))
        elif k > 0:
            carry = jnp.concatenate([0.25 * dinput] * 4, axis=0)
    daug = 0.25 * jnp.transpose(dinput)
    daug = jnp.concatenate([daug] * 4, axis=1)
    dimage = fold(dot(three(daug), pick[...], NT))
    dtanh = dimage * (1.0 - fake * fake)
    for k in range(4):
        dt_ref[8 * k : 8 * k + 8, :] = dtanh[:, 256 * k : 256 * k + 256]


def critic_kernel(
    scal_ref,
    share_ref,
    map_ref,
    real_ref,
    head_ref,
    left_ref,
    sigma_ref,
    e1, e2, e3, e4,
    r1, r2, r3, r4,
    m1, m2, m3, m4,
    c1, c2, c3, c4,
    out_ref,
    d1, d2, d3, d4,
    pick,
    first_map,
):
    extract, project = (e1, e2, e3, e4), (r1, r2, r3, r4)
    matrices, columns, grads = (m1, m2, m3, m4), (c1, c2, c3, c4), (d1, d2, d3, d4)
    first_map[:PIX, :] = map_ref[...]
    for slot in range(1, SLOTS):
        fill_pick(pick, scal_ref, slot, False)
        first_map[slot * PIX : slot * PIX + PIX, :] = augmented(real_ref[slot - 1], pick)
    levels = critic_levels(first_map[...], SLOTS, extract, project, matrices, head_ref, sigma_ref)
    loss_gen = jnp.zeros((1, 1), f32)
    loss_critic = jnp.zeros((1, 1), f32)
    out_ref[...] = jnp.zeros_like(out_ref)
    for k in range(4):
        pre, feat, raw, sigma, slope, leaky, head, scale, unit, logit = levels[k]
        count, width = logit.shape[0], KP[k]
        slot = lax.broadcasted_iota(jnp.int32, (count, 1), 0) // (count // SLOTS)
        share = share_ref[0:1, 0:1]
        for other in range(1, SLOTS):
            share = jnp.where(slot == other, share_ref[0:1, other : other + 1], share)
        sign = jnp.where(slot == 0, -1.0, 1.0)
        hinge = 1.0 - sign * logit
        loss_critic += jnp.sum(share * jnp.maximum(hinge, 0.0), axis=0, keepdims=True)
        dlogit = jnp.where(hinge > 0, -sign * share, 0.0)
        soft = jnp.maximum(-logit, 0.0) + jnp.log1p(jnp.exp(-jnp.abs(logit)))
        loss_gen += jnp.sum(jnp.where(slot == 0, share * soft, 0.0), axis=0, keepdims=True)
        dscaled = dlogit * unit * slope
        grad = dot(feat, (dscaled / sigma).astype(bf16), TN)
        dsigma = jnp.sum(jnp.sum(dscaled * raw, axis=1, keepdims=True), axis=0, keepdims=True)
        dsigma = -dsigma / (sigma * sigma)
        side = columns[k][...] * dsigma
        for b in range(width // 128):
            lanes = slice(128 * b, 128 * b + 128)
            grads[k][:, lanes] = grad[:, lanes] + side * left_ref[k : k + 1, lanes]
        dunit = jnp.sum(leaky * dlogit, axis=0, keepdims=True)
        inner = jnp.sum(head * dunit, axis=1, keepdims=True)
        out_ref[k : k + 1, :width] = scale * dunit - head * (scale * scale * scale * inner)
    out_ref[4:5, 0:128] = jnp.broadcast_to(loss_gen, (1, 128))
    out_ref[4:5, 128:256] = jnp.broadcast_to(loss_critic, (1, 128))


def local(
    groups,
    noise_maps,
    dataset_lowres_images,
    dataset_highres_images,
    occupied_mask,
    shift_amounts,
    mirror_indicator,
    erase_box_corner,
    update_ordinal,
    fixed_backbone_params,
    singular_estimate_dirs,
    maker_weight_arrays,
    maker_mean_estimate,
    maker_variance_estimate,
    judge_weight_arrays,
    judge_mean_estimate,
    judge_variance_estimate,
    output_weight_rows,
    output_mean_estimate,
    output_variance_estimate,
):
    devices = groups * GROUP
    rows = maker_weight_arrays.shape[0] // 1024
    chunk = GROUP * rows
    z = lax.axis_index("z")
    q = (lax.axis_index("y") * 2 + lax.axis_index("x")) * 2 + lax.axis_index("c")
    me = jnp.stack([q, z]).astype(jnp.int32)

    def swap(x, axis):
        return lax.ppermute(x, axis, [(0, 1), (1, 0)])

    crit_length = judge_weight_arrays.shape[0]
    frozen_length = fixed_backbone_params.shape[0]
    member = z * GROUP + q

    def windowed(x):
        length = x.shape[0]
        rows_here = window(length)
        if length % 128 == 0:
            return jnp.pad(x.reshape(-1, 128), ((0, rows_here - length // 128), (0, 0)))
        empty = jnp.zeros((rows_here * 128,), bf16)
        start = lax.rem(member * length, 128)
        return lax.dynamic_update_slice(empty, x, (start,)).reshape(rows_here, 128)

    own = occupied_mask.astype(f32)
    small = jnp.concatenate(
        [
            windowed(judge_weight_arrays.astype(bf16)),
            windowed(fixed_backbone_params),
            jnp.pad(own.astype(bf16), ((0, 15), (0, 128 - SLOTS))),
        ]
    )

    def rows_of(flat):
        out, offset = [], 0
        for k in range(4):
            out.append(jnp.pad(flat[offset : offset + KS[k]], (0, 512 - KS[k])))
            offset += KS[k]
        return jnp.pad(jnp.stack(out), ((0, 4), (0, 0)))

    head_rows = rows_of(output_weight_rows)
    start_rows = rows_of(singular_estimate_dirs)
    own_row = jnp.pad(own, ((0, 0), (0, 128 - SLOTS)))
    color_all = output_weight_rows[960:].reshape(GOUT, 3)
    color = jnp.pad(lax.dynamic_slice(color_all, (q * 64, 0), (64, 3)).T, ((0, 5), (0, 0)))
    none = jnp.zeros_like(color)
    color_left = jnp.concatenate(
        [
            jnp.concatenate([color, none, color, none], axis=1),
            jnp.concatenate([none, color, none, color], axis=1),
        ],
        axis=0,
    )
    color_twice = jnp.concatenate([color, color], axis=1)
    small_images = dataset_lowres_images.astype(f32)
    large = dataset_highres_images.astype(f32).reshape(1, 3, S, 2, S, 2)
    large = jnp.mean(large, axis=(3, 5)).reshape(1, 3, S * S)
    reals = jnp.pad(jnp.concatenate([small_images, large]), ((0, 0), (0, 5), (0, 0)))
    scalars = jnp.concatenate(
        [shift_amounts[0], mirror_indicator[0][:, None], erase_box_corner[0]], axis=1
    )

    noise_all = jnp.concatenate([noise_maps, swap(noise_maps, "y")])

    packed = call(
        pack_kernel,
        shape((GROUP, rows, 128), bf16),
        maker_weight_arrays.reshape(8 * rows, 128),
        us=3,
        name="pack",
    )
    slices = lax.all_to_all(packed, PLANE, 0, 0, tiled=True).reshape(chunk, 128)
    slices, noise_all = lax.optimization_barrier((slices, noise_all))
    for axis in ("x", "c"):
        noise_all = jnp.concatenate([noise_all, swap(noise_all, axis)])
    first_block = slices[:ROWS_FIRST]

    def hop(x, y):
        down = lax.ppermute(x, "z", [(0, 1), (1, 2), (2, 3)])
        return down, lax.ppermute(y, "z", [(1, 0), (2, 1), (3, 2)])

    if groups == 4:
        sent = [lax.ppermute(first_block, "z", [(0, k)]) for k in (1, 2, 3)]
        riding = jnp.concatenate([slices, small])
        hop_one = hop(riding, riding)
        ready = (head_rows, start_rows, own_row, color_left, color_twice, reals, scalars, me)
        sent, hop_one, ready = lax.optimization_barrier((sent, hop_one, ready))
        head_rows, start_rows, own_row, color_left, color_twice, reals, scalars, me = ready
        first_weights = jnp.where(z == 0, first_block, sent[0] + sent[1] + sent[2])
        hop_two = hop(*hop_one)
    else:
        first_weights = lax.all_gather(first_block, "z", axis=0)[0]
        blocks = [lax.all_gather(slices, "z", axis=0, tiled=True)]

    pixels = GROUP * PIX
    pre, hid = call(
        pre_kernel,
        [shape((pixels, 128), f32), shape((pixels, 128), bf16)],
        me,
        noise_all,
        first_weights,
        smem=(0,),
        us=4,
        name="pre",
    )
    first, second = hid[: pixels // 2], hid[pixels // 2 :]
    first = jnp.stack([first, swap(first, "y")])
    second = jnp.stack([second, swap(second, "x")])
    if groups == 4:
        first, second, hop_two = lax.optimization_barrier((first, second, hop_two))
        hop_three = hop(*hop_two)
    first = jnp.concatenate([first, swap(first, "x")])
    second = jnp.concatenate([second, swap(second, "y")])
    if groups == 4:
        first, second, hop_three = lax.optimization_barrier((first, second, hop_three))
        blocks = [hop_three[0], hop_two[0], hop_one[0], riding, hop_one[1], hop_two[1], hop_three[1]]
        small = lax.dynamic_slice_in_dim(jnp.stack([x[chunk:] for x in blocks]), 3 - z, 4, axis=0)
    else:
        small = lax.all_gather(small, "z", axis=0)
    near = jnp.concatenate([first, second])
    far = swap(near, "c")
    near, far, small = lax.optimization_barrier((near, far, small))
    small = lax.all_to_all(jnp.broadcast_to(small, (GROUP,) + small.shape), PLANE, 0, 0, tiled=True)
    factor, gated, rgb, wide = call(
        forward_kernel,
        [
            shape((4, pixels, 128), f32),
            shape((2, pixels, 128), f32),
            shape((GROUP, 32, PIX), f32),
            shape((GIN, 1280), bf16),
        ],
        me,
        near,
        far,
        color_left,
        *blocks,
        smem=(0,),
        hbm=range(4, 4 + len(blocks)),
        scratch=[
            pltpu.VMEM((TAPS + 1, 512, 128), f32),
            pltpu.VMEM((groups * chunk, 128), bf16),
            pltpu.SemaphoreType.DMA,
        ],
        us=14,
        name="forward",
    )
    got = lax.all_to_all(rgb, PLANE, 0, 0, tiled=True)
    near, far, factor, small = lax.optimization_barrier((near, far, factor, small))
    small = jnp.swapaxes(small, 0, 1).reshape((devices,) + small.shape[2:])
    squares = [shape((8, CP[0]), bf16)] + [shape((CP[k - 1], CP[k]), bf16) for k in (1, 2, 3)]
    squares += [shape((CP[k], KP[k]), bf16) for k in range(4)]
    squares += [shape((KP[k], KP[k]), bf16) for k in range(4)]
    squares += [shape((KP[k], 128), f32) for k in range(4)]
    squares += [shape((8, 512), f32), shape((8, 128), f32), shape((8, 128), f32)]
    crit_space = -(-((devices - 1) * crit_length // 128 + window(crit_length)) // 8) * 8
    frozen_space = -(-((devices - 1) * frozen_length // 128 + window(frozen_length)) // 8) * 8 + 8
    prepared = call(
        functools.partial(prepare_kernel, crit_length, frozen_length),
        squares,
        small,
        own_row,
        start_rows,
        scratch=[
            pltpu.VMEM((crit_space, 128), f32),
            pltpu.VMEM((frozen_space, 128), f32),
            pltpu.VMEM((frozen_space - 8, 128), f32),
            pltpu.VMEM((128, 128), f32),
        ],
        us=8,
        name="prepare",
    )
    frozen, matrices, right_cols = prepared[:8], prepared[8:12], prepared[12:16]
    left_rows, sigma_rows, share = prepared[16:]
    power_new = jnp.concatenate([left_rows[k, : KS[k]] for k in range(4)])
    hid_turned = call(turn_kernel, shape((GIN, pixels), bf16), near, far, us=5, name="turn")

    dtanh, first_map = call(
        image_grad_kernel,
        [shape((32, PIX), f32), shape((PIX, 8), bf16)],
        scalars,
        share,
        got,
        head_rows,
        sigma_rows,
        *frozen,
        *matrices,
        smem=(0,),
        scratch=[pltpu.VMEM((1024, 1024), bf16)],
        us=8,
        name="image_grad",
    )

    dtanh_all = lax.all_gather(dtanh, PLANE, axis=0)
    grad, dmixed = call(
        weight_grad_kernel,
        [shape((ROWS_FIRST + TAPS * GIN, 128), f32), shape((4, pixels, 128), bf16)],
        me,
        dtanh_all,
        factor,
        hid_turned,
        color_twice,
        smem=(0,),
        scratch=[pltpu.VMEM((8, pixels, 256), bf16)],
        us=20,
        name="weight_grad",
    )
    steps = []
    if groups == 4:

        def part(k):
            return lax.dynamic_slice_in_dim(grad, jnp.clip(k, 0, 3) * chunk, chunk, axis=0)

        def step(s, a, b):
            if s > 0:
                a, b = part(3 - s + z) + a, part(z - 3 + s) + b
            down = lax.ppermute(a, "z", [(k, k + 1) for k in range(s + 1)])
            up = lax.ppermute(b, "z", [(3 - k, 2 - k) for k in range(s + 1)])
            return lax.optimization_barrier((down, up))

        first_a, first_b, first_map, dmixed = lax.optimization_barrier(
            (part(3 + z), part(z - 3), first_map, dmixed)
        )
        steps.append(step(0, first_a, first_b))
    keep, send, color_grad = call(
        hidden_grad_kernel,
        [shape((4, pixels, 128), f32), shape((4, pixels, 128), f32), shape((16, 128), f32)],
        dmixed,
        wide,
        dtanh_all,
        gated,
        scratch=[pltpu.VMEM((2 * PIX, TAPS * 128), bf16)],
        us=18,
        name="hidden_grad",
    )
    heads, *crit_grads = call(
        critic_kernel,
        [shape((8, 512), f32)] + [shape((KP[k], KP[k]), f32) for k in range(4)],
        scalars,
        share,
        first_map,
        reals,
        head_rows,
        left_rows,
        sigma_rows,
        *frozen,
        *matrices,
        *right_cols,
        smem=(0,),
        scratch=[pltpu.VMEM((1024, 1024), bf16), pltpu.VMEM((SLOTS * PIX, 8), bf16)],
        us=12,
        name="critic",
    )
    if groups == 4:
        got, keep, send, heads = lax.optimization_barrier((steps[0], keep, send, heads))
        steps.append(step(1, *got))
    keep = keep + swap(send, "c")
    first, second = keep[:, : pixels // 2], keep[:, pixels // 2 :]
    first = first[:2] + swap(first[2:], "y")
    second = second[::2] + swap(second[1::2], "x")
    crit_grad = jnp.concatenate([crit_grads[k][: KS[k], : KS[k]].reshape(-1) for k in range(4)])
    crit_grad = crit_grad.reshape(groups, GROUP, crit_length)
    color_part = jnp.stack([color_grad[c, :64] + color_grad[8 + c, 64:] for c in range(3)], axis=1)
    color_full = lax.dynamic_update_slice(jnp.zeros((GOUT, 3), f32), color_part, (q * 64, 0))
    message = jnp.concatenate(
        [heads[k, : KS[k]] for k in range(4)]
        + [color_full.reshape(-1), heads[4, 0:1], heads[4, 128:129]]
    )
    message = jnp.pad(message, (0, 3072 - message.shape[0]))
    crit_sent = jnp.transpose(crit_grad, (1, 0, 2)).reshape(GROUP, groups * crit_length)
    both = jnp.concatenate([crit_sent, jnp.broadcast_to(message, (GROUP, 3072))], axis=1)
    width = both.shape[1]
    both = jnp.pad(both, ((0, 0), (0, -width % 1024))).reshape(GROUP, -1, 128)
    if groups == 4:
        got, first, second, both = lax.optimization_barrier((steps[1], first, second, both))
        steps.append(step(2, *got))
    first = first[0] + swap(first[1], "x")
    second = second[0] + swap(second[1], "y")
    dhidden = jnp.concatenate([first, second])
    first_grad = call(
        first_grad_kernel,
        shape((ROWS_FIRST, 128), f32),
        me,
        dhidden,
        pre,
        noise_all,
        smem=(0,),
        us=4,
        name="first_grad",
    )
    if groups == 4:
        got_first = [lax.ppermute(first_grad, "z", [(k, 0)]) for k in (1, 2, 3)]
        first_sum = first_grad + got_first[0] + got_first[1] + got_first[2]

        reduced = part(z) + steps[2][0] + steps[2][1]
    else:
        first_sum = lax.psum(first_grad, "z")
        reduced = lax.psum_scatter(grad, "z", scatter_dimension=0, tiled=True)
    first_sum = jnp.where(z == 0, first_sum, 0.0)
    reduced = jnp.concatenate([reduced[:ROWS_FIRST] + first_sum, reduced[ROWS_FIRST:]], axis=0)
    reduced = lax.all_to_all(reduced.reshape(GROUP, rows, 128), PLANE, 0, 0, tiled=True)

    both = lax.all_to_all(both, PLANE, 0, 0, tiled=True)
    both = jnp.sum(both, axis=0).reshape(-1)
    message = both[groups * crit_length : groups * crit_length + 3072]
    both = jnp.concatenate(
        [
            both[: groups * crit_length].reshape(groups, crit_length),
            jnp.broadcast_to(message, (groups, 3072)),
        ],
        axis=1,
    )
    width = both.shape[1]
    both = jnp.pad(both, ((0, 0), (0, -width % 1024))).reshape(groups, -1, 128)
    both = lax.all_to_all(both, "z", 0, 0, tiled=True)
    both = jnp.sum(both, axis=0).reshape(-1)
    crit_reduced = both[:crit_length]
    message = both[crit_length : crit_length + 3072]
    head_reduced, losses = message[:2496], message[2496:2498]

    fix = 1.0 - jnp.power(f32(beta_first), update_ordinal[0].astype(f32))
    flat = (8 * rows, 128)
    gen = call(
        adam_kernel,
        [shape(flat, f32)] * 3,
        fix.reshape(1),
        reduced,
        maker_weight_arrays.reshape(flat),
        maker_mean_estimate.reshape(flat),
        maker_variance_estimate.reshape(flat),
        smem=(0,),
        us=6,
        name="adam",
    )
    gen = [x.reshape(-1) for x in gen]
    crit = adamw_update(
        judge_weight_arrays, judge_mean_estimate, judge_variance_estimate, crit_reduced, fix
    )
    head = adamw_update(
        output_weight_rows, output_mean_estimate, output_variance_estimate, head_reduced, fix
    )
    return (*gen, *crit, *head, losses, power_new)


def solution(mesh):
    groups = mesh.shape["dp"] * mesh.shape["scale"] // GROUP
    grid = Mesh(mesh.devices.reshape(groups, 2, 2, 2), EVERY)
    split = P(EVERY)
    return jax.shard_map(
        functools.partial(local, groups),
        mesh=grid,
        in_specs=(split,) * 7 + (P(), split, P()) + (split,) * 6 + (P(),) * 3,
        out_specs=(split,) * 6 + (P(),) * 5,
        check_vma=False,
    )
```

```python
import functools

import jax
import jax.numpy as jnp
from jax import lax
from jax.experimental import pallas as pl
from jax.experimental.pallas import tpu as pltpu
from jax.sharding import Mesh
from jax.sharding import PartitionSpec as P

S = 32
Z = 256
GIN = 1024
GOUT = 512
CS = (24, 40, 112, 320)
KS = (64, 128, 256, 512)
CP = (128, 128, 128, 384)
KP = (128, 128, 256, 512)
SLOTS = 4
PIX = 256
GROUP = 8
IMAGE_TILES = 340
ROWS_FIRST = 256
TAPS = 9

leak_slope = 0.2
learn_rate = 0.03
beta_first = 0.5
beta_second = 0.5
adam_epsilon = 1e-08
weight_decay = 0.0001
norm_epsilon = 1e-06

f32 = jnp.float32
bf16 = jnp.bfloat16
PLANE = ("y", "x", "c")
EVERY = ("z", "y", "x", "c")
VMEM_LIMIT = 60 * 1024 * 1024

NN = (((1,), (0,)), ((), ()))
NT = (((1,), (1,)), ((), ()))
TN = (((0,), (0,)), ((), ()))


def dot(a, b, dims=NN):
    return lax.dot_general(a, b, dims, preferred_element_type=f32)


def call(kernel, out_shape, *args, scratch=(), smem=(), hbm=(), us=5, name=None):
    vmem = pl.BlockSpec(memory_space=pltpu.VMEM)
    spaces = {i: pl.BlockSpec(memory_space=pltpu.SMEM) for i in smem}
    spaces.update({i: pl.BlockSpec(memory_space=pl.ANY) for i in hbm})
    single = not isinstance(out_shape, (list, tuple))
    return pl.pallas_call(
        kernel,
        out_shape=out_shape,
        in_specs=[spaces.get(i, vmem) for i in range(len(args))],
        out_specs=vmem if single else [vmem] * len(out_shape),
        scratch_shapes=list(scratch),
        compiler_params=pltpu.CompilerParams(vmem_limit_bytes=VMEM_LIMIT),
        cost_estimate=pl.CostEstimate(
            flops=int(us * 1e8), bytes_accessed=int(us * 3e5), transcendentals=0
        ),
        name=name,
    )(*args)


def shape(dims, dtype):
    return jax.ShapeDtypeStruct(dims, dtype)


def split_two(x):
    high = x.astype(bf16)
    return high, (x - high.astype(f32)).astype(bf16)


def split_three(x):
    high = x.astype(bf16)
    rest = x - high.astype(f32)
    middle = rest.astype(bf16)
    return high, middle, (rest - middle.astype(f32)).astype(bf16)


def pack_kernel(w_ref, o_ref):
    rows = o_ref.shape[1]
    low_half = lax.broadcasted_iota(jnp.int32, (rows, 128), 1) < 64
    for j in range(4):
        a = w_ref[pl.ds(j, rows, stride=8), :]
        b = w_ref[pl.ds(j + 4, rows, stride=8), :]
        o_ref[2 * j] = jnp.where(low_half, a, pltpu.roll(b, 64, 1)).astype(bf16)
        o_ref[2 * j + 1] = jnp.where(low_half, pltpu.roll(a, 64, 1), b).astype(bf16)


def adam_kernel(fix_ref, g_ref, p_ref, m_ref, v_ref, po_ref, mo_ref, vo_ref):
    rows = g_ref.shape[1]
    low_half = lax.broadcasted_iota(jnp.int32, (rows, 128), 1) < 64
    for j in range(8):
        a = g_ref[2 * (j % 4)]
        b = g_ref[2 * (j % 4) + 1]
        if j < 4:
            g = jnp.where(low_half, a, pltpu.roll(b, 64, 1))
        else:
            g = jnp.where(low_half, pltpu.roll(a, 64, 1), b)
        at = pl.ds(j, rows, stride=8)
        new, first, second = adamw_update(p_ref[at, :], m_ref[at, :], v_ref[at, :], g, fix_ref[0])
        po_ref[at, :] = new
        mo_ref[at, :] = first
        vo_ref[at, :] = second


def adamw_update(master, first, second, grad, fix):
    first_new = beta_first * first + (1.0 - beta_first) * grad
    second_new = beta_second * second + (1.0 - beta_second) * grad * grad
    update = first_new / fix / (jnp.sqrt(second_new / fix) + adam_epsilon)
    return master - learn_rate * (update + weight_decay * master), first_new, second_new


SLOT_MASK = tuple(((m >> 1) & 1) * 4 + (m & 1) * 2 + (m >> 2) for m in range(GROUP))
SLOT_FIRST = tuple(2 * (m & 1) + ((m >> 1) & 1) for m in range(4))
SLOT_SECOND = tuple(4 + m for m in range(4))
NOISE_MASK = tuple((m & 1) * 4 + ((m >> 1) & 1) * 2 + (m >> 2) for m in range(GROUP))


def pre_kernel(me_ref, noise_ref, w_ref, pre_ref, hid_ref):
    for m in range(GROUP):
        rows = pl.ds(pl.multiple_of((me_ref[0] ^ NOISE_MASK[m]) * PIX, PIX), PIX)
        pre = dot(noise_ref[m], w_ref[...], TN)
        pre_ref[rows, :] = pre
        hid_ref[rows, :] = (pre * jax.nn.sigmoid(pre)).astype(bf16)


def turn_kernel(near_ref, far_ref, o_ref):
    for m in range(GROUP):
        source = near_ref if m < 4 else far_ref
        for part, at in enumerate((SLOT_FIRST[m % 4], SLOT_SECOND[m % 4])):
            o_ref[128 * m : 128 * m + 128, 1024 * part : 1024 * part + 1024] = jnp.transpose(
                source[at]
            )


def pixel_column():
    return lax.broadcasted_iota(jnp.int32, (PIX, 128), 0) & 15


def from_left(x, column):
    return jnp.where(column > 0, pltpu.roll(x, 1, 0), 0.0)


def from_right(x, column):
    return jnp.where(column < 15, pltpu.roll(x, PIX - 1, 0), 0.0)


def from_above(x):
    return jnp.concatenate([jnp.zeros((16, x.shape[1]), x.dtype), x[:-16]], axis=0)


def from_below(x):
    return jnp.concatenate([x[16:], jnp.zeros((16, x.shape[1]), x.dtype)], axis=0)


def block_row(tap, q, half):
    return ROWS_FIRST + tap * GIN + half * GOUT + q * 64


def forward_kernel(*refs):
    me_ref, near_ref, far_ref, color_ref = refs[:4]
    factor_ref, gated_ref, rgb_ref, wide, parts, w_ref, sem = refs[-7:]
    blocks = refs[4:-7]
    chunk = w_ref.shape[0] // 4
    if len(blocks) == 1:
        copy = pltpu.make_async_copy(blocks[0], w_ref, sem)
        copy.start()
        copy.wait()
    else:
        for here in range(4):

            @pl.when(me_ref[1] == here)
            def _():
                for k in range(4):
                    pltpu.make_async_copy(
                        blocks[3 + k - here].at[pl.ds(0, chunk), :],
                        w_ref.at[pl.ds(k * chunk, chunk), :],
                        sem,
                    ).start()

        pltpu.make_async_copy(w_ref, w_ref, sem).wait()
    for m in range(GROUP):
        q = me_ref[0] ^ SLOT_MASK[m]
        for tap in range(TAPS):
            for half in range(2):
                at = m * 128 + half * 64
                row = pl.multiple_of(block_row(tap, q, half), 64)
                wide[at : at + 64, 128 * tap : 128 * tap + 128] = w_ref[pl.ds(row, 64), :]
    wide[:, 128 * TAPS :] = jnp.zeros((GIN, 128), bf16)
    low_half = lax.broadcasted_iota(jnp.int32, (PIX, 128), 1) < 64
    column = pixel_column()
    color_high, color_low = split_two(color_ref[...])
    color = jnp.concatenate([color_high, color_low], axis=0)

    @pl.loop(0, 4)
    def _(pair):
        start = pl.multiple_of(pair * 512, 512)
        local = pl.multiple_of((pair & 1) * 512, 512)
        first = pair < 2
        left = []
        for m in range(GROUP):
            at = jnp.where(first, SLOT_FIRST[m % 4], SLOT_SECOND[m % 4])
            left.append((near_ref if m < 4 else far_ref)[at, pl.ds(local, 512), :])
        left = jnp.concatenate(left, axis=1)
        for k in range(5):
            y = dot(left, wide[:, 256 * k : 256 * k + 256])
            parts[2 * k] = y[:, :128]
            if k < 4:
                parts[2 * k + 1] = y[:, 128:]
        for one in range(2):
            rows = pl.ds(pl.multiple_of(start + one * PIX, PIX), PIX)
            here = slice(one * PIX, one * PIX + PIX)
            cols = []
            for a in range(3):
                y0, y1, y2 = (parts[3 * a + b, here, :] for b in range(3))
                cols.append((from_left(y0, column) + (y1 + y2), (y0 + y1) + from_right(y2, column)))
            for pi in range(2):
                gated = []
                for pj in range(2):
                    if pi == 0:
                        mixed = from_above(cols[0][pj]) + (cols[1][pj] + cols[2][pj])
                    else:
                        mixed = (cols[0][pj] + cols[1][pj]) + from_below(cols[2][pj])
                    turned = pltpu.roll(mixed, 64, 1)
                    gate = jax.nn.sigmoid(jnp.where(low_half, turned, mixed))
                    value = jnp.where(low_half, mixed, turned)
                    gated.append(value * gate)
                    factor_ref[2 * pi + pj, rows, :] = jnp.where(
                        low_half, gate, gated[-1] * (1.0 - gate)
                    )
                both = jnp.where(low_half, gated[0], gated[1])
                gated_ref[pi, rows, :] = both
                high, low = split_two(both)
                rgb = dot(color, jnp.concatenate([high, low], axis=1), NT)
                rgb_ref[2 * pair + one, 16 * pi : 16 * pi + 16, :] = rgb[:16] + rgb[16:]


def tap_sums(parts, column):
    sums = []
    for a in range(3):
        line = []
        for pj in range(2):
            even, odd = parts[pj], parts[2 + pj]
            if a == 0:
                line.append(odd + from_below(even))
            elif a == 1:
                line.append(even + odd)
            else:
                line.append(from_above(odd) + even)
        sums.append(line[1] + from_right(line[0], column))
        sums.append(line[0] + line[1])
        sums.append(from_left(line[1], column) + line[0])
    return sums


def weight_grad_kernel(me_ref, dt_ref, factor_ref, hid_ref, color_ref, g_ref, dm_ref, moved):
    column = pixel_column()
    g_ref[:ROWS_FIRST, :] = jnp.zeros((ROWS_FIRST, 128), f32)

    @pl.loop(0, GROUP)
    def _(b):
        rows = pl.ds(pl.multiple_of(b * PIX, PIX), PIX)
        turned = jnp.transpose(dt_ref[b])
        for phase in range(4):
            pi, pj = phase // 2, phase % 2
            spread = turned[:, 8 * phase : 8 * phase + 1] * color_ref[0:1, :]
            for c in (1, 2):
                spread = spread + turned[:, 8 * phase + c : 8 * phase + c + 1] * color_ref[c : c + 1, :]
            low = (spread * factor_ref[phase, rows, :]).astype(bf16)
            dm_ref[phase, rows, :] = low
            plain = low.astype(f32)
            side = (from_right if pj == 0 else from_left)(plain, column)
            lanes = slice(128 * pj, 128 * pj + 128)
            for k, value in enumerate((plain, side)):
                line = (from_below if pi == 0 else from_above)(value)
                moved[4 * pi + k, rows, lanes] = value.astype(bf16)
                moved[4 * pi + 2 + k, rows, lanes] = line.astype(bf16)

    def column_sums(at):
        plain = dot(hid_ref[...], moved[at])
        side = dot(hid_ref[...], moved[at + 1])
        return (
            plain[:, 128:] + side[:, :128],
            plain[:, :128] + plain[:, 128:],
            side[:, 128:] + plain[:, :128],
        )

    def put(tap, value, add):
        for m in range(GROUP):
            for half in range(2):
                q = me_ref[0] ^ SLOT_MASK[m]
                at = pl.ds(pl.multiple_of(block_row(tap, q, half), 64), 64)
                piece = value[128 * m + 64 * half : 128 * m + 64 * half + 64]
                g_ref[at, :] = g_ref[at, :] + piece if add else piece

    for at, takes in ((0, ((1, False), (2, False))), (4, ((0, False), (1, True)))):
        for b, value in enumerate(column_sums(at)):
            for a, add in takes:
                put(3 * a + b, value, add)
    for at, a in ((2, 0), (6, 2)):
        for b, value in enumerate(column_sums(at)):
            put(3 * a + b, value, True)


def hidden_grad_kernel(
    dm_ref, wide_ref, dt_ref, gated_ref, keep_ref, send_ref, rgb_ref, sums, color
):
    column = pixel_column()
    color[...] = jnp.zeros_like(color)

    @pl.loop(0, GROUP)
    def _(b):
        rows = pl.ds(pl.multiple_of(b * PIX, PIX), PIX)
        parts = [dm_ref[phase, rows, :].astype(f32) for phase in range(4)]
        for tap, total in enumerate(tap_sums(parts, column)):
            high, low = split_two(total)
            sums[:PIX, 128 * tap : 128 * tap + 128] = high
            sums[PIX:, 128 * tap : 128 * tap + 128] = low
        for k in range(4):
            out = dot(sums[...], wide_ref[256 * k : 256 * k + 256, : 128 * TAPS], NT)
            out = out[:PIX] + out[PIX:]
            put = keep_ref if k < 2 else send_ref
            put[2 * (k % 2), rows, :] = out[:, :128]
            put[2 * (k % 2) + 1, rows, :] = out[:, 128:]
        for pi in range(2):
            high, low = split_two(dt_ref[b, 16 * pi : 16 * pi + 16, :])
            g_high, g_low = split_two(gated_ref[pi, rows, :])
            left = jnp.concatenate([high, low], axis=0)
            out = dot(left, jnp.concatenate([g_high, g_low], axis=1))
            color[...] += out[:16, :128] + (out[:16, 128:] + out[16:, :128])

    low_half = lax.broadcasted_iota(jnp.int32, (8, 128), 1) < 64
    folded = color[:8, :] + pltpu.roll(color[8:, :], 64, 1)
    rgb_ref[...] = jnp.where(low_half, folded, 0.0)


def first_grad_kernel(me_ref, dh_ref, pre_ref, noise_ref, o_ref):
    o_ref[...] = jnp.zeros_like(o_ref)
    for m in range(GROUP):
        rows = pl.ds(pl.multiple_of((me_ref[0] ^ NOISE_MASK[m]) * PIX, PIX), PIX)
        pre = pre_ref[rows, :]
        gate = jax.nn.sigmoid(pre)
        slope = gate * (1.0 + pre * (1.0 - gate))
        o_ref[...] += dot(noise_ref[m], (slope * dh_ref[rows, :]).astype(bf16))


def row_normalized(row):
    return row * lax.rsqrt(jnp.sum(row * row, axis=1, keepdims=True) + norm_epsilon)


def row_times(row, matrix, dims):
    pieces = jnp.concatenate(
        [jnp.broadcast_to(x.astype(f32), (8, row.shape[1])) for x in split_three(row)], axis=0
    ).astype(bf16)
    out = dot(pieces, matrix, dims)
    return out[0:1] + out[8:9] + out[16:17]


INS = (3,) + CS[:3]
CRIT_AT = (0, 4096, 20480, 86016)


def window(length):
    rows = length // 128 if length % 128 == 0 else -(-(127 + length) // 128)
    return -(-rows // 16) * 16


def prepare_kernel(
    crit_length, frozen_length, small_ref, own_ref, u_ref,
    e1, e2, e3, e4, r1, r2, r3, r4, m1, m2, m3, m4, c1, c2, c3, c4,
    left_ref, sigma_ref, share_ref, crit, frozen, moved, rows_buf,
):
    devices = small_ref.shape[0]
    crit_rows, frozen_rows = window(crit_length), window(frozen_length)
    crit[...] = jnp.zeros_like(crit)
    frozen[...] = jnp.zeros_like(frozen)
    for k in range(devices):
        at = pl.ds((k * crit_length) // 128, crit_rows)
        crit[at, :] += small_ref[k, :crit_rows, :].astype(f32)
        at = pl.ds((k * frozen_length) // 128, frozen_rows)
        frozen[at, :] += small_ref[k, crit_rows : crit_rows + frozen_rows, :].astype(f32)
    live = jnp.zeros((1, 128), f32)
    for k in range(devices):
        at = crit_rows + frozen_rows
        live += small_ref[k, at : at + 16, :].astype(f32)[0:1]
    lane = lax.broadcasted_iota(jnp.int32, (1, 128), 1)
    real = jnp.sum(jnp.where((lane > 0) & (lane < SLOTS), live, 0.0), axis=1, keepdims=True)
    count = jnp.where(lane == 0, live, real) * float(IMAGE_TILES)
    share_ref[...] = jnp.broadcast_to(own_ref[...] / jnp.maximum(count, 1.0), share_ref.shape)

    def lanes_of(x):
        return lax.broadcasted_iota(jnp.int32, x.shape, 1)

    def shifted(a, b, lane_at):
        if lane_at == 0:
            return a
        turn = 128 - lane_at
        return jnp.where(lanes_of(a) < turn, pltpu.roll(a, turn, 1), pltpu.roll(b, turn, 1))

    def halves(x):
        low = lanes_of(x) < 64
        return jnp.where(low, x, 0.0), jnp.where(low, pltpu.roll(x, 64, 1), 0.0)

    def flush(ref, rows):
        ref[...] = rows_buf[: ref.shape[0], :].astype(bf16)
        rows_buf[:rows, :] = jnp.zeros((rows, 128), f32)

    total = frozen.shape[0] - 8
    moved[...] = shifted(frozen[:total, :], frozen[1 : total + 1, :], 8)
    rows_buf[...] = jnp.zeros_like(rows_buf)
    for ref, offset, rows, width in ((e1, 0, INS[0], CS[0]), (e2, 72, INS[1], CS[1])):
        for r in range(rows):
            a, lane_at = divmod(offset + r * width, 128)
            row = shifted(frozen[a : a + 1, :], frozen[a + 1 : a + 2, :], lane_at)
            rows_buf[r : r + 1, :] = jnp.where(lane < width, row, 0.0)
        flush(ref, 32)
    for i in range(8):
        a, lane_at = divmod(112 * i, 128)
        row = shifted(
            moved[pl.ds(8 + a, 5, stride=7), :], moved[pl.ds(9 + a, 5, stride=7), :], lane_at
        )
        rows_buf[pl.ds(i, 5, stride=8), :] = jnp.where(lanes_of(row) < 112, row, 0.0)
    flush(e3, 40)
    five = [moved[pl.ds(43 + k, 56, stride=5), :] for k in range(5)]
    pairs = (
        (five[0], shifted(five[2], five[3], 64)),
        (five[1], shifted(five[3], five[4], 64)),
        (halves(five[2])[0], halves(five[4])[1]),
    )
    e4[...] = jnp.zeros_like(e4)
    for b, (even, odd) in enumerate(pairs):
        rows_buf[pl.ds(0, 56, stride=2), :] = even
        rows_buf[pl.ds(1, 56, stride=2), :] = odd
        e4[:112, 128 * b : 128 * b + 128] = rows_buf[:112, :].astype(bf16)
    rows_buf[...] = jnp.zeros_like(rows_buf)
    even, odd = halves(moved[323:335, :])
    rows_buf[pl.ds(0, 12, stride=2), :] = even
    rows_buf[pl.ds(1, 12, stride=2), :] = odd
    flush(r1, 24)
    rows_buf[:40, :] = moved[335:375, :]
    flush(r2, 40)
    r3[...] = jnp.zeros_like(r3)
    r4[...] = jnp.zeros_like(r4)
    for b in range(2):
        r3[:112, 128 * b : 128 * b + 128] = moved[pl.ds(375 + b, 112, stride=2), :].astype(bf16)
    for b in range(4):
        r4[:320, 128 * b : 128 * b + 128] = moved[pl.ds(599 + b, 320, stride=4), :].astype(bf16)
    even, odd = halves(crit[:32, :])
    rows_buf[pl.ds(0, 32, stride=2), :] = even
    rows_buf[pl.ds(1, 32, stride=2), :] = odd
    flush(m1, 64)
    m2[...] = crit[32:160, :].astype(bf16)
    for b in range(2):
        m3[:, 128 * b : 128 * b + 128] = crit[pl.ds(160 + b, 256, stride=2), :].astype(bf16)
    for b in range(4):
        m4[:, 128 * b : 128 * b + 128] = crit[pl.ds(672 + b, 512, stride=4), :].astype(bf16)

    left_ref[...] = jnp.zeros_like(left_ref)
    sigma_ref[...] = jnp.ones_like(sigma_ref)
    for k, (m_ref, c_ref) in enumerate(((m1, c1), (m2, c2), (m3, c3), (m4, c4))):
        width = KP[k]
        matrix = m_ref[...]
        right = row_normalized(row_times(u_ref[k : k + 1, :width], matrix, NT))
        turned = row_times(right, matrix, NN)
        left = row_normalized(turned)
        left_ref[k : k + 1, :width] = left
        sigma = jnp.sum(left * turned, axis=1, keepdims=True)
        sigma_ref[k : k + 1, :] = jnp.broadcast_to(sigma, (1, 128))
        c_ref[...] = jnp.transpose(jnp.broadcast_to(right, (128, width)))


def wanted_code(scal_ref, slot):
    d = lax.broadcasted_iota(jnp.int32, (1, 1024), 1)

    def bit(k):
        return (d >> k) & 1

    i = bit(9) + 2 * bit(7) + 4 * bit(5) + 8 * bit(3) + 16 * bit(1)
    j = bit(8) + 2 * bit(6) + 4 * bit(4) + 8 * bit(2) + 16 * bit(0)
    down, across, flip, top, side = (scal_ref[slot, k] for k in range(5))
    row = i - down
    moved = j - across
    fine = (row >= 0) & (row < S) & (moved >= 0) & (moved < S)
    source = jnp.where(flip == 1, S - 1 - moved, moved)
    boxed = (i >= top) & (i < top + S // 2) & (j >= side) & (j < side + S // 2)
    return jnp.where(fine & jnp.logical_not(boxed), row * S + source, -1)


def three(x):
    return jnp.concatenate([v.astype(f32) for v in split_three(x)], axis=0).astype(bf16)


def fold(x):
    return x[0:8] + x[8:16] + x[16:24]


def fill_pick(pick, scal_ref, slot, phases):
    want = wanted_code(scal_ref, slot)

    @pl.loop(0, 8)
    def _(k):
        s = lax.broadcasted_iota(jnp.int32, (128, 1024), 0) + k * 128
        if phases:
            at = s & 255
            s = (2 * (at >> 4) + (s >> 9)) * S + 2 * (at & 15) + ((s >> 8) & 1)
        hit = jnp.where(s == want, 1.0, 0.0).astype(bf16)
        pick[pl.ds(pl.multiple_of(k * 128, 128), 128), :] = hit


def augmented(image, pick):
    seen = fold(dot(three(image), pick[...]))
    small = 0.25 * ((seen[:, :256] + seen[:, 256:512]) + (seen[:, 512:768] + seen[:, 768:]))
    return jnp.transpose(small).astype(bf16)


def last_pool(slots):
    row = lax.broadcasted_iota(jnp.int32, (16, 16 * slots), 0)
    col = lax.broadcasted_iota(jnp.int32, (16, 16 * slots), 1)
    pool = jnp.where((row // 4 == col // 16) & (row % 4 == col % 4), 0.25, 0.0)
    return jnp.concatenate([pool.astype(bf16)] * 3, axis=1)


def critic_levels(inputs, slots, extract, project, matrices, head_ref, sigma_ref):
    levels = []
    pool = last_pool(slots)
    for k in range(4):
        count = 16 if k == 3 else (slots * PIX) >> (2 * k)
        width = KP[k]
        pre = dot(inputs, extract[k][...])
        active = pre * jax.nn.sigmoid(pre)
        feat = dot(active.astype(bf16), project[k][...]).astype(bf16)
        raw = dot(feat, matrices[k][...])
        sigma = sigma_ref[k : k + 1, 0:1]
        scaled = raw / sigma
        slope = jnp.where(scaled >= 0, 1.0, leak_slope)
        leaky = scaled * slope
        head = head_ref[k : k + 1, :width]
        scale = lax.rsqrt(jnp.sum(head * head, axis=1, keepdims=True) + norm_epsilon)
        unit = head * scale
        logit = jnp.sum(leaky * unit, axis=1, keepdims=True)
        levels.append((pre, feat, raw, sigma, slope, leaky, head, scale, unit, logit))
        if k < 2:
            blocks = active.reshape(slots, 4, count // (4 * slots), CP[k])
            total = (blocks[:, 0] + blocks[:, 1]) + (blocks[:, 2] + blocks[:, 3])
            inputs = (0.25 * total).reshape(count // 4, CP[k]).astype(bf16)
        elif k == 2:
            inputs = dot(pool, three(active)).astype(bf16)
    return levels


def image_grad_kernel(
    scal_ref,
    share_ref,
    got_ref,
    head_ref,
    sigma_ref,
    e1, e2, e3, e4,
    r1, r2, r3, r4,
    m1, m2, m3, m4,
    dt_ref,
    map_ref,
    pick,
):
    extract, project, matrices = (e1, e2, e3, e4), (r1, r2, r3, r4), (m1, m2, m3, m4)
    fill_pick(pick, scal_ref, 0, True)
    color = got_ref[0]
    for k in range(1, GROUP):
        color = color + got_ref[k]
    color = jnp.tanh(color)
    fake = jnp.concatenate([color[8 * k : 8 * k + 8] for k in range(4)], axis=1)
    first_map = augmented(fake, pick)
    map_ref[...] = first_map
    levels = critic_levels(first_map, 1, extract, project, matrices, head_ref, sigma_ref)
    row = lax.broadcasted_iota(jnp.int32, (16, 16), 0)
    col = lax.broadcasted_iota(jnp.int32, (16, 16), 1)
    spread = jnp.where((col < 4) & (row % 4 == col), 0.25, 0.0)
    spread = jnp.concatenate([spread.astype(bf16)] * 3, axis=1)
    carry = None
    for k in (3, 2, 1, 0):
        pre, feat, raw, sigma, slope, leaky, head, scale, unit, logit = levels[k]
        dlogit = -share_ref[0:1, 0:1] * jax.nn.sigmoid(-logit)
        if k == 3:
            dlogit = jnp.where(lax.broadcasted_iota(jnp.int32, (16, 1), 0) < 4, dlogit, 0.0)
        dscaled = dlogit * unit * slope
        dfeat = dot((dscaled / sigma).astype(bf16), matrices[k][...], NT).astype(bf16)
        dactive = dot(dfeat, project[k][...], NT)
        if carry is not None:
            dactive = dactive + carry
        gate = jax.nn.sigmoid(pre)
        dpre = (gate * (1.0 + pre * (1.0 - gate)) * dactive).astype(bf16)
        dinput = dot(dpre, extract[k][...], NT)
        if k == 3:
            carry = dot(spread, three(dinput))
        elif k > 0:
            carry = jnp.concatenate([0.25 * dinput] * 4, axis=0)
    daug = 0.25 * jnp.transpose(dinput)
    daug = jnp.concatenate([daug] * 4, axis=1)
    dimage = fold(dot(three(daug), pick[...], NT))
    dtanh = dimage * (1.0 - fake * fake)
    for k in range(4):
        dt_ref[8 * k : 8 * k + 8, :] = dtanh[:, 256 * k : 256 * k + 256]


def critic_kernel(
    scal_ref,
    share_ref,
    map_ref,
    real_ref,
    head_ref,
    left_ref,
    sigma_ref,
    e1, e2, e3, e4,
    r1, r2, r3, r4,
    m1, m2, m3, m4,
    c1, c2, c3, c4,
    color_ref,
    sent_ref,
    pick,
    first_map,
    corner,
    out_ref,
    flat_ref,
):
    extract, project = (e1, e2, e3, e4), (r1, r2, r3, r4)
    matrices, columns = (m1, m2, m3, m4), (c1, c2, c3, c4)
    first_map[:PIX, :] = map_ref[...]
    for slot in range(1, SLOTS):
        fill_pick(pick, scal_ref, slot, False)
        first_map[slot * PIX : slot * PIX + PIX, :] = augmented(real_ref[slot - 1], pick)
    levels = critic_levels(first_map[...], SLOTS, extract, project, matrices, head_ref, sigma_ref)
    loss_gen = jnp.zeros((1, 1), f32)
    loss_critic = jnp.zeros((1, 1), f32)
    out_ref[...] = jnp.zeros_like(out_ref)
    for k in range(4):
        pre, feat, raw, sigma, slope, leaky, head, scale, unit, logit = levels[k]
        count, width = logit.shape[0], KP[k]
        slot = lax.broadcasted_iota(jnp.int32, (count, 1), 0) // (count // SLOTS)
        share = share_ref[0:1, 0:1]
        for other in range(1, SLOTS):
            share = jnp.where(slot == other, share_ref[0:1, other : other + 1], share)
        sign = jnp.where(slot == 0, -1.0, 1.0)
        hinge = 1.0 - sign * logit
        loss_critic += jnp.sum(share * jnp.maximum(hinge, 0.0), axis=0, keepdims=True)
        dlogit = jnp.where(hinge > 0, -sign * share, 0.0)
        soft = jnp.maximum(-logit, 0.0) + jnp.log1p(jnp.exp(-jnp.abs(logit)))
        loss_gen += jnp.sum(jnp.where(slot == 0, share * soft, 0.0), axis=0, keepdims=True)
        dscaled = dlogit * unit * slope
        grad = dot(feat, (dscaled / sigma).astype(bf16), TN)
        dsigma = jnp.sum(jnp.sum(dscaled * raw, axis=1, keepdims=True), axis=0, keepdims=True)
        dsigma = -dsigma / (sigma * sigma)
        side = columns[k][...] * dsigma
        for b in range(width // 128):
            lanes = slice(128 * b, 128 * b + 128)
            piece = grad[:, lanes] + side * left_ref[k : k + 1, lanes]
            if k == 0:
                corner[...] = piece
                low = lax.broadcasted_iota(jnp.int32, (32, 128), 1) < 64
                even, odd = corner[pl.ds(0, 32, stride=2), :], corner[pl.ds(1, 32, stride=2), :]
                flat_ref[:32, :] = jnp.where(low, even, pltpu.roll(odd, 64, 1))
            else:
                stride = width // 128
                flat_ref[pl.ds(CRIT_AT[k] // 128 + b, width, stride=stride), :] = piece
        dunit = jnp.sum(leaky * dlogit, axis=0, keepdims=True)
        inner = jnp.sum(head * dunit, axis=1, keepdims=True)
        out_ref[k : k + 1, :width] = scale * dunit - head * (scale * scale * scale * inner)
    out_ref[4:5, 0:128] = jnp.broadcast_to(loss_gen, (1, 128))
    out_ref[4:5, 128:256] = jnp.broadcast_to(loss_critic, (1, 128))
    rows = sent_ref.shape[1] - 40
    if sent_ref.shape[0] == GROUP:
        groups = rows // 85
        for q in range(GROUP):
            for z in range(groups):
                at = (z * GROUP + q) * 85
                sent_ref[q, z * 85 : z * 85 + 85, :] = flat_ref[at : at + 85, :]
            sent_ref[q, groups * 85 : rows, :] = jnp.zeros((rows - groups * 85, 128), f32)
    else:
        sent_ref[0, :rows, :] = flat_ref[...]
    for q in range(sent_ref.shape[0]):
        for k in range(8):
            for b in range(4):
                at = rows + 4 * k + b
                sent_ref[q, at : at + 1, :] = out_ref[k : k + 1, 128 * b : 128 * b + 128]
        sent_ref[q, rows + 32 :, :] = color_ref[...]


def local(
    groups,
    noise_maps,
    dataset_lowres_images,
    dataset_highres_images,
    occupied_mask,
    shift_amounts,
    mirror_indicator,
    erase_box_corner,
    update_ordinal,
    fixed_backbone_params,
    singular_estimate_dirs,
    maker_weight_arrays,
    maker_mean_estimate,
    maker_variance_estimate,
    judge_weight_arrays,
    judge_mean_estimate,
    judge_variance_estimate,
    output_weight_rows,
    output_mean_estimate,
    output_variance_estimate,
):
    devices = groups * GROUP
    rows = maker_weight_arrays.shape[0] // 1024
    chunk = GROUP * rows
    z = lax.axis_index("z")
    q = (lax.axis_index("y") * 2 + lax.axis_index("x")) * 2 + lax.axis_index("c")
    me = jnp.stack([q, z]).astype(jnp.int32)

    def pad_rows(x):
        return jnp.pad(x, ((0, 0), (0, -x.shape[1] % 1024))).reshape(x.shape[0], -1, 128)

    def swap(x, axis):
        return lax.ppermute(x, axis, [(0, 1), (1, 0)])

    crit_length = judge_weight_arrays.shape[0]
    frozen_length = fixed_backbone_params.shape[0]
    member = z * GROUP + q

    def windowed(x):
        length = x.shape[0]
        rows_here = window(length)
        if length % 128 == 0:
            return jnp.pad(x.reshape(-1, 128), ((0, rows_here - length // 128), (0, 0)))
        empty = jnp.zeros((rows_here * 128,), bf16)
        start = lax.rem(member * length, 128)
        return lax.dynamic_update_slice(empty, x, (start,)).reshape(rows_here, 128)

    own = occupied_mask.astype(f32)
    small = jnp.concatenate(
        [
            windowed(judge_weight_arrays.astype(bf16)),
            windowed(fixed_backbone_params),
            jnp.pad(own.astype(bf16), ((0, 15), (0, 128 - SLOTS))),
        ]
    )

    def rows_of(flat):
        out, offset = [], 0
        for k in range(4):
            out.append(jnp.pad(flat[offset : offset + KS[k]], (0, 512 - KS[k])))
            offset += KS[k]
        return jnp.pad(jnp.stack(out), ((0, 4), (0, 0)))

    head_rows = rows_of(output_weight_rows)
    start_rows = rows_of(singular_estimate_dirs)
    own_row = jnp.pad(own, ((0, 0), (0, 128 - SLOTS)))
    color_all = output_weight_rows[960:].reshape(GOUT, 3)
    color = jnp.pad(lax.dynamic_slice(color_all, (q * 64, 0), (64, 3)).T, ((0, 5), (0, 0)))
    none = jnp.zeros_like(color)
    color_left = jnp.concatenate(
        [
            jnp.concatenate([color, none, color, none], axis=1),
            jnp.concatenate([none, color, none, color], axis=1),
        ],
        axis=0,
    )
    color_twice = jnp.concatenate([color, color], axis=1)
    small_images = dataset_lowres_images.astype(f32)
    large = dataset_highres_images.astype(f32).reshape(1, 3, S, 2, S, 2)
    large = jnp.mean(large, axis=(3, 5)).reshape(1, 3, S * S)
    reals = jnp.pad(jnp.concatenate([small_images, large]), ((0, 0), (0, 5), (0, 0)))
    scalars = jnp.concatenate(
        [shift_amounts[0], mirror_indicator[0][:, None], erase_box_corner[0]], axis=1
    )

    noise_all = jnp.concatenate([noise_maps, swap(noise_maps, "y")])

    packed = call(
        pack_kernel,
        shape((GROUP, rows, 128), bf16),
        maker_weight_arrays.reshape(8 * rows, 128),
        us=3,
        name="pack",
    )
    slices = lax.all_to_all(packed, PLANE, 0, 0, tiled=True).reshape(chunk, 128)
    slices, noise_all = lax.optimization_barrier((slices, noise_all))
    for axis in ("x", "c"):
        noise_all = jnp.concatenate([noise_all, swap(noise_all, axis)])
    first_block = slices[:ROWS_FIRST]

    def hop(x, y):
        down = lax.ppermute(x, "z", [(0, 1), (1, 2), (2, 3)])
        return down, lax.ppermute(y, "z", [(1, 0), (2, 1), (3, 2)])

    if groups == 4:
        sent = [lax.ppermute(first_block, "z", [(0, k)]) for k in (1, 2, 3)]
        riding = jnp.concatenate([slices, small])
        hop_one = hop(riding, riding)
        ready = (head_rows, start_rows, own_row, color_left, color_twice, reals, scalars, me)
        sent, hop_one, ready = lax.optimization_barrier((sent, hop_one, ready))
        head_rows, start_rows, own_row, color_left, color_twice, reals, scalars, me = ready
        first_weights = jnp.where(z == 0, first_block, sent[0] + sent[1] + sent[2])
        hop_two = hop(*hop_one)
    else:
        first_weights = lax.all_gather(first_block, "z", axis=0)[0]
        blocks = [lax.all_gather(slices, "z", axis=0, tiled=True)]

    pixels = GROUP * PIX
    pre, hid = call(
        pre_kernel,
        [shape((pixels, 128), f32), shape((pixels, 128), bf16)],
        me,
        noise_all,
        first_weights,
        smem=(0,),
        us=4,
        name="pre",
    )
    first, second = hid[: pixels // 2], hid[pixels // 2 :]
    first = jnp.stack([first, swap(first, "y")])
    second = jnp.stack([second, swap(second, "x")])
    if groups == 4:
        first, second, hop_two = lax.optimization_barrier((first, second, hop_two))
        hop_three = hop(*hop_two)
    first = jnp.concatenate([first, swap(first, "x")])
    second = jnp.concatenate([second, swap(second, "y")])
    if groups == 4:
        first, second, hop_three = lax.optimization_barrier((first, second, hop_three))
        blocks = [hop_three[0], hop_two[0], hop_one[0], riding, hop_one[1], hop_two[1], hop_three[1]]
        small = lax.dynamic_slice_in_dim(jnp.stack([x[chunk:] for x in blocks]), 3 - z, 4, axis=0)
    else:
        small = lax.all_gather(small, "z", axis=0)
    near = jnp.concatenate([first, second])
    far = swap(near, "c")
    near, far, small = lax.optimization_barrier((near, far, small))
    small = lax.all_to_all(jnp.broadcast_to(small, (GROUP,) + small.shape), PLANE, 0, 0, tiled=True)
    factor, gated, rgb, wide = call(
        forward_kernel,
        [
            shape((4, pixels, 128), f32),
            shape((2, pixels, 128), f32),
            shape((GROUP, 32, PIX), f32),
            shape((GIN, 1280), bf16),
        ],
        me,
        near,
        far,
        color_left,
        *blocks,
        smem=(0,),
        hbm=range(4, 4 + len(blocks)),
        scratch=[
            pltpu.VMEM((TAPS + 1, 512, 128), f32),
            pltpu.VMEM((groups * chunk, 128), bf16),
            pltpu.SemaphoreType.DMA,
        ],
        us=14,
        name="forward",
    )
    got = lax.all_to_all(rgb, PLANE, 0, 0, tiled=True)
    near, far, factor, small = lax.optimization_barrier((near, far, factor, small))
    small = jnp.swapaxes(small, 0, 1).reshape((devices,) + small.shape[2:])
    squares = [shape((8, CP[0]), bf16)] + [shape((CP[k - 1], CP[k]), bf16) for k in (1, 2, 3)]
    squares += [shape((CP[k], KP[k]), bf16) for k in range(4)]
    squares += [shape((KP[k], KP[k]), bf16) for k in range(4)]
    squares += [shape((KP[k], 128), f32) for k in range(4)]
    squares += [shape((8, 512), f32), shape((8, 128), f32), shape((8, 128), f32)]
    crit_space = -(-((devices - 1) * crit_length // 128 + window(crit_length)) // 8) * 8
    frozen_space = -(-((devices - 1) * frozen_length // 128 + window(frozen_length)) // 8) * 8 + 8
    prepared = call(
        functools.partial(prepare_kernel, crit_length, frozen_length),
        squares,
        small,
        own_row,
        start_rows,
        scratch=[
            pltpu.VMEM((crit_space, 128), f32),
            pltpu.VMEM((frozen_space, 128), f32),
            pltpu.VMEM((frozen_space - 8, 128), f32),
            pltpu.VMEM((128, 128), f32),
        ],
        us=8,
        name="prepare",
    )
    frozen, matrices, right_cols = prepared[:8], prepared[8:12], prepared[12:16]
    left_rows, sigma_rows, share = prepared[16:]
    power_new = jnp.concatenate([left_rows[k, : KS[k]] for k in range(4)])
    dtanh, first_map = call(
        image_grad_kernel,
        [shape((32, PIX), f32), shape((PIX, 8), bf16)],
        scalars,
        share,
        got,
        head_rows,
        sigma_rows,
        *frozen,
        *matrices,
        smem=(0,),
        scratch=[pltpu.VMEM((1024, 1024), bf16)],
        us=8,
        name="image_grad",
    )

    near, far, dtanh = lax.optimization_barrier((near, far, dtanh))
    hid_turned = call(turn_kernel, shape((GIN, pixels), bf16), near, far, us=5, name="turn")
    dtanh_all = lax.all_to_all(
        jnp.broadcast_to(dtanh, (GROUP,) + dtanh.shape), PLANE, 0, 0, tiled=True
    )
    grad, dmixed = call(
        weight_grad_kernel,
        [shape((ROWS_FIRST + TAPS * GIN, 128), f32), shape((4, pixels, 128), bf16)],
        me,
        dtanh_all,
        factor,
        hid_turned,
        color_twice,
        smem=(0,),
        scratch=[pltpu.VMEM((8, pixels, 256), bf16)],
        us=20,
        name="weight_grad",
    )
    steps = []
    if groups == 4:

        def part(k):
            return lax.dynamic_slice_in_dim(grad, jnp.clip(k, 0, 3) * chunk, chunk, axis=0)

        def step(s, a, b):
            if s == 1:
                a, b = part(2 + z) + a, part(z - 2) + b
            down = lax.ppermute(a, "z", [(k, k + 1) for k in range(s + 1)])
            up = lax.ppermute(b, "z", [(3 - k, 2 - k) for k in range(s + 1)])
            return lax.optimization_barrier((down, up))

        first_a, first_b, first_map, dmixed = lax.optimization_barrier(
            (part(3 + z), part(z - 3), first_map, dmixed)
        )
        steps.append(step(0, first_a, first_b))
    keep, send, color_grad = call(
        hidden_grad_kernel,
        [shape((4, pixels, 128), f32), shape((4, pixels, 128), f32), shape((8, 128), f32)],
        dmixed,
        wide,
        dtanh_all,
        gated,
        scratch=[pltpu.VMEM((2 * PIX, TAPS * 128), bf16), pltpu.VMEM((16, 128), f32)],
        us=18,
        name="hidden_grad",
    )
    aligned = crit_length == 85 * 128
    sent_rows = -(-85 * groups // 8) * 8 if aligned else devices * crit_length // 128
    both = call(
        critic_kernel,
        shape((GROUP if aligned else 1, sent_rows + 40, 128), f32),
        scalars,
        share,
        first_map,
        reals,
        head_rows,
        left_rows,
        sigma_rows,
        *frozen,
        *matrices,
        *right_cols,
        color_grad,
        smem=(0,),
        scratch=[
            pltpu.VMEM((1024, 1024), bf16),
            pltpu.VMEM((SLOTS * PIX, 8), bf16),
            pltpu.VMEM((128, 128), f32),
            pltpu.VMEM((8, 512), f32),
            pltpu.VMEM((devices * crit_length // 128, 128), f32),
        ],
        us=12,
        name="critic",
    )
    if groups == 4:
        got, keep, send, both = lax.optimization_barrier((steps[0], keep, send, both))
        steps.append(step(1, *got))
    keep = keep + swap(send, "c")
    first, second = keep[:, : pixels // 2], keep[:, pixels // 2 :]
    first = first[:2] + swap(first[2:], "y")
    second = second[::2] + swap(second[1::2], "x")
    if not aligned:
        message = both[0, sent_rows:]
        both = both[0, :sent_rows].reshape(groups, GROUP, crit_length)
        both = pad_rows(jnp.swapaxes(both, 0, 1).reshape(GROUP, -1))
        both = jnp.concatenate([both, jnp.broadcast_to(message, (GROUP, 40, 128))], axis=1)
    crit_rows = both.shape[1] - 40
    if groups == 4:
        got, first, second, both = lax.optimization_barrier((steps[1], first, second, both))
        a, b = part(1 + z) + got[0], part(z - 1) + got[1]
        a, b, first, second, both = lax.optimization_barrier((a, b, first, second, both))
        steps.append(step(2, a, b))
    first = first[0] + swap(first[1], "x")
    second = second[0] + swap(second[1], "y")
    dhidden = jnp.concatenate([first, second])
    both = lax.all_to_all(both, PLANE, 0, 0, tiled=True)
    first_grad = call(
        first_grad_kernel,
        shape((ROWS_FIRST, 128), f32),
        me,
        dhidden,
        pre,
        noise_all,
        smem=(0,),
        us=4,
        name="first_grad",
    )
    summed = jnp.sum(both[:, : crit_rows + 32], axis=0)
    message = jnp.concatenate([summed[crit_rows:], both[:, crit_rows + 32 :].reshape(64, 128)])
    both = pad_rows(summed[:crit_rows].reshape(-1)[: groups * crit_length].reshape(groups, -1))
    crit_rows = both.shape[1]
    both = jnp.concatenate([both, jnp.broadcast_to(message, (groups, 96, 128))], axis=1)
    if groups == 4:
        got_first = [lax.ppermute(first_grad, "z", [(k, 0)]) for k in (1, 2, 3)]
        first_sum = first_grad + got_first[0] + got_first[1] + got_first[2]
        reduced = part(z) + steps[2][0] + steps[2][1]
    else:
        first_sum = lax.psum(first_grad, "z")
        reduced = lax.psum_scatter(grad, "z", scatter_dimension=0, tiled=True)
    first_sum = jnp.where(z == 0, first_sum, 0.0)
    reduced = jnp.concatenate([reduced[:ROWS_FIRST] + first_sum, reduced[ROWS_FIRST:]], axis=0)
    reduced = lax.all_to_all(reduced.reshape(GROUP, rows, 128), PLANE, 0, 0, tiled=True)
    if groups == 4:
        rolled = [both[z]]
        for k in (1, 2, 3):
            piece = lax.dynamic_index_in_dim(both, lax.rem(z + k, 4), 0, keepdims=False)
            rolled.append(lax.ppermute(piece, "z", [(i, (i + k) % 4) for i in range(4)]))
        rolled = jnp.stack(rolled)
        both = jnp.stack([rolled[lax.rem(z + 4 - i, 4)] for i in range(4)])
    else:
        both = lax.all_to_all(both, "z", 0, 0, tiled=True)
    both = jnp.sum(both, axis=0)
    crit_reduced = both[:crit_rows].reshape(-1)[:crit_length]
    message = both[crit_rows : crit_rows + 32].reshape(8, 512)
    color_grad = both[crit_rows + 32 :].reshape(GROUP, 8, 128)[:, :3, :64]
    head_reduced = jnp.concatenate(
        [message[k, : KS[k]] for k in range(4)]
        + [jnp.swapaxes(color_grad, 1, 2).reshape(-1)]
    )
    losses = jnp.stack([message[4, 0], message[4, 128]])

    fix = 1.0 - jnp.power(f32(beta_first), update_ordinal[0].astype(f32))
    flat = (8 * rows, 128)
    gen = call(
        adam_kernel,
        [shape(flat, f32)] * 3,
        fix.reshape(1),
        reduced,
        maker_weight_arrays.reshape(flat),
        maker_mean_estimate.reshape(flat),
        maker_variance_estimate.reshape(flat),
        smem=(0,),
        us=6,
        name="adam",
    )
    gen = [x.reshape(-1) for x in gen]
    crit = adamw_update(
        judge_weight_arrays, judge_mean_estimate, judge_variance_estimate, crit_reduced, fix
    )
    head = adamw_update(
        output_weight_rows, output_mean_estimate, output_variance_estimate, head_reduced, fix
    )
    return (*gen, *crit, *head, losses, power_new)


def solution(mesh):
    groups = mesh.shape["dp"] * mesh.shape["scale"] // GROUP
    grid = Mesh(mesh.devices.reshape(groups, 2, 2, 2), EVERY)
    split = P(EVERY)
    return jax.shard_map(
        functools.partial(local, groups),
        mesh=grid,
        in_specs=(split,) * 7 + (P(), split, P()) + (split,) * 6 + (P(),) * 3,
        out_specs=(split,) * 6 + (P(),) * 5,
        check_vma=False,
    )
```

```python
import functools

import jax
import jax.numpy as jnp
from jax import lax
from jax.experimental import pallas as pl
from jax.experimental.pallas import tpu as pltpu
from jax.sharding import Mesh
from jax.sharding import PartitionSpec as P

S = 32
Z = 256
GIN = 1024
GOUT = 512
CS = (24, 40, 112, 320)
KS = (64, 128, 256, 512)
CP = (128, 128, 128, 384)
KP = (128, 128, 256, 512)
SLOTS = 4
PIX = 256
GROUP = 8
IMAGE_TILES = 340
ROWS_FIRST = 256
TAPS = 9

leak_slope = 0.2
learn_rate = 0.03
beta_first = 0.5
beta_second = 0.5
adam_epsilon = 1e-08
weight_decay = 0.0001
norm_epsilon = 1e-06

f32 = jnp.float32
bf16 = jnp.bfloat16
PLANE = ("y", "x", "c")
EVERY = ("z", "y", "x", "c")
VMEM_LIMIT = 60 * 1024 * 1024

NN = (((1,), (0,)), ((), ()))
NT = (((1,), (1,)), ((), ()))
TN = (((0,), (0,)), ((), ()))


def dot(a, b, dims=NN):
    return lax.dot_general(a, b, dims, preferred_element_type=f32)


def call(kernel, out_shape, *args, scratch=(), smem=(), hbm=(), out_hbm=(), us=5, name=None):
    vmem = pl.BlockSpec(memory_space=pltpu.VMEM)
    spaces = {i: pl.BlockSpec(memory_space=pltpu.SMEM) for i in smem}
    spaces.update({i: pl.BlockSpec(memory_space=pl.ANY) for i in hbm})
    single = not isinstance(out_shape, (list, tuple))
    return pl.pallas_call(
        kernel,
        out_shape=out_shape,
        in_specs=[spaces.get(i, vmem) for i in range(len(args))],
        out_specs=vmem
        if single
        else [
            pl.BlockSpec(memory_space=pl.ANY) if i in out_hbm else vmem
            for i in range(len(out_shape))
        ],
        scratch_shapes=list(scratch),
        compiler_params=pltpu.CompilerParams(vmem_limit_bytes=VMEM_LIMIT),
        cost_estimate=pl.CostEstimate(
            flops=int(us * 1e8), bytes_accessed=int(us * 3e5), transcendentals=0
        ),
        name=name,
    )(*args)


def shape(dims, dtype):
    return jax.ShapeDtypeStruct(dims, dtype)


def split_two(x):
    high = x.astype(bf16)
    return high, (x - high.astype(f32)).astype(bf16)


def split_three(x):
    high = x.astype(bf16)
    rest = x - high.astype(f32)
    middle = rest.astype(bf16)
    return high, middle, (rest - middle.astype(f32)).astype(bf16)


def pack_kernel(w_ref, o_ref):
    rows = o_ref.shape[1]
    low_half = lax.broadcasted_iota(jnp.int32, (rows, 128), 1) < 64
    for j in range(4):
        a = w_ref[pl.ds(j, rows, stride=8), :]
        b = w_ref[pl.ds(j + 4, rows, stride=8), :]
        o_ref[2 * j] = jnp.where(low_half, a, pltpu.roll(b, 64, 1)).astype(bf16)
        o_ref[2 * j + 1] = jnp.where(low_half, pltpu.roll(a, 64, 1), b).astype(bf16)


def adam_pieces(rows):
    if rows % 8:
        return [(0, rows)]
    tiles = rows // 8
    cuts = [8 * (tiles * k // 4) for k in range(5)]
    return list(zip(cuts[:-1], cuts[1:]))


def adam_kernel(
    fix_ref, g_hbm, p_hbm, m_hbm, v_hbm, po_hbm, mo_hbm, vo_hbm,
    g_ref, p_ref, m_ref, v_ref, flat, in_sems, out_sems,
):
    pieces = adam_pieces(g_ref.shape[1])
    arrived, leaving = [], []
    for k, (low, high) in enumerate(pieces):
        here, wide = pl.ds(low, high - low), pl.ds(8 * low, 8 * (high - low))
        copies = [pltpu.make_async_copy(g_hbm.at[:, here, :], g_ref.at[:, here, :], in_sems.at[4 * k])]
        for n, (a, b) in enumerate(((p_hbm, p_ref), (m_hbm, m_ref), (v_hbm, v_ref))):
            copies.append(pltpu.make_async_copy(a.at[wide, :], b.at[wide, :], in_sems.at[4 * k + n + 1]))
        for copy in copies:
            copy.start()
        arrived.append(copies)
    for k, (low, high) in enumerate(pieces):
        for copy in arrived[k]:
            copy.wait()
        count = high - low
        half = lax.broadcasted_iota(jnp.int32, (count, 128), 1) < 64
        for j in range(4):
            a, b = g_ref[2 * j, low:high, :], g_ref[2 * j + 1, low:high, :]
            flat[pl.ds(8 * low + j, count, stride=8), :] = jnp.where(half, a, pltpu.roll(b, 64, 1))
            flat[pl.ds(8 * low + j + 4, count, stride=8), :] = jnp.where(half, pltpu.roll(a, 64, 1), b)
        wide = slice(8 * low, 8 * high)
        new, first, second = adamw_update(
            p_ref[wide, :], m_ref[wide, :], v_ref[wide, :], flat[wide, :], fix_ref[0]
        )
        p_ref[wide, :] = new
        m_ref[wide, :] = first
        v_ref[wide, :] = second
        wide = pl.ds(8 * low, 8 * count)
        for n, (a, b) in enumerate(((p_ref, po_hbm), (m_ref, mo_hbm), (v_ref, vo_hbm))):
            copy = pltpu.make_async_copy(a.at[wide, :], b.at[wide, :], out_sems.at[3 * k + n])
            copy.start()
            leaving.append(copy)
    for copy in leaving:
        copy.wait()


def adamw_update(master, first, second, grad, fix):
    first_new = beta_first * first + (1.0 - beta_first) * grad
    second_new = beta_second * second + (1.0 - beta_second) * grad * grad
    update = first_new / fix / (jnp.sqrt(second_new / fix) + adam_epsilon)
    return master - learn_rate * (update + weight_decay * master), first_new, second_new


SLOT_MASK = tuple(((m >> 1) & 1) * 4 + (m & 1) * 2 + (m >> 2) for m in range(GROUP))
SLOT_FIRST = tuple(2 * (m & 1) + ((m >> 1) & 1) for m in range(4))
SLOT_SECOND = tuple(4 + m for m in range(4))
NOISE_MASK = tuple((m & 1) * 4 + ((m >> 1) & 1) * 2 + (m >> 2) for m in range(GROUP))


def pre_kernel(me_ref, noise_ref, w_ref, pre_ref, hid_ref):
    for m in range(GROUP):
        rows = pl.ds(pl.multiple_of((me_ref[0] ^ NOISE_MASK[m]) * PIX, PIX), PIX)
        pre = dot(noise_ref[m], w_ref[...], TN)
        pre_ref[rows, :] = pre
        hid_ref[rows, :] = (pre * jax.nn.sigmoid(pre)).astype(bf16)


def turn_kernel(near_ref, far_ref, o_ref):
    for m in range(GROUP):
        source = near_ref if m < 4 else far_ref
        for part, at in enumerate((SLOT_FIRST[m % 4], SLOT_SECOND[m % 4])):
            o_ref[128 * m : 128 * m + 128, 1024 * part : 1024 * part + 1024] = jnp.transpose(
                source[at]
            )


def pixel_column():
    return lax.broadcasted_iota(jnp.int32, (PIX, 128), 0) & 15


def from_left(x, column):
    return jnp.where(column > 0, pltpu.roll(x, 1, 0), 0.0)


def from_right(x, column):
    return jnp.where(column < 15, pltpu.roll(x, PIX - 1, 0), 0.0)


def from_above(x):
    return jnp.concatenate([jnp.zeros((16, x.shape[1]), x.dtype), x[:-16]], axis=0)


def from_below(x):
    return jnp.concatenate([x[16:], jnp.zeros((16, x.shape[1]), x.dtype)], axis=0)


def block_row(tap, q, half):
    return ROWS_FIRST + tap * GIN + half * GOUT + q * 64


def forward_kernel(*refs):
    me_ref, near_hbm, far_hbm, color_ref = refs[:4]
    factor_hbm, gated_hbm, rgb_ref, wide_hbm = refs[-13:-9]
    parts, w_ref, sem, near_ref, far_ref, factor_ref, gated_ref, wide, sems = refs[-9:]
    blocks = refs[4:-13]
    near_copy = pltpu.make_async_copy(near_hbm, near_ref, sems.at[0])
    far_copy = pltpu.make_async_copy(far_hbm, far_ref, sems.at[1])
    chunk = w_ref.shape[0] // 4
    if len(blocks) == 1:
        copy = pltpu.make_async_copy(blocks[0], w_ref, sem)
        copy.start()
        near_copy.start()
        far_copy.start()
        copy.wait()
    else:
        for here in range(4):

            @pl.when(me_ref[1] == here)
            def _():
                for k in range(4):
                    pltpu.make_async_copy(
                        blocks[3 + k - here].at[pl.ds(0, chunk), :],
                        w_ref.at[pl.ds(k * chunk, chunk), :],
                        sem,
                    ).start()

        near_copy.start()
        far_copy.start()
        pltpu.make_async_copy(w_ref, w_ref, sem).wait()
    for m in range(GROUP):
        q = me_ref[0] ^ SLOT_MASK[m]
        for tap in range(TAPS):
            for half in range(2):
                at = m * 128 + half * 64
                row = pl.multiple_of(block_row(tap, q, half), 64)
                wide[at : at + 64, 128 * tap : 128 * tap + 128] = w_ref[pl.ds(row, 64), :]
    wide[:, 128 * TAPS :] = jnp.zeros((GIN, 128), bf16)
    wide_copy = pltpu.make_async_copy(wide, wide_hbm, sems.at[2])
    wide_copy.start()
    near_copy.wait()
    far_copy.wait()

    def outgoing(b):
        rows = pl.ds(pl.multiple_of(b * PIX, PIX), PIX)
        return (
            pltpu.make_async_copy(
                factor_ref.at[:, rows, :], factor_hbm.at[:, rows, :], sems.at[3 + b]
            ),
            pltpu.make_async_copy(
                gated_ref.at[:, rows, :], gated_hbm.at[:, rows, :], sems.at[3 + GROUP + b]
            ),
        )

    low_half = lax.broadcasted_iota(jnp.int32, (PIX, 128), 1) < 64
    column = pixel_column()
    color_high, color_low = split_two(color_ref[...])
    color = jnp.concatenate([color_high, color_low], axis=0)

    @pl.loop(0, 4)
    def _(pair):
        start = pl.multiple_of(pair * 512, 512)
        local = pl.multiple_of((pair & 1) * 512, 512)
        first = pair < 2
        left = []
        for m in range(GROUP):
            at = jnp.where(first, SLOT_FIRST[m % 4], SLOT_SECOND[m % 4])
            left.append((near_ref if m < 4 else far_ref)[at, pl.ds(local, 512), :])
        left = jnp.concatenate(left, axis=1)
        for k in range(5):
            y = dot(left, wide[:, 256 * k : 256 * k + 256])
            parts[2 * k] = y[:, :128]
            if k < 4:
                parts[2 * k + 1] = y[:, 128:]
        for one in range(2):
            rows = pl.ds(pl.multiple_of(start + one * PIX, PIX), PIX)
            here = slice(one * PIX, one * PIX + PIX)
            cols = []
            for a in range(3):
                y0, y1, y2 = (parts[3 * a + b, here, :] for b in range(3))
                cols.append((from_left(y0, column) + (y1 + y2), (y0 + y1) + from_right(y2, column)))
            for pi in range(2):
                gated = []
                for pj in range(2):
                    if pi == 0:
                        mixed = from_above(cols[0][pj]) + (cols[1][pj] + cols[2][pj])
                    else:
                        mixed = (cols[0][pj] + cols[1][pj]) + from_below(cols[2][pj])
                    turned = pltpu.roll(mixed, 64, 1)
                    gate = jax.nn.sigmoid(jnp.where(low_half, turned, mixed))
                    value = jnp.where(low_half, mixed, turned)
                    gated.append(value * gate)
                    factor_ref[2 * pi + pj, rows, :] = jnp.where(
                        low_half, gate, gated[-1] * (1.0 - gate)
                    )
                both = jnp.where(low_half, gated[0], gated[1])
                gated_ref[pi, rows, :] = both
                high, low = split_two(both)
                rgb = dot(color, jnp.concatenate([high, low], axis=1), NT)
                rgb_ref[2 * pair + one, 16 * pi : 16 * pi + 16, :] = rgb[:16] + rgb[16:]
            for copy in outgoing(2 * pair + one):
                copy.start()

    @pl.loop(0, GROUP)
    def _(b):
        for copy in outgoing(b):
            copy.wait()

    wide_copy.wait()


def tap_sums(parts, column):
    sums = []
    for a in range(3):
        line = []
        for pj in range(2):
            even, odd = parts[pj], parts[2 + pj]
            if a == 0:
                line.append(odd + from_below(even))
            elif a == 1:
                line.append(even + odd)
            else:
                line.append(from_above(odd) + even)
        sums.append(line[1] + from_right(line[0], column))
        sums.append(line[0] + line[1])
        sums.append(from_left(line[1], column) + line[0])
    return sums


def weight_grad_kernel(
    me_ref, dt_ref, factor_hbm, hid_hbm, color_ref, g_hbm, dm_hbm,
    moved, factor_ref, hid_ref, g_ref, dm_ref, in_sems, dm_sems, out_sems,
):
    column = pixel_column()

    def piece(b):
        return pl.ds(pl.multiple_of(b * PIX, PIX), PIX)

    def factor_copy(b):
        return pltpu.make_async_copy(
            factor_hbm.at[:, piece(b), :], factor_ref.at[:, piece(b), :], in_sems.at[b]
        )

    def dm_copy(b):
        return pltpu.make_async_copy(
            dm_ref.at[:, piece(b), :], dm_hbm.at[:, piece(b), :], dm_sems.at[b]
        )

    def taps_copy(a):
        start = 0 if a == 0 else ROWS_FIRST + 3 * a * GIN
        at = pl.ds(start, ROWS_FIRST + 3 * (a + 1) * GIN - start)
        return pltpu.make_async_copy(g_ref.at[at, :], g_hbm.at[at, :], out_sems.at[a])

    for b in range(GROUP):
        factor_copy(b).start()
    hid_copy = pltpu.make_async_copy(hid_hbm, hid_ref, in_sems.at[GROUP])
    hid_copy.start()
    g_ref[:ROWS_FIRST, :] = jnp.zeros((ROWS_FIRST, 128), f32)
    c_high, c_middle, c_low = (x.astype(f32) for x in split_three(color_ref[...]))
    colors = jnp.concatenate([c_high, c_middle, c_low, c_high, c_middle, c_high], axis=0)
    colors = colors.astype(bf16)

    @pl.loop(0, GROUP)
    def _(b):
        rows = piece(b)
        factor_copy(b).wait()
        for phase in range(4):
            pi, pj = phase // 2, phase % 2
            high, middle, low = (
                x.astype(f32) for x in split_three(dt_ref[b, 8 * phase : 8 * phase + 8, :])
            )
            left = jnp.concatenate([high, high, high, middle, middle, low], axis=0).astype(bf16)
            spread = dot(left, colors, TN)
            low = (spread * factor_ref[phase, rows, :]).astype(bf16)
            dm_ref[phase, rows, :] = low
            plain = low.astype(f32)
            side = (from_right if pj == 0 else from_left)(plain, column)
            lanes = slice(128 * pj, 128 * pj + 128)
            for k, value in enumerate((plain, side)):
                line = (from_below if pi == 0 else from_above)(value)
                moved[4 * pi + k, rows, lanes] = value.astype(bf16)
                moved[4 * pi + 2 + k, rows, lanes] = line.astype(bf16)
        dm_copy(b).start()

    hid_copy.wait()

    def column_sums(at):
        plain = dot(hid_ref[...], moved[at])
        side = dot(hid_ref[...], moved[at + 1])
        return (
            plain[:, 128:] + side[:, :128],
            plain[:, :128] + plain[:, 128:],
            side[:, 128:] + plain[:, :128],
        )

    def put(tap, value, add):
        for m in range(GROUP):
            for half in range(2):
                q = me_ref[0] ^ SLOT_MASK[m]
                at = pl.ds(pl.multiple_of(block_row(tap, q, half), 64), 64)
                piece = value[128 * m + 64 * half : 128 * m + 64 * half + 64]
                g_ref[at, :] = g_ref[at, :] + piece if add else piece

    for at, takes in ((0, ((1, False), (2, False))), (4, ((0, False), (1, True)))):
        for b, value in enumerate(column_sums(at)):
            for a, add in takes:
                put(3 * a + b, value, add)
    taps_copy(1).start()
    for at, a in ((2, 0), (6, 2)):
        for b, value in enumerate(column_sums(at)):
            put(3 * a + b, value, True)
        taps_copy(a).start()
    for a in range(3):
        taps_copy(a).wait()

    @pl.loop(0, GROUP)
    def _(b):
        dm_copy(b).wait()


def hidden_grad_kernel(
    dm_ref, wide_ref, dt_ref, gated_ref, keep_ref, send_ref, rgb_ref, sums, color
):
    column = pixel_column()
    color[...] = jnp.zeros_like(color)

    @pl.loop(0, GROUP)
    def _(b):
        rows = pl.ds(pl.multiple_of(b * PIX, PIX), PIX)
        parts = [dm_ref[phase, rows, :].astype(f32) for phase in range(4)]
        for tap, total in enumerate(tap_sums(parts, column)):
            high, low = split_two(total)
            sums[:PIX, 128 * tap : 128 * tap + 128] = high
            sums[PIX:, 128 * tap : 128 * tap + 128] = low
        for k in range(4):
            out = dot(sums[...], wide_ref[256 * k : 256 * k + 256, : 128 * TAPS], NT)
            out = out[:PIX] + out[PIX:]
            put = keep_ref if k < 2 else send_ref
            put[2 * (k % 2), rows, :] = out[:, :128]
            put[2 * (k % 2) + 1, rows, :] = out[:, 128:]
        for pi in range(2):
            high, low = split_two(dt_ref[b, 16 * pi : 16 * pi + 16, :])
            g_high, g_low = split_two(gated_ref[pi, rows, :])
            left = jnp.concatenate([high, low], axis=0)
            out = dot(left, jnp.concatenate([g_high, g_low], axis=1))
            color[...] += out[:16, :128] + (out[:16, 128:] + out[16:, :128])

    low_half = lax.broadcasted_iota(jnp.int32, (8, 128), 1) < 64
    folded = color[:8, :] + pltpu.roll(color[8:, :], 64, 1)
    rgb_ref[...] = jnp.where(low_half, folded, 0.0)


def first_grad_kernel(me_ref, dh_ref, pre_ref, noise_ref, o_ref):
    o_ref[...] = jnp.zeros_like(o_ref)
    for m in range(GROUP):
        rows = pl.ds(pl.multiple_of((me_ref[0] ^ NOISE_MASK[m]) * PIX, PIX), PIX)
        pre = pre_ref[rows, :]
        gate = jax.nn.sigmoid(pre)
        slope = gate * (1.0 + pre * (1.0 - gate))
        o_ref[...] += dot(noise_ref[m], (slope * dh_ref[rows, :]).astype(bf16))


def row_normalized(row):
    return row * lax.rsqrt(jnp.sum(row * row, axis=1, keepdims=True) + norm_epsilon)


def row_times(row, matrix, dims):
    pieces = jnp.concatenate(
        [jnp.broadcast_to(x.astype(f32), (8, row.shape[1])) for x in split_three(row)], axis=0
    ).astype(bf16)
    out = dot(pieces, matrix, dims)
    return out[0:1] + out[8:9] + out[16:17]


INS = (3,) + CS[:3]
CRIT_AT = (0, 4096, 20480, 86016)


def window(length):
    rows = length // 128 if length % 128 == 0 else -(-(127 + length) // 128)
    return -(-rows // 16) * 16


def prepare_kernel(
    crit_length, frozen_length, small_ref, own_ref, u_ref,
    e1, e2, e3, e4, r1, r2, r3, r4, m1, m2, m3, m4, c1, c2, c3, c4,
    left_ref, sigma_ref, share_ref, crit, frozen, moved, rows_buf,
):
    devices = small_ref.shape[0]
    crit_rows, frozen_rows = window(crit_length), window(frozen_length)
    crit[...] = jnp.zeros_like(crit)
    frozen[...] = jnp.zeros_like(frozen)
    for k in range(devices):
        at = pl.ds((k * crit_length) // 128, crit_rows)
        crit[at, :] += small_ref[k, :crit_rows, :].astype(f32)
        at = pl.ds((k * frozen_length) // 128, frozen_rows)
        frozen[at, :] += small_ref[k, crit_rows : crit_rows + frozen_rows, :].astype(f32)
    live = jnp.zeros((1, 128), f32)
    for k in range(devices):
        at = crit_rows + frozen_rows
        live += small_ref[k, at : at + 16, :].astype(f32)[0:1]
    lane = lax.broadcasted_iota(jnp.int32, (1, 128), 1)
    real = jnp.sum(jnp.where((lane > 0) & (lane < SLOTS), live, 0.0), axis=1, keepdims=True)
    count = jnp.where(lane == 0, live, real) * float(IMAGE_TILES)
    share_ref[...] = jnp.broadcast_to(own_ref[...] / jnp.maximum(count, 1.0), share_ref.shape)

    def lanes_of(x):
        return lax.broadcasted_iota(jnp.int32, x.shape, 1)

    def shifted(a, b, lane_at):
        if lane_at == 0:
            return a
        turn = 128 - lane_at
        return jnp.where(lanes_of(a) < turn, pltpu.roll(a, turn, 1), pltpu.roll(b, turn, 1))

    def halves(x):
        low = lanes_of(x) < 64
        return jnp.where(low, x, 0.0), jnp.where(low, pltpu.roll(x, 64, 1), 0.0)

    def flush(ref, rows):
        ref[...] = rows_buf[: ref.shape[0], :].astype(bf16)
        rows_buf[:rows, :] = jnp.zeros((rows, 128), f32)

    total = frozen.shape[0] - 8
    moved[...] = shifted(frozen[:total, :], frozen[1 : total + 1, :], 8)
    rows_buf[...] = jnp.zeros_like(rows_buf)
    for ref, offset, rows, width in ((e1, 0, INS[0], CS[0]), (e2, 72, INS[1], CS[1])):
        for r in range(rows):
            a, lane_at = divmod(offset + r * width, 128)
            row = shifted(frozen[a : a + 1, :], frozen[a + 1 : a + 2, :], lane_at)
            rows_buf[r : r + 1, :] = jnp.where(lane < width, row, 0.0)
        flush(ref, 32)
    for i in range(8):
        a, lane_at = divmod(112 * i, 128)
        row = shifted(
            moved[pl.ds(8 + a, 5, stride=7), :], moved[pl.ds(9 + a, 5, stride=7), :], lane_at
        )
        rows_buf[pl.ds(i, 5, stride=8), :] = jnp.where(lanes_of(row) < 112, row, 0.0)
    flush(e3, 40)
    five = [moved[pl.ds(43 + k, 56, stride=5), :] for k in range(5)]
    pairs = (
        (five[0], shifted(five[2], five[3], 64)),
        (five[1], shifted(five[3], five[4], 64)),
        (halves(five[2])[0], halves(five[4])[1]),
    )
    e4[...] = jnp.zeros_like(e4)
    for b, (even, odd) in enumerate(pairs):
        rows_buf[pl.ds(0, 56, stride=2), :] = even
        rows_buf[pl.ds(1, 56, stride=2), :] = odd
        e4[:112, 128 * b : 128 * b + 128] = rows_buf[:112, :].astype(bf16)
    rows_buf[...] = jnp.zeros_like(rows_buf)
    even, odd = halves(moved[323:335, :])
    rows_buf[pl.ds(0, 12, stride=2), :] = even
    rows_buf[pl.ds(1, 12, stride=2), :] = odd
    flush(r1, 24)
    rows_buf[:40, :] = moved[335:375, :]
    flush(r2, 40)
    r3[...] = jnp.zeros_like(r3)
    r4[...] = jnp.zeros_like(r4)
    for b in range(2):
        r3[:112, 128 * b : 128 * b + 128] = moved[pl.ds(375 + b, 112, stride=2), :].astype(bf16)
    for b in range(4):
        r4[:320, 128 * b : 128 * b + 128] = moved[pl.ds(599 + b, 320, stride=4), :].astype(bf16)
    even, odd = halves(crit[:32, :])
    rows_buf[pl.ds(0, 32, stride=2), :] = even
    rows_buf[pl.ds(1, 32, stride=2), :] = odd
    flush(m1, 64)
    m2[...] = crit[32:160, :].astype(bf16)
    for b in range(2):
        m3[:, 128 * b : 128 * b + 128] = crit[pl.ds(160 + b, 256, stride=2), :].astype(bf16)
    for b in range(4):
        m4[:, 128 * b : 128 * b + 128] = crit[pl.ds(672 + b, 512, stride=4), :].astype(bf16)

    left_ref[...] = jnp.zeros_like(left_ref)
    sigma_ref[...] = jnp.ones_like(sigma_ref)
    for k, (m_ref, c_ref) in enumerate(((m1, c1), (m2, c2), (m3, c3), (m4, c4))):
        width = KP[k]
        matrix = m_ref[...]
        right = row_normalized(row_times(u_ref[k : k + 1, :width], matrix, NT))
        turned = row_times(right, matrix, NN)
        left = row_normalized(turned)
        left_ref[k : k + 1, :width] = left
        sigma = jnp.sum(left * turned, axis=1, keepdims=True)
        sigma_ref[k : k + 1, :] = jnp.broadcast_to(sigma, (1, 128))
        c_ref[...] = jnp.transpose(jnp.broadcast_to(right, (128, width)))


def wanted_code(scal_ref, slot):
    d = lax.broadcasted_iota(jnp.int32, (1, 1024), 1)

    def bit(k):
        return (d >> k) & 1

    i = bit(9) + 2 * bit(7) + 4 * bit(5) + 8 * bit(3) + 16 * bit(1)
    j = bit(8) + 2 * bit(6) + 4 * bit(4) + 8 * bit(2) + 16 * bit(0)
    down, across, flip, top, side = (scal_ref[slot, k] for k in range(5))
    row = i - down
    moved = j - across
    fine = (row >= 0) & (row < S) & (moved >= 0) & (moved < S)
    source = jnp.where(flip == 1, S - 1 - moved, moved)
    boxed = (i >= top) & (i < top + S // 2) & (j >= side) & (j < side + S // 2)
    return jnp.where(fine & jnp.logical_not(boxed), row * S + source, -1)


def three(x):
    return jnp.concatenate([v.astype(f32) for v in split_three(x)], axis=0).astype(bf16)


def fold(x):
    return x[0:8] + x[8:16] + x[16:24]


def fill_pick(pick, scal_ref, slot, phases):
    want = wanted_code(scal_ref, slot)

    @pl.loop(0, 8)
    def _(k):
        s = lax.broadcasted_iota(jnp.int32, (128, 1024), 0) + k * 128
        if phases:
            at = s & 255
            s = (2 * (at >> 4) + (s >> 9)) * S + 2 * (at & 15) + ((s >> 8) & 1)
        hit = jnp.where(s == want, 1.0, 0.0).astype(bf16)
        pick[pl.ds(pl.multiple_of(k * 128, 128), 128), :] = hit


def augmented(image, pick):
    seen = fold(dot(three(image), pick[...]))
    small = 0.25 * ((seen[:, :256] + seen[:, 256:512]) + (seen[:, 512:768] + seen[:, 768:]))
    return jnp.transpose(small).astype(bf16)


def last_pool(slots):
    row = lax.broadcasted_iota(jnp.int32, (16, 16 * slots), 0)
    col = lax.broadcasted_iota(jnp.int32, (16, 16 * slots), 1)
    pool = jnp.where((row // 4 == col // 16) & (row % 4 == col % 4), 0.25, 0.0)
    return jnp.concatenate([pool.astype(bf16)] * 3, axis=1)


def critic_levels(inputs, slots, extract, project, matrices, head_ref, sigma_ref):
    levels = []
    pool = last_pool(slots)
    for k in range(4):
        count = 16 if k == 3 else (slots * PIX) >> (2 * k)
        width = KP[k]
        pre = dot(inputs, extract[k][...])
        active = pre * jax.nn.sigmoid(pre)
        feat = dot(active.astype(bf16), project[k][...]).astype(bf16)
        raw = dot(feat, matrices[k][...])
        sigma = sigma_ref[k : k + 1, 0:1]
        scaled = raw / sigma
        slope = jnp.where(scaled >= 0, 1.0, leak_slope)
        leaky = scaled * slope
        head = head_ref[k : k + 1, :width]
        scale = lax.rsqrt(jnp.sum(head * head, axis=1, keepdims=True) + norm_epsilon)
        unit = head * scale
        logit = jnp.sum(leaky * unit, axis=1, keepdims=True)
        levels.append((pre, feat, raw, sigma, slope, leaky, head, scale, unit, logit))
        if k < 2:
            blocks = active.reshape(slots, 4, count // (4 * slots), CP[k])
            total = (blocks[:, 0] + blocks[:, 1]) + (blocks[:, 2] + blocks[:, 3])
            inputs = (0.25 * total).reshape(count // 4, CP[k]).astype(bf16)
        elif k == 2:
            inputs = dot(pool, three(active)).astype(bf16)
    return levels


def image_grad_kernel(
    scal_ref,
    share_ref,
    got_ref,
    head_ref,
    sigma_ref,
    e1, e2, e3, e4,
    r1, r2, r3, r4,
    m1, m2, m3, m4,
    dt_ref,
    map_ref,
    pick,
):
    extract, project, matrices = (e1, e2, e3, e4), (r1, r2, r3, r4), (m1, m2, m3, m4)
    fill_pick(pick, scal_ref, 0, True)
    color = got_ref[0]
    for k in range(1, GROUP):
        color = color + got_ref[k]
    color = jnp.tanh(color)
    fake = jnp.concatenate([color[8 * k : 8 * k + 8] for k in range(4)], axis=1)
    first_map = augmented(fake, pick)
    map_ref[...] = first_map
    levels = critic_levels(first_map, 1, extract, project, matrices, head_ref, sigma_ref)
    row = lax.broadcasted_iota(jnp.int32, (16, 16), 0)
    col = lax.broadcasted_iota(jnp.int32, (16, 16), 1)
    spread = jnp.where((col < 4) & (row % 4 == col), 0.25, 0.0)
    spread = jnp.concatenate([spread.astype(bf16)] * 3, axis=1)
    carry = None
    for k in (3, 2, 1, 0):
        pre, feat, raw, sigma, slope, leaky, head, scale, unit, logit = levels[k]
        dlogit = -share_ref[0:1, 0:1] * jax.nn.sigmoid(-logit)
        if k == 3:
            dlogit = jnp.where(lax.broadcasted_iota(jnp.int32, (16, 1), 0) < 4, dlogit, 0.0)
        dscaled = dlogit * unit * slope
        dfeat = dot((dscaled / sigma).astype(bf16), matrices[k][...], NT).astype(bf16)
        dactive = dot(dfeat, project[k][...], NT)
        if carry is not None:
            dactive = dactive + carry
        gate = jax.nn.sigmoid(pre)
        dpre = (gate * (1.0 + pre * (1.0 - gate)) * dactive).astype(bf16)
        dinput = dot(dpre, extract[k][...], NT)
        if k == 3:
            carry = dot(spread, three(dinput))
        elif k > 0:
            carry = jnp.concatenate([0.25 * dinput] * 4, axis=0)
    daug = 0.25 * jnp.transpose(dinput)
    daug = jnp.concatenate([daug] * 4, axis=1)
    dimage = fold(dot(three(daug), pick[...], NT))
    dtanh = dimage * (1.0 - fake * fake)
    for k in range(4):
        dt_ref[8 * k : 8 * k + 8, :] = dtanh[:, 256 * k : 256 * k + 256]


def critic_kernel(
    scal_ref,
    share_ref,
    map_ref,
    real_ref,
    head_ref,
    left_ref,
    sigma_ref,
    e1, e2, e3, e4,
    r1, r2, r3, r4,
    m1, m2, m3, m4,
    c1, c2, c3, c4,
    color_ref,
    sent_ref,
    pick,
    first_map,
    corner,
    out_ref,
    flat_ref,
):
    extract, project = (e1, e2, e3, e4), (r1, r2, r3, r4)
    matrices, columns = (m1, m2, m3, m4), (c1, c2, c3, c4)
    first_map[:PIX, :] = map_ref[...]
    for slot in range(1, SLOTS):
        fill_pick(pick, scal_ref, slot, False)
        first_map[slot * PIX : slot * PIX + PIX, :] = augmented(real_ref[slot - 1], pick)
    levels = critic_levels(first_map[...], SLOTS, extract, project, matrices, head_ref, sigma_ref)
    loss_gen = jnp.zeros((1, 1), f32)
    loss_critic = jnp.zeros((1, 1), f32)
    out_ref[...] = jnp.zeros_like(out_ref)
    for k in range(4):
        pre, feat, raw, sigma, slope, leaky, head, scale, unit, logit = levels[k]
        count, width = logit.shape[0], KP[k]
        slot = lax.broadcasted_iota(jnp.int32, (count, 1), 0) // (count // SLOTS)
        share = share_ref[0:1, 0:1]
        for other in range(1, SLOTS):
            share = jnp.where(slot == other, share_ref[0:1, other : other + 1], share)
        sign = jnp.where(slot == 0, -1.0, 1.0)
        hinge = 1.0 - sign * logit
        loss_critic += jnp.sum(share * jnp.maximum(hinge, 0.0), axis=0, keepdims=True)
        dlogit = jnp.where(hinge > 0, -sign * share, 0.0)
        soft = jnp.maximum(-logit, 0.0) + jnp.log1p(jnp.exp(-jnp.abs(logit)))
        loss_gen += jnp.sum(jnp.where(slot == 0, share * soft, 0.0), axis=0, keepdims=True)
        dscaled = dlogit * unit * slope
        grad = dot(feat, (dscaled / sigma).astype(bf16), TN)
        dsigma = jnp.sum(jnp.sum(dscaled * raw, axis=1, keepdims=True), axis=0, keepdims=True)
        dsigma = -dsigma / (sigma * sigma)
        side = columns[k][...] * dsigma
        for b in range(width // 128):
            lanes = slice(128 * b, 128 * b + 128)
            piece = grad[:, lanes] + side * left_ref[k : k + 1, lanes]
            if k == 0:
                corner[...] = piece
                low = lax.broadcasted_iota(jnp.int32, (32, 128), 1) < 64
                even, odd = corner[pl.ds(0, 32, stride=2), :], corner[pl.ds(1, 32, stride=2), :]
                flat_ref[:32, :] = jnp.where(low, even, pltpu.roll(odd, 64, 1))
            else:
                stride = width // 128
                flat_ref[pl.ds(CRIT_AT[k] // 128 + b, width, stride=stride), :] = piece
        dunit = jnp.sum(leaky * dlogit, axis=0, keepdims=True)
        inner = jnp.sum(head * dunit, axis=1, keepdims=True)
        out_ref[k : k + 1, :width] = scale * dunit - head * (scale * scale * scale * inner)
    out_ref[4:5, 0:128] = jnp.broadcast_to(loss_gen, (1, 128))
    out_ref[4:5, 128:256] = jnp.broadcast_to(loss_critic, (1, 128))
    rows = sent_ref.shape[1] - 40
    if sent_ref.shape[0] == GROUP:
        groups = rows // 85
        for q in range(GROUP):
            for z in range(groups):
                at = (z * GROUP + q) * 85
                sent_ref[q, z * 85 : z * 85 + 85, :] = flat_ref[at : at + 85, :]
            sent_ref[q, groups * 85 : rows, :] = jnp.zeros((rows - groups * 85, 128), f32)
    else:
        sent_ref[0, :rows, :] = flat_ref[...]
    for q in range(sent_ref.shape[0]):
        for k in range(8):
            for b in range(4):
                at = rows + 4 * k + b
                sent_ref[q, at : at + 1, :] = out_ref[k : k + 1, 128 * b : 128 * b + 128]
        sent_ref[q, rows + 32 :, :] = color_ref[...]


def local(
    groups,
    noise_maps,
    dataset_lowres_images,
    dataset_highres_images,
    occupied_mask,
    shift_amounts,
    mirror_indicator,
    erase_box_corner,
    update_ordinal,
    fixed_backbone_params,
    singular_estimate_dirs,
    maker_weight_arrays,
    maker_mean_estimate,
    maker_variance_estimate,
    judge_weight_arrays,
    judge_mean_estimate,
    judge_variance_estimate,
    output_weight_rows,
    output_mean_estimate,
    output_variance_estimate,
):
    devices = groups * GROUP
    rows = maker_weight_arrays.shape[0] // 1024
    chunk = GROUP * rows
    z = lax.axis_index("z")
    q = (lax.axis_index("y") * 2 + lax.axis_index("x")) * 2 + lax.axis_index("c")
    me = jnp.stack([q, z]).astype(jnp.int32)

    def pad_rows(x):
        return jnp.pad(x, ((0, 0), (0, -x.shape[1] % 1024))).reshape(x.shape[0], -1, 128)

    def swap(x, axis):
        return lax.ppermute(x, axis, [(0, 1), (1, 0)])

    crit_length = judge_weight_arrays.shape[0]
    frozen_length = fixed_backbone_params.shape[0]
    member = z * GROUP + q

    def windowed(x):
        length = x.shape[0]
        rows_here = window(length)
        if length % 128 == 0:
            return jnp.pad(x.reshape(-1, 128), ((0, rows_here - length // 128), (0, 0)))
        empty = jnp.zeros((rows_here * 128,), bf16)
        start = lax.rem(member * length, 128)
        return lax.dynamic_update_slice(empty, x, (start,)).reshape(rows_here, 128)

    own = occupied_mask.astype(f32)
    small = jnp.concatenate(
        [
            windowed(judge_weight_arrays.astype(bf16)),
            windowed(fixed_backbone_params),
            jnp.pad(own.astype(bf16), ((0, 15), (0, 128 - SLOTS))),
        ]
    )

    def rows_of(flat):
        out, offset = [], 0
        for k in range(4):
            out.append(jnp.pad(flat[offset : offset + KS[k]], (0, 512 - KS[k])))
            offset += KS[k]
        return jnp.pad(jnp.stack(out), ((0, 4), (0, 0)))

    head_rows = rows_of(output_weight_rows)
    start_rows = rows_of(singular_estimate_dirs)
    own_row = jnp.pad(own, ((0, 0), (0, 128 - SLOTS)))
    color_all = output_weight_rows[960:].reshape(GOUT, 3)
    color = jnp.pad(lax.dynamic_slice(color_all, (q * 64, 0), (64, 3)).T, ((0, 5), (0, 0)))
    none = jnp.zeros_like(color)
    color_left = jnp.concatenate(
        [
            jnp.concatenate([color, none, color, none], axis=1),
            jnp.concatenate([none, color, none, color], axis=1),
        ],
        axis=0,
    )
    color_twice = jnp.concatenate([color, color], axis=1)
    small_images = dataset_lowres_images.astype(f32)
    large = dataset_highres_images.astype(f32).reshape(1, 3, S, 2, S, 2)
    large = jnp.mean(large, axis=(3, 5)).reshape(1, 3, S * S)
    reals = jnp.pad(jnp.concatenate([small_images, large]), ((0, 0), (0, 5), (0, 0)))
    scalars = jnp.concatenate(
        [shift_amounts[0], mirror_indicator[0][:, None], erase_box_corner[0]], axis=1
    )

    noise_all = jnp.concatenate([noise_maps, swap(noise_maps, "y")])

    packed = call(
        pack_kernel,
        shape((GROUP, rows, 128), bf16),
        maker_weight_arrays.reshape(8 * rows, 128),
        us=3,
        name="pack",
    )
    slices = lax.all_to_all(packed, PLANE, 0, 0, tiled=True).reshape(chunk, 128)
    slices, noise_all = lax.optimization_barrier((slices, noise_all))
    for axis in ("x", "c"):
        noise_all = jnp.concatenate([noise_all, swap(noise_all, axis)])
    first_block = slices[:ROWS_FIRST]

    def hop(x, y):
        down = lax.ppermute(x, "z", [(0, 1), (1, 2), (2, 3)])
        return down, lax.ppermute(y, "z", [(1, 0), (2, 1), (3, 2)])

    if groups == 4:
        sent = [lax.ppermute(first_block, "z", [(0, k)]) for k in (1, 2, 3)]
        riding = jnp.concatenate([slices, small])
        hop_one = hop(riding, riding)
        ready = (head_rows, start_rows, own_row, color_left, color_twice, reals, scalars, me)
        sent, hop_one, ready = lax.optimization_barrier((sent, hop_one, ready))
        head_rows, start_rows, own_row, color_left, color_twice, reals, scalars, me = ready
        first_weights = jnp.where(z == 0, first_block, sent[0] + sent[1] + sent[2])
        hop_two = hop(*hop_one)
    else:
        first_weights = lax.all_gather(first_block, "z", axis=0)[0]
        blocks = [lax.all_gather(slices, "z", axis=0, tiled=True)]

    pixels = GROUP * PIX
    pre, hid = call(
        pre_kernel,
        [shape((pixels, 128), f32), shape((pixels, 128), bf16)],
        me,
        noise_all,
        first_weights,
        smem=(0,),
        us=4,
        name="pre",
    )
    first, second = hid[: pixels // 2], hid[pixels // 2 :]
    first = jnp.stack([first, swap(first, "y")])
    second = jnp.stack([second, swap(second, "x")])
    if groups == 4:
        first, second, hop_two = lax.optimization_barrier((first, second, hop_two))
        hop_three = hop(*hop_two)
    first = jnp.concatenate([first, swap(first, "x")])
    second = jnp.concatenate([second, swap(second, "y")])
    if groups == 4:
        first, second, hop_three = lax.optimization_barrier((first, second, hop_three))
        blocks = [hop_three[0], hop_two[0], hop_one[0], riding, hop_one[1], hop_two[1], hop_three[1]]
        small = lax.dynamic_slice_in_dim(jnp.stack([x[chunk:] for x in blocks]), 3 - z, 4, axis=0)
    else:
        small = lax.all_gather(small, "z", axis=0)
    near = jnp.concatenate([first, second])
    far = swap(near, "c")
    near, far, small = lax.optimization_barrier((near, far, small))
    small = lax.all_to_all(jnp.broadcast_to(small, (GROUP,) + small.shape), PLANE, 0, 0, tiled=True)
    factor, gated, rgb, wide = call(
        forward_kernel,
        [
            shape((4, pixels, 128), f32),
            shape((2, pixels, 128), f32),
            shape((GROUP, 32, PIX), f32),
            shape((GIN, 1280), bf16),
        ],
        me,
        near,
        far,
        color_left,
        *blocks,
        smem=(0,),
        hbm=(1, 2, *range(4, 4 + len(blocks))),
        out_hbm=(0, 1, 3),
        scratch=[
            pltpu.VMEM((TAPS + 1, 512, 128), f32),
            pltpu.VMEM((groups * chunk, 128), bf16),
            pltpu.SemaphoreType.DMA,
            pltpu.VMEM((GROUP, pixels // 2, 128), bf16),
            pltpu.VMEM((GROUP, pixels // 2, 128), bf16),
            pltpu.VMEM((4, pixels, 128), f32),
            pltpu.VMEM((2, pixels, 128), f32),
            pltpu.VMEM((GIN, 1280), bf16),
            pltpu.SemaphoreType.DMA((3 + 2 * GROUP,)),
        ],
        us=14,
        name="forward",
    )
    got = lax.all_to_all(rgb, PLANE, 0, 0, tiled=True)
    near, far, factor, small = lax.optimization_barrier((near, far, factor, small))
    small = jnp.swapaxes(small, 0, 1).reshape((devices,) + small.shape[2:])
    squares = [shape((8, CP[0]), bf16)] + [shape((CP[k - 1], CP[k]), bf16) for k in (1, 2, 3)]
    squares += [shape((CP[k], KP[k]), bf16) for k in range(4)]
    squares += [shape((KP[k], KP[k]), bf16) for k in range(4)]
    squares += [shape((KP[k], 128), f32) for k in range(4)]
    squares += [shape((8, 512), f32), shape((8, 128), f32), shape((8, 128), f32)]
    crit_space = -(-((devices - 1) * crit_length // 128 + window(crit_length)) // 8) * 8
    frozen_space = -(-((devices - 1) * frozen_length // 128 + window(frozen_length)) // 8) * 8 + 8
    prepared = call(
        functools.partial(prepare_kernel, crit_length, frozen_length),
        squares,
        small,
        own_row,
        start_rows,
        scratch=[
            pltpu.VMEM((crit_space, 128), f32),
            pltpu.VMEM((frozen_space, 128), f32),
            pltpu.VMEM((frozen_space - 8, 128), f32),
            pltpu.VMEM((128, 128), f32),
        ],
        us=8,
        name="prepare",
    )
    frozen, matrices, right_cols = prepared[:8], prepared[8:12], prepared[12:16]
    left_rows, sigma_rows, share = prepared[16:]
    power_new = jnp.concatenate([left_rows[k, : KS[k]] for k in range(4)])
    dtanh, first_map = call(
        image_grad_kernel,
        [shape((32, PIX), f32), shape((PIX, 8), bf16)],
        scalars,
        share,
        got,
        head_rows,
        sigma_rows,
        *frozen,
        *matrices,
        smem=(0,),
        scratch=[pltpu.VMEM((1024, 1024), bf16)],
        us=8,
        name="image_grad",
    )

    near, far, dtanh = lax.optimization_barrier((near, far, dtanh))
    hid_turned = call(turn_kernel, shape((GIN, pixels), bf16), near, far, us=5, name="turn")
    dtanh_all = lax.all_to_all(
        jnp.broadcast_to(dtanh, (GROUP,) + dtanh.shape), PLANE, 0, 0, tiled=True
    )
    grad, dmixed = call(
        weight_grad_kernel,
        [shape((ROWS_FIRST + TAPS * GIN, 128), f32), shape((4, pixels, 128), bf16)],
        me,
        dtanh_all,
        factor,
        hid_turned,
        color_twice,
        smem=(0,),
        hbm=(2, 3),
        out_hbm=(0, 1),
        scratch=[
            pltpu.VMEM((8, pixels, 256), bf16),
            pltpu.VMEM((4, pixels, 128), f32),
            pltpu.VMEM((GIN, pixels), bf16),
            pltpu.VMEM((ROWS_FIRST + TAPS * GIN, 128), f32),
            pltpu.VMEM((4, pixels, 128), bf16),
            pltpu.SemaphoreType.DMA((GROUP + 1,)),
            pltpu.SemaphoreType.DMA((GROUP,)),
            pltpu.SemaphoreType.DMA((3,)),
        ],
        us=20,
        name="weight_grad",
    )
    steps = []
    if groups == 4:

        def part(k):
            return lax.dynamic_slice_in_dim(grad, jnp.clip(k, 0, 3) * chunk, chunk, axis=0)

        def step(s, a, b):
            if s == 1:
                a, b = part(2 + z) + a, part(z - 2) + b
            down = lax.ppermute(a, "z", [(k, k + 1) for k in range(s + 1)])
            up = lax.ppermute(b, "z", [(3 - k, 2 - k) for k in range(s + 1)])
            return lax.optimization_barrier((down, up))

        first_a, first_b, first_map, dmixed = lax.optimization_barrier(
            (part(3 + z), part(z - 3), first_map, dmixed)
        )
        steps.append(step(0, first_a, first_b))
    keep, send, color_grad = call(
        hidden_grad_kernel,
        [shape((4, pixels, 128), f32), shape((4, pixels, 128), f32), shape((8, 128), f32)],
        dmixed,
        wide,
        dtanh_all,
        gated,
        scratch=[pltpu.VMEM((2 * PIX, TAPS * 128), bf16), pltpu.VMEM((16, 128), f32)],
        us=18,
        name="hidden_grad",
    )
    aligned = crit_length == 85 * 128
    sent_rows = -(-85 * groups // 8) * 8 if aligned else devices * crit_length // 128
    both = call(
        critic_kernel,
        shape((GROUP if aligned else 1, sent_rows + 40, 128), f32),
        scalars,
        share,
        first_map,
        reals,
        head_rows,
        left_rows,
        sigma_rows,
        *frozen,
        *matrices,
        *right_cols,
        color_grad,
        smem=(0,),
        scratch=[
            pltpu.VMEM((1024, 1024), bf16),
            pltpu.VMEM((SLOTS * PIX, 8), bf16),
            pltpu.VMEM((128, 128), f32),
            pltpu.VMEM((8, 512), f32),
            pltpu.VMEM((devices * crit_length // 128, 128), f32),
        ],
        us=12,
        name="critic",
    )
    if groups == 4:
        got, keep, send, both = lax.optimization_barrier((steps[0], keep, send, both))
        steps.append(step(1, *got))
    keep = keep + swap(send, "c")
    first, second = keep[:, : pixels // 2], keep[:, pixels // 2 :]
    first = first[:2] + swap(first[2:], "y")
    second = second[::2] + swap(second[1::2], "x")
    if not aligned:
        message = both[0, sent_rows:]
        both = both[0, :sent_rows].reshape(groups, GROUP, crit_length)
        both = pad_rows(jnp.swapaxes(both, 0, 1).reshape(GROUP, -1))
        both = jnp.concatenate([both, jnp.broadcast_to(message, (GROUP, 40, 128))], axis=1)
    crit_rows = both.shape[1] - 40
    if groups == 4:
        got, first, second, both = lax.optimization_barrier((steps[1], first, second, both))
        a, b = part(1 + z) + got[0], part(z - 1) + got[1]
        a, b, first, second, both = lax.optimization_barrier((a, b, first, second, both))
        steps.append(step(2, a, b))
    first = first[0] + swap(first[1], "x")
    second = second[0] + swap(second[1], "y")
    dhidden = jnp.concatenate([first, second])
    both = lax.all_to_all(both, PLANE, 0, 0, tiled=True)
    first_grad = call(
        first_grad_kernel,
        shape((ROWS_FIRST, 128), f32),
        me,
        dhidden,
        pre,
        noise_all,
        smem=(0,),
        us=4,
        name="first_grad",
    )
    summed = jnp.sum(both[:, : crit_rows + 32], axis=0)
    message = jnp.concatenate([summed[crit_rows:], both[:, crit_rows + 32 :].reshape(64, 128)])
    both = pad_rows(summed[:crit_rows].reshape(-1)[: groups * crit_length].reshape(groups, -1))
    crit_rows = both.shape[1]
    both = jnp.concatenate([both, jnp.broadcast_to(message, (groups, 96, 128))], axis=1)
    if groups == 4:
        got_first = [lax.ppermute(first_grad, "z", [(k, 0)]) for k in (1, 2, 3)]
        first_sum = first_grad + got_first[0] + got_first[1] + got_first[2]
        reduced = part(z) + steps[2][0] + steps[2][1]
    else:
        first_sum = lax.psum(first_grad, "z")
        reduced = lax.psum_scatter(grad, "z", scatter_dimension=0, tiled=True)
    first_sum = jnp.where(z == 0, first_sum, 0.0)
    reduced = jnp.concatenate([reduced[:ROWS_FIRST] + first_sum, reduced[ROWS_FIRST:]], axis=0)
    reduced = lax.all_to_all(reduced.reshape(GROUP, rows, 128), PLANE, 0, 0, tiled=True)
    if groups == 4:
        rolled = [both[z]]
        for k in (1, 2, 3):
            piece = lax.dynamic_index_in_dim(both, lax.rem(z + k, 4), 0, keepdims=False)
            rolled.append(lax.ppermute(piece, "z", [(i, (i + k) % 4) for i in range(4)]))
        rolled = jnp.stack(rolled)
        both = jnp.stack([rolled[lax.rem(z + 4 - i, 4)] for i in range(4)])
    else:
        both = lax.all_to_all(both, "z", 0, 0, tiled=True)
    both = jnp.sum(both, axis=0)
    crit_reduced = both[:crit_rows].reshape(-1)[:crit_length]
    message = both[crit_rows : crit_rows + 32].reshape(8, 512)
    color_grad = both[crit_rows + 32 :].reshape(GROUP, 8, 128)[:, :3, :64]
    head_reduced = jnp.concatenate(
        [message[k, : KS[k]] for k in range(4)]
        + [jnp.swapaxes(color_grad, 1, 2).reshape(-1)]
    )
    losses = jnp.stack([message[4, 0], message[4, 128]])

    fix = 1.0 - jnp.power(f32(beta_first), update_ordinal[0].astype(f32))
    flat = (8 * rows, 128)
    gen = call(
        adam_kernel,
        [shape(flat, f32)] * 3,
        fix.reshape(1),
        reduced,
        maker_weight_arrays.reshape(flat),
        maker_mean_estimate.reshape(flat),
        maker_variance_estimate.reshape(flat),
        smem=(0,),
        hbm=(1, 2, 3, 4),
        out_hbm=(0, 1, 2),
        scratch=[pltpu.VMEM((GROUP, rows, 128), f32)]
        + [pltpu.VMEM(flat, f32)] * 4
        + [pltpu.SemaphoreType.DMA((16,)), pltpu.SemaphoreType.DMA((12,))],
        us=6,
        name="adam",
    )
    gen = [x.reshape(-1) for x in gen]
    crit = adamw_update(
        judge_weight_arrays, judge_mean_estimate, judge_variance_estimate, crit_reduced, fix
    )
    head = adamw_update(
        output_weight_rows, output_mean_estimate, output_variance_estimate, head_reduced, fix
    )
    return (*gen, *crit, *head, losses, power_new)


def solution(mesh):
    groups = mesh.shape["dp"] * mesh.shape["scale"] // GROUP
    grid = Mesh(mesh.devices.reshape(groups, 2, 2, 2), EVERY)
    split = P(EVERY)
    return jax.shard_map(
        functools.partial(local, groups),
        mesh=grid,
        in_specs=(split,) * 7 + (P(), split, P()) + (split,) * 6 + (P(),) * 3,
        out_specs=(split,) * 6 + (P(),) * 5,
        check_vma=False,
    )
```

```python
import functools

import jax
import jax.numpy as jnp
from jax import lax
from jax.experimental import pallas as pl
from jax.experimental.pallas import tpu as pltpu
from jax.sharding import Mesh
from jax.sharding import PartitionSpec as P

S = 32
Z = 256
GIN = 1024
GOUT = 512
CS = (24, 40, 112, 320)
KS = (64, 128, 256, 512)
CP = (128, 128, 128, 384)
KP = (128, 128, 256, 512)
SLOTS = 4
PIX = 256
GROUP = 8
IMAGE_TILES = 340
ROWS_FIRST = 256
TAPS = 9

leak_slope = 0.2
learn_rate = 0.03
beta_first = 0.5
beta_second = 0.5
adam_epsilon = 1e-08
weight_decay = 0.0001
norm_epsilon = 1e-06

f32 = jnp.float32
bf16 = jnp.bfloat16
PLANE = ("y", "x", "c")
EVERY = ("z", "y", "x", "c")
VMEM_LIMIT = 60 * 1024 * 1024

NN = (((1,), (0,)), ((), ()))
NT = (((1,), (1,)), ((), ()))
TN = (((0,), (0,)), ((), ()))


def dot(a, b, dims=NN):
    return lax.dot_general(a, b, dims, preferred_element_type=f32)


def call(kernel, out_shape, *args, scratch=(), smem=(), hbm=(), out_hbm=(), us=5, name=None):
    vmem = pl.BlockSpec(memory_space=pltpu.VMEM)
    spaces = {i: pl.BlockSpec(memory_space=pltpu.SMEM) for i in smem}
    spaces.update({i: pl.BlockSpec(memory_space=pl.ANY) for i in hbm})
    single = not isinstance(out_shape, (list, tuple))
    return pl.pallas_call(
        kernel,
        out_shape=out_shape,
        in_specs=[spaces.get(i, vmem) for i in range(len(args))],
        out_specs=vmem
        if single
        else [
            pl.BlockSpec(memory_space=pl.ANY) if i in out_hbm else vmem
            for i in range(len(out_shape))
        ],
        scratch_shapes=list(scratch),
        compiler_params=pltpu.CompilerParams(vmem_limit_bytes=VMEM_LIMIT),
        cost_estimate=pl.CostEstimate(
            flops=int(us * 1e8), bytes_accessed=int(us * 3e5), transcendentals=0
        ),
        name=name,
    )(*args)


def shape(dims, dtype):
    return jax.ShapeDtypeStruct(dims, dtype)


def split_two(x):
    high = x.astype(bf16)
    return high, (x - high.astype(f32)).astype(bf16)


def split_three(x):
    high = x.astype(bf16)
    rest = x - high.astype(f32)
    middle = rest.astype(bf16)
    return high, middle, (rest - middle.astype(f32)).astype(bf16)


def pack_kernel(w_ref, o_ref):
    rows = o_ref.shape[1]
    low_half = lax.broadcasted_iota(jnp.int32, (rows, 128), 1) < 64
    for j in range(4):
        a = w_ref[pl.ds(j, rows, stride=8), :]
        b = w_ref[pl.ds(j + 4, rows, stride=8), :]
        o_ref[2 * j] = jnp.where(low_half, a, pltpu.roll(b, 64, 1)).astype(bf16)
        o_ref[2 * j + 1] = jnp.where(low_half, pltpu.roll(a, 64, 1), b).astype(bf16)


def adam_pieces(rows):
    if rows % 8:
        return [(0, rows)]
    tiles = rows // 8
    cuts = [8 * (tiles * k // 4) for k in range(5)]
    return list(zip(cuts[:-1], cuts[1:]))


def adam_kernel(
    fix_ref, g_hbm, p_hbm, m_hbm, v_hbm, po_hbm, mo_hbm, vo_hbm,
    g_ref, p_ref, m_ref, v_ref, flat, in_sems, out_sems,
):
    pieces = adam_pieces(g_ref.shape[1])
    arrived, leaving = [], []
    for k, (low, high) in enumerate(pieces):
        here, wide = pl.ds(low, high - low), pl.ds(8 * low, 8 * (high - low))
        copies = [pltpu.make_async_copy(g_hbm.at[:, here, :], g_ref.at[:, here, :], in_sems.at[4 * k])]
        for n, (a, b) in enumerate(((p_hbm, p_ref), (m_hbm, m_ref), (v_hbm, v_ref))):
            copies.append(pltpu.make_async_copy(a.at[wide, :], b.at[wide, :], in_sems.at[4 * k + n + 1]))
        for copy in copies:
            copy.start()
        arrived.append(copies)
    for k, (low, high) in enumerate(pieces):
        for copy in arrived[k]:
            copy.wait()
        count = high - low
        half = lax.broadcasted_iota(jnp.int32, (count, 128), 1) < 64
        for j in range(4):
            a, b = g_ref[2 * j, low:high, :], g_ref[2 * j + 1, low:high, :]
            flat[pl.ds(8 * low + j, count, stride=8), :] = jnp.where(half, a, pltpu.roll(b, 64, 1))
            flat[pl.ds(8 * low + j + 4, count, stride=8), :] = jnp.where(half, pltpu.roll(a, 64, 1), b)
        wide = slice(8 * low, 8 * high)
        new, first, second = adamw_update(
            p_ref[wide, :], m_ref[wide, :], v_ref[wide, :], flat[wide, :], fix_ref[0]
        )
        p_ref[wide, :] = new
        m_ref[wide, :] = first
        v_ref[wide, :] = second
        wide = pl.ds(8 * low, 8 * count)
        for n, (a, b) in enumerate(((p_ref, po_hbm), (m_ref, mo_hbm), (v_ref, vo_hbm))):
            copy = pltpu.make_async_copy(a.at[wide, :], b.at[wide, :], out_sems.at[3 * k + n])
            copy.start()
            leaving.append(copy)
    for copy in leaving:
        copy.wait()


def adamw_update(master, first, second, grad, fix):
    first_new = beta_first * first + (1.0 - beta_first) * grad
    second_new = beta_second * second + (1.0 - beta_second) * grad * grad
    update = first_new / fix / (jnp.sqrt(second_new / fix) + adam_epsilon)
    return master - learn_rate * (update + weight_decay * master), first_new, second_new


SLOT_MASK = tuple(((m >> 1) & 1) * 4 + (m & 1) * 2 + (m >> 2) for m in range(GROUP))
SLOT_FIRST = tuple(2 * (m & 1) + ((m >> 1) & 1) for m in range(4))
SLOT_SECOND = tuple(4 + m for m in range(4))
NOISE_MASK = tuple((m & 1) * 4 + ((m >> 1) & 1) * 2 + (m >> 2) for m in range(GROUP))


def pre_kernel(me_ref, noise_ref, w_ref, pre_ref, hid_ref):
    for m in range(GROUP):
        rows = pl.ds(pl.multiple_of((me_ref[0] ^ NOISE_MASK[m]) * PIX, PIX), PIX)
        pre = dot(noise_ref[m], w_ref[...], TN)
        pre_ref[rows, :] = pre
        hid_ref[rows, :] = (pre * jax.nn.sigmoid(pre)).astype(bf16)


def turn_kernel(near_ref, far_ref, o_ref):
    for m in range(GROUP):
        source = near_ref if m < 4 else far_ref
        for part, at in enumerate((SLOT_FIRST[m % 4], SLOT_SECOND[m % 4])):
            o_ref[128 * m : 128 * m + 128, 1024 * part : 1024 * part + 1024] = jnp.transpose(
                source[at]
            )


def share_kernel(me_ref, *refs):
    blocks, out, four, sem = refs[:-3], refs[-3], refs[-2], refs[-1]
    rows = out.shape[2]
    tail = pl.ds(blocks[0].shape[0] - rows, rows)
    for here in range(4):

        @pl.when(me_ref[1] == here)
        def _():
            for k in range(4):
                pltpu.make_async_copy(blocks[3 + k - here].at[tail, :], four.at[k], sem).start()

    pltpu.make_async_copy(four, four, sem).wait()
    for q in range(GROUP):
        out[q] = four[...]


def pixel_column():
    return lax.broadcasted_iota(jnp.int32, (PIX, 128), 0) & 15


def from_left(x, column):
    return jnp.where(column > 0, pltpu.roll(x, 1, 0), 0.0)


def from_right(x, column):
    return jnp.where(column < 15, pltpu.roll(x, PIX - 1, 0), 0.0)


def from_above(x):
    return jnp.concatenate([jnp.zeros((16, x.shape[1]), x.dtype), x[:-16]], axis=0)


def from_below(x):
    return jnp.concatenate([x[16:], jnp.zeros((16, x.shape[1]), x.dtype)], axis=0)


def block_row(tap, q, half):
    return ROWS_FIRST + tap * GIN + half * GOUT + q * 64


def forward_kernel(*refs):
    me_ref, near_hbm, far_hbm, color_ref = refs[:4]
    factor_hbm, gated_hbm, rgb_ref, wide_hbm = refs[-13:-9]
    parts, w_ref, sem, near_ref, far_ref, factor_ref, gated_ref, wide, sems = refs[-9:]
    blocks = refs[4:-13]
    near_copy = pltpu.make_async_copy(near_hbm, near_ref, sems.at[0])
    far_copy = pltpu.make_async_copy(far_hbm, far_ref, sems.at[1])
    chunk = w_ref.shape[0] // 4
    if len(blocks) == 1:
        copy = pltpu.make_async_copy(blocks[0], w_ref, sem)
        copy.start()
        near_copy.start()
        far_copy.start()
        copy.wait()
    else:
        for here in range(4):

            @pl.when(me_ref[1] == here)
            def _():
                for k in range(4):
                    pltpu.make_async_copy(
                        blocks[3 + k - here].at[pl.ds(0, chunk), :],
                        w_ref.at[pl.ds(k * chunk, chunk), :],
                        sem,
                    ).start()

        near_copy.start()
        far_copy.start()
        pltpu.make_async_copy(w_ref, w_ref, sem).wait()
    for m in range(GROUP):
        q = me_ref[0] ^ SLOT_MASK[m]
        for tap in range(TAPS):
            for half in range(2):
                at = m * 128 + half * 64
                row = pl.multiple_of(block_row(tap, q, half), 64)
                wide[at : at + 64, 128 * tap : 128 * tap + 128] = w_ref[pl.ds(row, 64), :]
    wide[:, 128 * TAPS :] = jnp.zeros((GIN, 128), bf16)
    wide_copy = pltpu.make_async_copy(wide, wide_hbm, sems.at[2])
    wide_copy.start()
    near_copy.wait()
    far_copy.wait()

    def outgoing(b):
        rows = pl.ds(pl.multiple_of(b * PIX, PIX), PIX)
        return (
            pltpu.make_async_copy(
                factor_ref.at[:, rows, :], factor_hbm.at[:, rows, :], sems.at[3 + b]
            ),
            pltpu.make_async_copy(
                gated_ref.at[:, rows, :], gated_hbm.at[:, rows, :], sems.at[3 + GROUP + b]
            ),
        )

    low_half = lax.broadcasted_iota(jnp.int32, (PIX, 128), 1) < 64
    column = pixel_column()
    color_high, color_low = split_two(color_ref[...])
    color = jnp.concatenate([color_high, color_low], axis=0)

    @pl.loop(0, 4)
    def _(pair):
        start = pl.multiple_of(pair * 512, 512)
        local = pl.multiple_of((pair & 1) * 512, 512)
        first = pair < 2
        left = []
        for m in range(GROUP):
            at = jnp.where(first, SLOT_FIRST[m % 4], SLOT_SECOND[m % 4])
            left.append((near_ref if m < 4 else far_ref)[at, pl.ds(local, 512), :])
        left = jnp.concatenate(left, axis=1)
        for k in range(5):
            y = dot(left, wide[:, 256 * k : 256 * k + 256])
            parts[2 * k] = y[:, :128]
            if k < 4:
                parts[2 * k + 1] = y[:, 128:]
        for one in range(2):
            rows = pl.ds(pl.multiple_of(start + one * PIX, PIX), PIX)
            here = slice(one * PIX, one * PIX + PIX)
            cols = []
            for a in range(3):
                y0, y1, y2 = (parts[3 * a + b, here, :] for b in range(3))
                cols.append((from_left(y0, column) + (y1 + y2), (y0 + y1) + from_right(y2, column)))
            for pi in range(2):
                gated = []
                for pj in range(2):
                    if pi == 0:
                        mixed = from_above(cols[0][pj]) + (cols[1][pj] + cols[2][pj])
                    else:
                        mixed = (cols[0][pj] + cols[1][pj]) + from_below(cols[2][pj])
                    turned = pltpu.roll(mixed, 64, 1)
                    gate = jax.nn.sigmoid(jnp.where(low_half, turned, mixed))
                    value = jnp.where(low_half, mixed, turned)
                    gated.append(value * gate)
                    factor_ref[2 * pi + pj, rows, :] = jnp.where(
                        low_half, gate, gated[-1] * (1.0 - gate)
                    )
                both = jnp.where(low_half, gated[0], gated[1])
                gated_ref[pi, rows, :] = both
                high, low = split_two(both)
                rgb = dot(color, jnp.concatenate([high, low], axis=1), NT)
                rgb_ref[2 * pair + one, 16 * pi : 16 * pi + 16, :] = rgb[:16] + rgb[16:]
            for copy in outgoing(2 * pair + one):
                copy.start()

    @pl.loop(0, GROUP)
    def _(b):
        for copy in outgoing(b):
            copy.wait()

    wide_copy.wait()


def tap_sums(parts, column):
    sums = []
    for a in range(3):
        line = []
        for pj in range(2):
            even, odd = parts[pj], parts[2 + pj]
            if a == 0:
                line.append(odd + from_below(even))
            elif a == 1:
                line.append(even + odd)
            else:
                line.append(from_above(odd) + even)
        sums.append(line[1] + from_right(line[0], column))
        sums.append(line[0] + line[1])
        sums.append(from_left(line[1], column) + line[0])
    return sums


def weight_grad_kernel(
    me_ref, dt_ref, factor_hbm, hid_hbm, color_ref, g_hbm, dm_hbm, last_hbm, first_hbm,
    moved, factor_ref, hid_ref, g_ref, dm_ref, in_sems, dm_sems, out_sems,
):
    column = pixel_column()

    def piece(b):
        return pl.ds(pl.multiple_of(b * PIX, PIX), PIX)

    def factor_copy(b):
        return pltpu.make_async_copy(
            factor_hbm.at[:, piece(b), :], factor_ref.at[:, piece(b), :], in_sems.at[b]
        )

    def dm_copy(b):
        return pltpu.make_async_copy(
            dm_ref.at[:, piece(b), :], dm_hbm.at[:, piece(b), :], dm_sems.at[b]
        )

    def taps_copy(a):
        start = 0 if a == 0 else ROWS_FIRST + 3 * a * GIN
        at = pl.ds(start, ROWS_FIRST + 3 * (a + 1) * GIN - start)
        return pltpu.make_async_copy(g_ref.at[at, :], g_hbm.at[at, :], out_sems.at[a])

    chunk = last_hbm.shape[0]
    low = pl.ds(0, chunk)
    high = pl.ds(g_ref.shape[0] - chunk, chunk)
    first_copy = pltpu.make_async_copy(g_ref.at[low, :], first_hbm, out_sems.at[3])
    last_copy = pltpu.make_async_copy(g_ref.at[high, :], last_hbm, out_sems.at[4])
    for b in range(GROUP):
        factor_copy(b).start()
    hid_copy = pltpu.make_async_copy(hid_hbm, hid_ref, in_sems.at[GROUP])
    hid_copy.start()
    g_ref[:ROWS_FIRST, :] = jnp.zeros((ROWS_FIRST, 128), f32)
    c_high, c_middle, c_low = (x.astype(f32) for x in split_three(color_ref[...]))
    colors = jnp.concatenate([c_high, c_middle, c_low, c_high, c_middle, c_high], axis=0)
    colors = colors.astype(bf16)

    @pl.loop(0, GROUP)
    def _(b):
        rows = piece(b)
        factor_copy(b).wait()
        for phase in range(4):
            pi, pj = phase // 2, phase % 2
            high, middle, low = (
                x.astype(f32) for x in split_three(dt_ref[b, 8 * phase : 8 * phase + 8, :])
            )
            left = jnp.concatenate([high, high, high, middle, middle, low], axis=0).astype(bf16)
            spread = dot(left, colors, TN)
            low = (spread * factor_ref[phase, rows, :]).astype(bf16)
            dm_ref[phase, rows, :] = low
            plain = low.astype(f32)
            side = (from_right if pj == 0 else from_left)(plain, column)
            lanes = slice(128 * pj, 128 * pj + 128)
            for k, value in enumerate((plain, side)):
                line = (from_below if pi == 0 else from_above)(value)
                moved[4 * pi + k, rows, lanes] = value.astype(bf16)
                moved[4 * pi + 2 + k, rows, lanes] = line.astype(bf16)
        dm_copy(b).start()

    hid_copy.wait()

    def column_sums(at):
        plain = dot(hid_ref[...], moved[at])
        side = dot(hid_ref[...], moved[at + 1])
        return (
            plain[:, 128:] + side[:, :128],
            plain[:, :128] + plain[:, 128:],
            side[:, 128:] + plain[:, :128],
        )

    def put(tap, value, add):
        for m in range(GROUP):
            for half in range(2):
                q = me_ref[0] ^ SLOT_MASK[m]
                at = pl.ds(pl.multiple_of(block_row(tap, q, half), 64), 64)
                piece = value[128 * m + 64 * half : 128 * m + 64 * half + 64]
                g_ref[at, :] = g_ref[at, :] + piece if add else piece

    for at, takes in ((0, ((1, False), (2, False))), (4, ((0, False), (1, True)))):
        for b, value in enumerate(column_sums(at)):
            for a, add in takes:
                put(3 * a + b, value, add)
    taps_copy(1).start()
    for at, a in ((2, 0), (6, 2)):
        for b, value in enumerate(column_sums(at)):
            put(3 * a + b, value, True)
        (first_copy if a == 0 else last_copy).start()
        taps_copy(a).start()
    for a in range(3):
        taps_copy(a).wait()
    first_copy.wait()
    last_copy.wait()

    @pl.loop(0, GROUP)
    def _(b):
        dm_copy(b).wait()


def hidden_grad_kernel(
    dm_ref, wide_ref, dt_ref, gated_ref, keep_ref, send_ref, rgb_ref, sums, color
):
    column = pixel_column()
    color[...] = jnp.zeros_like(color)

    @pl.loop(0, GROUP)
    def _(b):
        rows = pl.ds(pl.multiple_of(b * PIX, PIX), PIX)
        parts = [dm_ref[phase, rows, :].astype(f32) for phase in range(4)]
        for tap, total in enumerate(tap_sums(parts, column)):
            high, low = split_two(total)
            sums[:PIX, 128 * tap : 128 * tap + 128] = high
            sums[PIX:, 128 * tap : 128 * tap + 128] = low
        for k in range(4):
            out = dot(sums[...], wide_ref[256 * k : 256 * k + 256, : 128 * TAPS], NT)
            out = out[:PIX] + out[PIX:]
            put = keep_ref if k < 2 else send_ref
            put[2 * (k % 2), rows, :] = out[:, :128]
            put[2 * (k % 2) + 1, rows, :] = out[:, 128:]
        for pi in range(2):
            high, low = split_two(dt_ref[b, 16 * pi : 16 * pi + 16, :])
            g_high, g_low = split_two(gated_ref[pi, rows, :])
            left = jnp.concatenate([high, low], axis=0)
            out = dot(left, jnp.concatenate([g_high, g_low], axis=1))
            color[...] += out[:16, :128] + (out[:16, 128:] + out[16:, :128])

    low_half = lax.broadcasted_iota(jnp.int32, (8, 128), 1) < 64
    folded = color[:8, :] + pltpu.roll(color[8:, :], 64, 1)
    rgb_ref[...] = jnp.where(low_half, folded, 0.0)


def first_grad_kernel(me_ref, dh_ref, pre_ref, noise_ref, o_ref):
    o_ref[...] = jnp.zeros_like(o_ref)
    for m in range(GROUP):
        rows = pl.ds(pl.multiple_of((me_ref[0] ^ NOISE_MASK[m]) * PIX, PIX), PIX)
        pre = pre_ref[rows, :]
        gate = jax.nn.sigmoid(pre)
        slope = gate * (1.0 + pre * (1.0 - gate))
        o_ref[...] += dot(noise_ref[m], (slope * dh_ref[rows, :]).astype(bf16))


def row_normalized(row):
    return row * lax.rsqrt(jnp.sum(row * row, axis=1, keepdims=True) + norm_epsilon)


def row_times(row, matrix, dims):
    pieces = jnp.concatenate(
        [jnp.broadcast_to(x.astype(f32), (8, row.shape[1])) for x in split_three(row)], axis=0
    ).astype(bf16)
    out = dot(pieces, matrix, dims)
    return out[0:1] + out[8:9] + out[16:17]


INS = (3,) + CS[:3]
CRIT_AT = (0, 4096, 20480, 86016)


def window(length):
    rows = length // 128 if length % 128 == 0 else -(-(127 + length) // 128)
    return -(-rows // 16) * 16


def prepare_kernel(
    crit_length, frozen_length, small_ref, own_ref, u_ref,
    e1, e2, e3, e4, r1, r2, r3, r4, m1, m2, m3, m4, c1, c2, c3, c4,
    left_ref, sigma_ref, share_ref, crit, frozen, moved, rows_buf,
):
    devices = GROUP * small_ref.shape[1]
    crit_rows, frozen_rows = window(crit_length), window(frozen_length)
    crit[...] = jnp.zeros_like(crit)
    frozen[...] = jnp.zeros_like(frozen)
    for k in range(devices):
        at = pl.ds((k * crit_length) // 128, crit_rows)
        crit[at, :] += small_ref[k % GROUP, k // GROUP, :crit_rows, :].astype(f32)
        at = pl.ds((k * frozen_length) // 128, frozen_rows)
        frozen[at, :] += small_ref[k % GROUP, k // GROUP, crit_rows : crit_rows + frozen_rows, :].astype(f32)
    live = jnp.zeros((1, 128), f32)
    for k in range(devices):
        at = crit_rows + frozen_rows
        live += small_ref[k % GROUP, k // GROUP, at : at + 16, :].astype(f32)[0:1]
    lane = lax.broadcasted_iota(jnp.int32, (1, 128), 1)
    real = jnp.sum(jnp.where((lane > 0) & (lane < SLOTS), live, 0.0), axis=1, keepdims=True)
    count = jnp.where(lane == 0, live, real) * float(IMAGE_TILES)
    share_ref[...] = jnp.broadcast_to(own_ref[...] / jnp.maximum(count, 1.0), share_ref.shape)

    def lanes_of(x):
        return lax.broadcasted_iota(jnp.int32, x.shape, 1)

    def shifted(a, b, lane_at):
        if lane_at == 0:
            return a
        turn = 128 - lane_at
        return jnp.where(lanes_of(a) < turn, pltpu.roll(a, turn, 1), pltpu.roll(b, turn, 1))

    def halves(x):
        low = lanes_of(x) < 64
        return jnp.where(low, x, 0.0), jnp.where(low, pltpu.roll(x, 64, 1), 0.0)

    def flush(ref, rows):
        ref[...] = rows_buf[: ref.shape[0], :].astype(bf16)
        rows_buf[:rows, :] = jnp.zeros((rows, 128), f32)

    total = frozen.shape[0] - 8
    moved[...] = shifted(frozen[:total, :], frozen[1 : total + 1, :], 8)
    rows_buf[...] = jnp.zeros_like(rows_buf)
    for ref, offset, rows, width in ((e1, 0, INS[0], CS[0]), (e2, 72, INS[1], CS[1])):
        for r in range(rows):
            a, lane_at = divmod(offset + r * width, 128)
            row = shifted(frozen[a : a + 1, :], frozen[a + 1 : a + 2, :], lane_at)
            rows_buf[r : r + 1, :] = jnp.where(lane < width, row, 0.0)
        flush(ref, 32)
    for i in range(8):
        a, lane_at = divmod(112 * i, 128)
        row = shifted(
            moved[pl.ds(8 + a, 5, stride=7), :], moved[pl.ds(9 + a, 5, stride=7), :], lane_at
        )
        rows_buf[pl.ds(i, 5, stride=8), :] = jnp.where(lanes_of(row) < 112, row, 0.0)
    flush(e3, 40)
    five = [moved[pl.ds(43 + k, 56, stride=5), :] for k in range(5)]
    pairs = (
        (five[0], shifted(five[2], five[3], 64)),
        (five[1], shifted(five[3], five[4], 64)),
        (halves(five[2])[0], halves(five[4])[1]),
    )
    e4[...] = jnp.zeros_like(e4)
    for b, (even, odd) in enumerate(pairs):
        rows_buf[pl.ds(0, 56, stride=2), :] = even
        rows_buf[pl.ds(1, 56, stride=2), :] = odd
        e4[:112, 128 * b : 128 * b + 128] = rows_buf[:112, :].astype(bf16)
    rows_buf[...] = jnp.zeros_like(rows_buf)
    even, odd = halves(moved[323:335, :])
    rows_buf[pl.ds(0, 12, stride=2), :] = even
    rows_buf[pl.ds(1, 12, stride=2), :] = odd
    flush(r1, 24)
    rows_buf[:40, :] = moved[335:375, :]
    flush(r2, 40)
    r3[...] = jnp.zeros_like(r3)
    r4[...] = jnp.zeros_like(r4)
    for b in range(2):
        r3[:112, 128 * b : 128 * b + 128] = moved[pl.ds(375 + b, 112, stride=2), :].astype(bf16)
    for b in range(4):
        r4[:320, 128 * b : 128 * b + 128] = moved[pl.ds(599 + b, 320, stride=4), :].astype(bf16)
    even, odd = halves(crit[:32, :])
    rows_buf[pl.ds(0, 32, stride=2), :] = even
    rows_buf[pl.ds(1, 32, stride=2), :] = odd
    flush(m1, 64)
    m2[...] = crit[32:160, :].astype(bf16)
    for b in range(2):
        m3[:, 128 * b : 128 * b + 128] = crit[pl.ds(160 + b, 256, stride=2), :].astype(bf16)
    for b in range(4):
        m4[:, 128 * b : 128 * b + 128] = crit[pl.ds(672 + b, 512, stride=4), :].astype(bf16)

    left_ref[...] = jnp.zeros_like(left_ref)
    sigma_ref[...] = jnp.ones_like(sigma_ref)
    for k, (m_ref, c_ref) in enumerate(((m1, c1), (m2, c2), (m3, c3), (m4, c4))):
        width = KP[k]
        matrix = m_ref[...]
        right = row_normalized(row_times(u_ref[k : k + 1, :width], matrix, NT))
        turned = row_times(right, matrix, NN)
        left = row_normalized(turned)
        left_ref[k : k + 1, :width] = left
        sigma = jnp.sum(left * turned, axis=1, keepdims=True)
        sigma_ref[k : k + 1, :] = jnp.broadcast_to(sigma, (1, 128))
        c_ref[...] = jnp.transpose(jnp.broadcast_to(right, (128, width)))


def wanted_code(scal_ref, slot):
    d = lax.broadcasted_iota(jnp.int32, (1, 1024), 1)

    def bit(k):
        return (d >> k) & 1

    i = bit(9) + 2 * bit(7) + 4 * bit(5) + 8 * bit(3) + 16 * bit(1)
    j = bit(8) + 2 * bit(6) + 4 * bit(4) + 8 * bit(2) + 16 * bit(0)
    down, across, flip, top, side = (scal_ref[slot, k] for k in range(5))
    row = i - down
    moved = j - across
    fine = (row >= 0) & (row < S) & (moved >= 0) & (moved < S)
    source = jnp.where(flip == 1, S - 1 - moved, moved)
    boxed = (i >= top) & (i < top + S // 2) & (j >= side) & (j < side + S // 2)
    return jnp.where(fine & jnp.logical_not(boxed), row * S + source, -1)


def three(x):
    return jnp.concatenate([v.astype(f32) for v in split_three(x)], axis=0).astype(bf16)


def fold(x):
    return x[0:8] + x[8:16] + x[16:24]


def fill_pick(pick, scal_ref, slot, phases):
    want = wanted_code(scal_ref, slot)

    @pl.loop(0, 8)
    def _(k):
        s = lax.broadcasted_iota(jnp.int32, (128, 1024), 0) + k * 128
        if phases:
            at = s & 255
            s = (2 * (at >> 4) + (s >> 9)) * S + 2 * (at & 15) + ((s >> 8) & 1)
        hit = jnp.where(s == want, 1.0, 0.0).astype(bf16)
        pick[pl.ds(pl.multiple_of(k * 128, 128), 128), :] = hit


def augmented(image, pick):
    seen = fold(dot(three(image), pick[...]))
    small = 0.25 * ((seen[:, :256] + seen[:, 256:512]) + (seen[:, 512:768] + seen[:, 768:]))
    return jnp.transpose(small).astype(bf16)


def last_pool(slots):
    row = lax.broadcasted_iota(jnp.int32, (16, 16 * slots), 0)
    col = lax.broadcasted_iota(jnp.int32, (16, 16 * slots), 1)
    pool = jnp.where((row // 4 == col // 16) & (row % 4 == col % 4), 0.25, 0.0)
    return jnp.concatenate([pool.astype(bf16)] * 3, axis=1)


def critic_levels(inputs, slots, extract, project, matrices, head_ref, sigma_ref):
    levels = []
    pool = last_pool(slots)
    for k in range(4):
        count = 16 if k == 3 else (slots * PIX) >> (2 * k)
        width = KP[k]
        pre = dot(inputs, extract[k][...])
        active = pre * jax.nn.sigmoid(pre)
        feat = dot(active.astype(bf16), project[k][...]).astype(bf16)
        raw = dot(feat, matrices[k][...])
        sigma = sigma_ref[k : k + 1, 0:1]
        scaled = raw / sigma
        slope = jnp.where(scaled >= 0, 1.0, leak_slope)
        leaky = scaled * slope
        head = head_ref[k : k + 1, :width]
        scale = lax.rsqrt(jnp.sum(head * head, axis=1, keepdims=True) + norm_epsilon)
        unit = head * scale
        logit = jnp.sum(leaky * unit, axis=1, keepdims=True)
        levels.append((pre, feat, raw, sigma, slope, leaky, head, scale, unit, logit))
        if k < 2:
            blocks = active.reshape(slots, 4, count // (4 * slots), CP[k])
            total = (blocks[:, 0] + blocks[:, 1]) + (blocks[:, 2] + blocks[:, 3])
            inputs = (0.25 * total).reshape(count // 4, CP[k]).astype(bf16)
        elif k == 2:
            inputs = dot(pool, three(active)).astype(bf16)
    return levels


def image_grad_kernel(
    scal_ref,
    share_ref,
    got_ref,
    head_ref,
    sigma_ref,
    e1, e2, e3, e4,
    r1, r2, r3, r4,
    m1, m2, m3, m4,
    dt_ref,
    map_ref,
    pick,
):
    extract, project, matrices = (e1, e2, e3, e4), (r1, r2, r3, r4), (m1, m2, m3, m4)
    fill_pick(pick, scal_ref, 0, True)
    color = got_ref[0]
    for k in range(1, GROUP):
        color = color + got_ref[k]
    color = jnp.tanh(color)
    fake = jnp.concatenate([color[8 * k : 8 * k + 8] for k in range(4)], axis=1)
    first_map = augmented(fake, pick)
    map_ref[...] = first_map
    levels = critic_levels(first_map, 1, extract, project, matrices, head_ref, sigma_ref)
    row = lax.broadcasted_iota(jnp.int32, (16, 16), 0)
    col = lax.broadcasted_iota(jnp.int32, (16, 16), 1)
    spread = jnp.where((col < 4) & (row % 4 == col), 0.25, 0.0)
    spread = jnp.concatenate([spread.astype(bf16)] * 3, axis=1)
    carry = None
    for k in (3, 2, 1, 0):
        pre, feat, raw, sigma, slope, leaky, head, scale, unit, logit = levels[k]
        dlogit = -share_ref[0:1, 0:1] * jax.nn.sigmoid(-logit)
        if k == 3:
            dlogit = jnp.where(lax.broadcasted_iota(jnp.int32, (16, 1), 0) < 4, dlogit, 0.0)
        dscaled = dlogit * unit * slope
        dfeat = dot((dscaled / sigma).astype(bf16), matrices[k][...], NT).astype(bf16)
        dactive = dot(dfeat, project[k][...], NT)
        if carry is not None:
            dactive = dactive + carry
        gate = jax.nn.sigmoid(pre)
        dpre = (gate * (1.0 + pre * (1.0 - gate)) * dactive).astype(bf16)
        dinput = dot(dpre, extract[k][...], NT)
        if k == 3:
            carry = dot(spread, three(dinput))
        elif k > 0:
            carry = jnp.concatenate([0.25 * dinput] * 4, axis=0)
    daug = 0.25 * jnp.transpose(dinput)
    daug = jnp.concatenate([daug] * 4, axis=1)
    dimage = fold(dot(three(daug), pick[...], NT))
    dtanh = dimage * (1.0 - fake * fake)
    for q in range(GROUP):
        for k in range(4):
            dt_ref[q, 8 * k : 8 * k + 8, :] = dtanh[:, 256 * k : 256 * k + 256]


def critic_kernel(
    scal_ref,
    share_ref,
    map_ref,
    real_ref,
    head_ref,
    left_ref,
    sigma_ref,
    e1, e2, e3, e4,
    r1, r2, r3, r4,
    m1, m2, m3, m4,
    c1, c2, c3, c4,
    color_ref,
    sent_ref,
    pick,
    first_map,
    corner,
    out_ref,
    flat_ref,
):
    extract, project = (e1, e2, e3, e4), (r1, r2, r3, r4)
    matrices, columns = (m1, m2, m3, m4), (c1, c2, c3, c4)
    first_map[:PIX, :] = map_ref[...]
    for slot in range(1, SLOTS):
        fill_pick(pick, scal_ref, slot, False)
        first_map[slot * PIX : slot * PIX + PIX, :] = augmented(real_ref[slot - 1], pick)
    levels = critic_levels(first_map[...], SLOTS, extract, project, matrices, head_ref, sigma_ref)
    loss_gen = jnp.zeros((1, 1), f32)
    loss_critic = jnp.zeros((1, 1), f32)
    out_ref[...] = jnp.zeros_like(out_ref)
    for k in range(4):
        pre, feat, raw, sigma, slope, leaky, head, scale, unit, logit = levels[k]
        count, width = logit.shape[0], KP[k]
        slot = lax.broadcasted_iota(jnp.int32, (count, 1), 0) // (count // SLOTS)
        share = share_ref[0:1, 0:1]
        for other in range(1, SLOTS):
            share = jnp.where(slot == other, share_ref[0:1, other : other + 1], share)
        sign = jnp.where(slot == 0, -1.0, 1.0)
        hinge = 1.0 - sign * logit
        loss_critic += jnp.sum(share * jnp.maximum(hinge, 0.0), axis=0, keepdims=True)
        dlogit = jnp.where(hinge > 0, -sign * share, 0.0)
        soft = jnp.maximum(-logit, 0.0) + jnp.log1p(jnp.exp(-jnp.abs(logit)))
        loss_gen += jnp.sum(jnp.where(slot == 0, share * soft, 0.0), axis=0, keepdims=True)
        dscaled = dlogit * unit * slope
        grad = dot(feat, (dscaled / sigma).astype(bf16), TN)
        dsigma = jnp.sum(jnp.sum(dscaled * raw, axis=1, keepdims=True), axis=0, keepdims=True)
        dsigma = -dsigma / (sigma * sigma)
        side = columns[k][...] * dsigma
        for b in range(width // 128):
            lanes = slice(128 * b, 128 * b + 128)
            piece = grad[:, lanes] + side * left_ref[k : k + 1, lanes]
            if k == 0:
                corner[...] = piece
                low = lax.broadcasted_iota(jnp.int32, (32, 128), 1) < 64
                even, odd = corner[pl.ds(0, 32, stride=2), :], corner[pl.ds(1, 32, stride=2), :]
                flat_ref[:32, :] = jnp.where(low, even, pltpu.roll(odd, 64, 1))
            else:
                stride = width // 128
                flat_ref[pl.ds(CRIT_AT[k] // 128 + b, width, stride=stride), :] = piece
        dunit = jnp.sum(leaky * dlogit, axis=0, keepdims=True)
        inner = jnp.sum(head * dunit, axis=1, keepdims=True)
        out_ref[k : k + 1, :width] = scale * dunit - head * (scale * scale * scale * inner)
    out_ref[4:5, 0:128] = jnp.broadcast_to(loss_gen, (1, 128))
    out_ref[4:5, 128:256] = jnp.broadcast_to(loss_critic, (1, 128))
    rows = sent_ref.shape[1] - 40
    if sent_ref.shape[0] == GROUP:
        groups = rows // 85
        for q in range(GROUP):
            for z in range(groups):
                at = (z * GROUP + q) * 85
                sent_ref[q, z * 85 : z * 85 + 85, :] = flat_ref[at : at + 85, :]
            sent_ref[q, groups * 85 : rows, :] = jnp.zeros((rows - groups * 85, 128), f32)
    else:
        sent_ref[0, :rows, :] = flat_ref[...]
    for q in range(sent_ref.shape[0]):
        for k in range(8):
            for b in range(4):
                at = rows + 4 * k + b
                sent_ref[q, at : at + 1, :] = out_ref[k : k + 1, 128 * b : 128 * b + 128]
        sent_ref[q, rows + 32 :, :] = color_ref[...]


def local(
    groups,
    noise_maps,
    dataset_lowres_images,
    dataset_highres_images,
    occupied_mask,
    shift_amounts,
    mirror_indicator,
    erase_box_corner,
    update_ordinal,
    fixed_backbone_params,
    singular_estimate_dirs,
    maker_weight_arrays,
    maker_mean_estimate,
    maker_variance_estimate,
    judge_weight_arrays,
    judge_mean_estimate,
    judge_variance_estimate,
    output_weight_rows,
    output_mean_estimate,
    output_variance_estimate,
):
    devices = groups * GROUP
    rows = maker_weight_arrays.shape[0] // 1024
    chunk = GROUP * rows
    z = lax.axis_index("z")
    q = (lax.axis_index("y") * 2 + lax.axis_index("x")) * 2 + lax.axis_index("c")
    me = jnp.stack([q, z]).astype(jnp.int32)

    def pad_rows(x):
        return jnp.pad(x, ((0, 0), (0, -x.shape[1] % 1024))).reshape(x.shape[0], -1, 128)

    def swap(x, axis):
        return lax.ppermute(x, axis, [(0, 1), (1, 0)])

    crit_length = judge_weight_arrays.shape[0]
    frozen_length = fixed_backbone_params.shape[0]
    member = z * GROUP + q

    def windowed(x):
        length = x.shape[0]
        rows_here = window(length)
        if length % 128 == 0:
            return jnp.pad(x.reshape(-1, 128), ((0, rows_here - length // 128), (0, 0)))
        empty = jnp.zeros((rows_here * 128,), bf16)
        start = lax.rem(member * length, 128)
        return lax.dynamic_update_slice(empty, x, (start,)).reshape(rows_here, 128)

    own = occupied_mask.astype(f32)
    small = jnp.concatenate(
        [
            windowed(judge_weight_arrays.astype(bf16)),
            windowed(fixed_backbone_params),
            jnp.pad(own.astype(bf16), ((0, 15), (0, 128 - SLOTS))),
        ]
    )

    def rows_of(flat):
        out, offset = [], 0
        for k in range(4):
            out.append(jnp.pad(flat[offset : offset + KS[k]], (0, 512 - KS[k])))
            offset += KS[k]
        return jnp.pad(jnp.stack(out), ((0, 4), (0, 0)))

    head_rows = rows_of(output_weight_rows)
    start_rows = rows_of(singular_estimate_dirs)
    own_row = jnp.pad(own, ((0, 0), (0, 128 - SLOTS)))
    color_all = output_weight_rows[960:].reshape(GOUT, 3)
    color = jnp.pad(lax.dynamic_slice(color_all, (q * 64, 0), (64, 3)).T, ((0, 5), (0, 0)))
    none = jnp.zeros_like(color)
    color_left = jnp.concatenate(
        [
            jnp.concatenate([color, none, color, none], axis=1),
            jnp.concatenate([none, color, none, color], axis=1),
        ],
        axis=0,
    )
    color_twice = jnp.concatenate([color, color], axis=1)
    small_images = dataset_lowres_images.astype(f32)
    large = dataset_highres_images.astype(f32).reshape(1, 3, S, 2, S, 2)
    large = jnp.mean(large, axis=(3, 5)).reshape(1, 3, S * S)
    reals = jnp.pad(jnp.concatenate([small_images, large]), ((0, 0), (0, 5), (0, 0)))
    scalars = jnp.concatenate(
        [shift_amounts[0], mirror_indicator[0][:, None], erase_box_corner[0]], axis=1
    )

    noise_all = jnp.concatenate([noise_maps, swap(noise_maps, "y")])

    packed = call(
        pack_kernel,
        shape((GROUP, rows, 128), bf16),
        maker_weight_arrays.reshape(8 * rows, 128),
        us=3,
        name="pack",
    )
    slices = lax.all_to_all(packed, PLANE, 0, 0, tiled=True).reshape(chunk, 128)
    slices, noise_all = lax.optimization_barrier((slices, noise_all))
    for axis in ("x", "c"):
        noise_all = jnp.concatenate([noise_all, swap(noise_all, axis)])
    first_block = slices[:ROWS_FIRST]

    def hop(x, y):
        down = lax.ppermute(x, "z", [(0, 1), (1, 2), (2, 3)])
        return down, lax.ppermute(y, "z", [(1, 0), (2, 1), (3, 2)])

    if groups == 4:
        sent = [lax.ppermute(first_block, "z", [(0, k)]) for k in (1, 2, 3)]
        riding = jnp.concatenate([slices, small])
        hop_one = hop(riding, riding)
        ready = (head_rows, start_rows, own_row, color_left, color_twice, reals, scalars, me)
        sent, hop_one, ready = lax.optimization_barrier((sent, hop_one, ready))
        head_rows, start_rows, own_row, color_left, color_twice, reals, scalars, me = ready
        first_weights = jnp.where(z == 0, first_block, sent[0] + sent[1] + sent[2])
        hop_two = hop(*hop_one)
    else:
        first_weights = lax.all_gather(first_block, "z", axis=0)[0]
        blocks = [lax.all_gather(slices, "z", axis=0, tiled=True)]

    pixels = GROUP * PIX
    pre, hid = call(
        pre_kernel,
        [shape((pixels, 128), f32), shape((pixels, 128), bf16)],
        me,
        noise_all,
        first_weights,
        smem=(0,),
        us=4,
        name="pre",
    )
    first, second = hid[: pixels // 2], hid[pixels // 2 :]
    first = jnp.stack([first, swap(first, "y")])
    second = jnp.stack([second, swap(second, "x")])
    if groups == 4:
        first, second, hop_two = lax.optimization_barrier((first, second, hop_two))
        hop_three = hop(*hop_two)
    first = jnp.concatenate([first, swap(first, "x")])
    second = jnp.concatenate([second, swap(second, "y")])
    if groups == 4:
        first, second, hop_three = lax.optimization_barrier((first, second, hop_three))
        blocks = [hop_three[0], hop_two[0], hop_one[0], riding, hop_one[1], hop_two[1], hop_three[1]]
        (small,) = call(
            share_kernel,
            [shape((GROUP, 4) + small.shape, bf16)],
            me,
            *blocks,
            smem=(0,),
            hbm=range(1, 8),
            scratch=[pltpu.VMEM((4,) + small.shape, bf16), pltpu.SemaphoreType.DMA],
            us=3,
            name="share",
        )
    else:
        small = lax.all_gather(small, "z", axis=0)
        small = jnp.broadcast_to(small, (GROUP,) + small.shape)
    near = jnp.concatenate([first, second])
    far = swap(near, "c")
    near, far, small = lax.optimization_barrier((near, far, small))
    small = lax.all_to_all(small, PLANE, 0, 0, tiled=True)
    factor, gated, rgb, wide = call(
        forward_kernel,
        [
            shape((4, pixels, 128), f32),
            shape((2, pixels, 128), f32),
            shape((GROUP, 32, PIX), f32),
            shape((GIN, 1280), bf16),
        ],
        me,
        near,
        far,
        color_left,
        *blocks,
        smem=(0,),
        hbm=(1, 2, *range(4, 4 + len(blocks))),
        out_hbm=(0, 1, 3),
        scratch=[
            pltpu.VMEM((TAPS + 1, 512, 128), f32),
            pltpu.VMEM((groups * chunk, 128), bf16),
            pltpu.SemaphoreType.DMA,
            pltpu.VMEM((GROUP, pixels // 2, 128), bf16),
            pltpu.VMEM((GROUP, pixels // 2, 128), bf16),
            pltpu.VMEM((4, pixels, 128), f32),
            pltpu.VMEM((2, pixels, 128), f32),
            pltpu.VMEM((GIN, 1280), bf16),
            pltpu.SemaphoreType.DMA((3 + 2 * GROUP,)),
        ],
        us=14,
        name="forward",
    )
    got = lax.all_to_all(rgb, PLANE, 0, 0, tiled=True)
    near, far, factor, small = lax.optimization_barrier((near, far, factor, small))
    squares = [shape((8, CP[0]), bf16)] + [shape((CP[k - 1], CP[k]), bf16) for k in (1, 2, 3)]
    squares += [shape((CP[k], KP[k]), bf16) for k in range(4)]
    squares += [shape((KP[k], KP[k]), bf16) for k in range(4)]
    squares += [shape((KP[k], 128), f32) for k in range(4)]
    squares += [shape((8, 512), f32), shape((8, 128), f32), shape((8, 128), f32)]
    crit_space = -(-((devices - 1) * crit_length // 128 + window(crit_length)) // 8) * 8
    frozen_space = -(-((devices - 1) * frozen_length // 128 + window(frozen_length)) // 8) * 8 + 8
    prepared = call(
        functools.partial(prepare_kernel, crit_length, frozen_length),
        squares,
        small,
        own_row,
        start_rows,
        scratch=[
            pltpu.VMEM((crit_space, 128), f32),
            pltpu.VMEM((frozen_space, 128), f32),
            pltpu.VMEM((frozen_space - 8, 128), f32),
            pltpu.VMEM((128, 128), f32),
        ],
        us=8,
        name="prepare",
    )
    frozen, matrices, right_cols = prepared[:8], prepared[8:12], prepared[12:16]
    left_rows, sigma_rows, share = prepared[16:]
    power_new = jnp.concatenate([left_rows[k, : KS[k]] for k in range(4)])
    dtanh, first_map = call(
        image_grad_kernel,
        [shape((GROUP, 32, PIX), f32), shape((PIX, 8), bf16)],
        scalars,
        share,
        got,
        head_rows,
        sigma_rows,
        *frozen,
        *matrices,
        smem=(0,),
        scratch=[pltpu.VMEM((1024, 1024), bf16)],
        us=8,
        name="image_grad",
    )

    near, far, dtanh = lax.optimization_barrier((near, far, dtanh))
    hid_turned = call(turn_kernel, shape((GIN, pixels), bf16), near, far, us=5, name="turn")
    dtanh_all = lax.all_to_all(dtanh, PLANE, 0, 0, tiled=True)
    grad, dmixed, last_chunk, first_chunk = call(
        weight_grad_kernel,
        [shape((ROWS_FIRST + TAPS * GIN, 128), f32), shape((4, pixels, 128), bf16)]
        + [shape((chunk, 128), f32)] * 2,
        me,
        dtanh_all,
        factor,
        hid_turned,
        color_twice,
        smem=(0,),
        hbm=(2, 3),
        out_hbm=(0, 1, 2, 3),
        scratch=[
            pltpu.VMEM((8, pixels, 256), bf16),
            pltpu.VMEM((4, pixels, 128), f32),
            pltpu.VMEM((GIN, pixels), bf16),
            pltpu.VMEM((ROWS_FIRST + TAPS * GIN, 128), f32),
            pltpu.VMEM((4, pixels, 128), bf16),
            pltpu.SemaphoreType.DMA((GROUP + 1,)),
            pltpu.SemaphoreType.DMA((GROUP,)),
            pltpu.SemaphoreType.DMA((5,)),
        ],
        us=20,
        name="weight_grad",
    )
    steps = []
    if groups == 4:

        def part(k):
            return lax.dynamic_slice_in_dim(grad, jnp.clip(k, 0, 3) * chunk, chunk, axis=0)

        def step(s, a, b):
            if s == 1:
                a, b = part(2 + z) + a, part(z - 2) + b
            down = lax.ppermute(a, "z", [(k, k + 1) for k in range(s + 1)])
            up = lax.ppermute(b, "z", [(3 - k, 2 - k) for k in range(s + 1)])
            return lax.optimization_barrier((down, up))

        first_a, first_b, first_map, dmixed = lax.optimization_barrier(
            (last_chunk, first_chunk, first_map, dmixed)
        )
        steps.append(step(0, first_a, first_b))
    keep, send, color_grad = call(
        hidden_grad_kernel,
        [shape((4, pixels, 128), f32), shape((4, pixels, 128), f32), shape((8, 128), f32)],
        dmixed,
        wide,
        dtanh_all,
        gated,
        scratch=[pltpu.VMEM((2 * PIX, TAPS * 128), bf16), pltpu.VMEM((16, 128), f32)],
        us=18,
        name="hidden_grad",
    )
    aligned = crit_length == 85 * 128
    sent_rows = -(-85 * groups // 8) * 8 if aligned else devices * crit_length // 128
    both = call(
        critic_kernel,
        shape((GROUP if aligned else 1, sent_rows + 40, 128), f32),
        scalars,
        share,
        first_map,
        reals,
        head_rows,
        left_rows,
        sigma_rows,
        *frozen,
        *matrices,
        *right_cols,
        color_grad,
        smem=(0,),
        scratch=[
            pltpu.VMEM((1024, 1024), bf16),
            pltpu.VMEM((SLOTS * PIX, 8), bf16),
            pltpu.VMEM((128, 128), f32),
            pltpu.VMEM((8, 512), f32),
            pltpu.VMEM((devices * crit_length // 128, 128), f32),
        ],
        us=12,
        name="critic",
    )
    if groups == 4:
        got, keep, send, both = lax.optimization_barrier((steps[0], keep, send, both))
        steps.append(step(1, *got))
    keep = keep + swap(send, "c")
    first, second = keep[:, : pixels // 2], keep[:, pixels // 2 :]
    first = first[:2] + swap(first[2:], "y")
    second = second[::2] + swap(second[1::2], "x")
    if not aligned:
        message = both[0, sent_rows:]
        both = both[0, :sent_rows].reshape(groups, GROUP, crit_length)
        both = pad_rows(jnp.swapaxes(both, 0, 1).reshape(GROUP, -1))
        both = jnp.concatenate([both, jnp.broadcast_to(message, (GROUP, 40, 128))], axis=1)
    crit_rows = both.shape[1] - 40
    if groups == 4:
        got, first, second, both = lax.optimization_barrier((steps[1], first, second, both))
        a, b = part(1 + z) + got[0], part(z - 1) + got[1]
        a, b, first, second, both = lax.optimization_barrier((a, b, first, second, both))
        steps.append(step(2, a, b))
    first = first[0] + swap(first[1], "x")
    second = second[0] + swap(second[1], "y")
    dhidden = jnp.concatenate([first, second])
    both = lax.all_to_all(both, PLANE, 0, 0, tiled=True)
    first_grad = call(
        first_grad_kernel,
        shape((ROWS_FIRST, 128), f32),
        me,
        dhidden,
        pre,
        noise_all,
        smem=(0,),
        us=4,
        name="first_grad",
    )
    summed = jnp.sum(both[:, : crit_rows + 32], axis=0)
    message = jnp.concatenate([summed[crit_rows:], both[:, crit_rows + 32 :].reshape(64, 128)])
    both = pad_rows(summed[:crit_rows].reshape(-1)[: groups * crit_length].reshape(groups, -1))
    crit_rows = both.shape[1]
    both = jnp.concatenate([both, jnp.broadcast_to(message, (groups, 96, 128))], axis=1)
    if groups == 4:
        got_first = [lax.ppermute(first_grad, "z", [(k, 0)]) for k in (1, 2, 3)]
        first_sum = first_grad + got_first[0] + got_first[1] + got_first[2]
        reduced = part(z) + steps[2][0] + steps[2][1]
    else:
        first_sum = lax.psum(first_grad, "z")
        reduced = lax.psum_scatter(grad, "z", scatter_dimension=0, tiled=True)
    first_sum = jnp.where(z == 0, first_sum, 0.0)
    reduced = jnp.concatenate([reduced[:ROWS_FIRST] + first_sum, reduced[ROWS_FIRST:]], axis=0)
    reduced = lax.all_to_all(reduced.reshape(GROUP, rows, 128), PLANE, 0, 0, tiled=True)
    if groups == 4:
        rolled = [both[z]]
        for k in (1, 2, 3):
            piece = lax.dynamic_index_in_dim(both, lax.rem(z + k, 4), 0, keepdims=False)
            rolled.append(lax.ppermute(piece, "z", [(i, (i + k) % 4) for i in range(4)]))
        rolled = jnp.stack(rolled)
        both = jnp.stack([rolled[lax.rem(z + 4 - i, 4)] for i in range(4)])
    else:
        both = lax.all_to_all(both, "z", 0, 0, tiled=True)
    both = jnp.sum(both, axis=0)
    crit_reduced = both[:crit_rows].reshape(-1)[:crit_length]
    message = both[crit_rows : crit_rows + 32].reshape(8, 512)
    color_grad = both[crit_rows + 32 :].reshape(GROUP, 8, 128)[:, :3, :64]
    head_reduced = jnp.concatenate(
        [message[k, : KS[k]] for k in range(4)]
        + [jnp.swapaxes(color_grad, 1, 2).reshape(-1)]
    )
    losses = jnp.stack([message[4, 0], message[4, 128]])

    fix = 1.0 - jnp.power(f32(beta_first), update_ordinal[0].astype(f32))
    flat = (8 * rows, 128)
    gen = call(
        adam_kernel,
        [shape(flat, f32)] * 3,
        fix.reshape(1),
        reduced,
        maker_weight_arrays.reshape(flat),
        maker_mean_estimate.reshape(flat),
        maker_variance_estimate.reshape(flat),
        smem=(0,),
        hbm=(1, 2, 3, 4),
        out_hbm=(0, 1, 2),
        scratch=[pltpu.VMEM((GROUP, rows, 128), f32)]
        + [pltpu.VMEM(flat, f32)] * 4
        + [pltpu.SemaphoreType.DMA((16,)), pltpu.SemaphoreType.DMA((12,))],
        us=6,
        name="adam",
    )
    gen = [x.reshape(-1) for x in gen]
    crit = adamw_update(
        judge_weight_arrays, judge_mean_estimate, judge_variance_estimate, crit_reduced, fix
    )
    head = adamw_update(
        output_weight_rows, output_mean_estimate, output_variance_estimate, head_reduced, fix
    )
    return (*gen, *crit, *head, losses, power_new)


def solution(mesh):
    groups = mesh.shape["dp"] * mesh.shape["scale"] // GROUP
    grid = Mesh(mesh.devices.reshape(groups, 2, 2, 2), EVERY)
    split = P(EVERY)
    return jax.shard_map(
        functools.partial(local, groups),
        mesh=grid,
        in_specs=(split,) * 7 + (P(), split, P()) + (split,) * 6 + (P(),) * 3,
        out_specs=(split,) * 6 + (P(),) * 5,
        check_vma=False,
    )
```

```python
import functools

import jax
import jax.numpy as jnp
from jax import lax
from jax.experimental import pallas as pl
from jax.experimental.pallas import tpu as pltpu
from jax.sharding import Mesh
from jax.sharding import PartitionSpec as P

S = 32
Z = 256
GIN = 1024
GOUT = 512
CS = (24, 40, 112, 320)
KS = (64, 128, 256, 512)
CP = (128, 128, 128, 384)
KP = (128, 128, 256, 512)
SLOTS = 4
PIX = 256
GROUP = 8
IMAGE_TILES = 340
ROWS_FIRST = 256
TAPS = 9

leak_slope = 0.2
learn_rate = 0.03
beta_first = 0.5
beta_second = 0.5
adam_epsilon = 1e-08
weight_decay = 0.0001
norm_epsilon = 1e-06

f32 = jnp.float32
bf16 = jnp.bfloat16
PLANE = ("y", "x", "c")
EVERY = ("z", "y", "x", "c")
VMEM_LIMIT = 60 * 1024 * 1024

NN = (((1,), (0,)), ((), ()))
NT = (((1,), (1,)), ((), ()))
TN = (((0,), (0,)), ((), ()))


def dot(a, b, dims=NN):
    return lax.dot_general(a, b, dims, preferred_element_type=f32)


def call(kernel, out_shape, *args, scratch=(), smem=(), hbm=(), out_hbm=(), us=5, name=None):
    vmem = pl.BlockSpec(memory_space=pltpu.VMEM)
    spaces = {i: pl.BlockSpec(memory_space=pltpu.SMEM) for i in smem}
    spaces.update({i: pl.BlockSpec(memory_space=pl.ANY) for i in hbm})
    single = not isinstance(out_shape, (list, tuple))
    return pl.pallas_call(
        kernel,
        out_shape=out_shape,
        in_specs=[spaces.get(i, vmem) for i in range(len(args))],
        out_specs=vmem
        if single
        else [
            pl.BlockSpec(memory_space=pl.ANY) if i in out_hbm else vmem
            for i in range(len(out_shape))
        ],
        scratch_shapes=list(scratch),
        compiler_params=pltpu.CompilerParams(vmem_limit_bytes=VMEM_LIMIT),
        cost_estimate=pl.CostEstimate(
            flops=int(us * 1e8), bytes_accessed=int(us * 3e5), transcendentals=0
        ),
        name=name,
    )(*args)


def shape(dims, dtype):
    return jax.ShapeDtypeStruct(dims, dtype)


def split_two(x):
    high = x.astype(bf16)
    return high, (x - high.astype(f32)).astype(bf16)


def split_three(x):
    high = x.astype(bf16)
    rest = x - high.astype(f32)
    middle = rest.astype(bf16)
    return high, middle, (rest - middle.astype(f32)).astype(bf16)


def pack_kernel(w_ref, o_ref):
    rows = o_ref.shape[1]
    low_half = lax.broadcasted_iota(jnp.int32, (rows, 128), 1) < 64
    for j in range(4):
        a = w_ref[pl.ds(j, rows, stride=8), :]
        b = w_ref[pl.ds(j + 4, rows, stride=8), :]
        o_ref[2 * j] = jnp.where(low_half, a, pltpu.roll(b, 64, 1)).astype(bf16)
        o_ref[2 * j + 1] = jnp.where(low_half, pltpu.roll(a, 64, 1), b).astype(bf16)


def adam_pieces(rows):
    if rows % 8:
        return [(0, rows)]
    tiles = rows // 8
    cuts = [8 * (tiles * k // 4) for k in range(5)]
    return list(zip(cuts[:-1], cuts[1:]))


def adam_kernel(
    fix_ref, g_hbm, p_hbm, m_hbm, v_hbm, po_hbm, mo_hbm, vo_hbm,
    g_ref, p_ref, m_ref, v_ref, flat, in_sems, out_sems,
):
    pieces = adam_pieces(g_ref.shape[1])
    arrived, leaving = [], []
    for k, (low, high) in enumerate(pieces):
        here, wide = pl.ds(low, high - low), pl.ds(8 * low, 8 * (high - low))
        copies = [pltpu.make_async_copy(g_hbm.at[:, here, :], g_ref.at[:, here, :], in_sems.at[4 * k])]
        for n, (a, b) in enumerate(((p_hbm, p_ref), (m_hbm, m_ref), (v_hbm, v_ref))):
            copies.append(pltpu.make_async_copy(a.at[wide, :], b.at[wide, :], in_sems.at[4 * k + n + 1]))
        for copy in copies:
            copy.start()
        arrived.append(copies)
    for k, (low, high) in enumerate(pieces):
        for copy in arrived[k]:
            copy.wait()
        count = high - low
        half = lax.broadcasted_iota(jnp.int32, (count, 128), 1) < 64
        for j in range(4):
            a, b = g_ref[2 * j, low:high, :], g_ref[2 * j + 1, low:high, :]
            flat[pl.ds(8 * low + j, count, stride=8), :] = jnp.where(half, a, pltpu.roll(b, 64, 1))
            flat[pl.ds(8 * low + j + 4, count, stride=8), :] = jnp.where(half, pltpu.roll(a, 64, 1), b)
        wide = slice(8 * low, 8 * high)
        new, first, second = adamw_update(
            p_ref[wide, :], m_ref[wide, :], v_ref[wide, :], flat[wide, :], fix_ref[0]
        )
        p_ref[wide, :] = new
        m_ref[wide, :] = first
        v_ref[wide, :] = second
        wide = pl.ds(8 * low, 8 * count)
        for n, (a, b) in enumerate(((p_ref, po_hbm), (m_ref, mo_hbm), (v_ref, vo_hbm))):
            copy = pltpu.make_async_copy(a.at[wide, :], b.at[wide, :], out_sems.at[3 * k + n])
            copy.start()
            leaving.append(copy)
    for copy in leaving:
        copy.wait()


def adamw_update(master, first, second, grad, fix):
    first_new = beta_first * first + (1.0 - beta_first) * grad
    second_new = beta_second * second + (1.0 - beta_second) * grad * grad
    update = first_new / fix / (jnp.sqrt(second_new / fix) + adam_epsilon)
    return master - learn_rate * (update + weight_decay * master), first_new, second_new


SLOT_MASK = tuple(((m >> 1) & 1) * 4 + (m & 1) * 2 + (m >> 2) for m in range(GROUP))
SLOT_FIRST = tuple(2 * (m & 1) + ((m >> 1) & 1) for m in range(4))
SLOT_SECOND = tuple(4 + m for m in range(4))
NOISE_MASK = tuple((m & 1) * 4 + ((m >> 1) & 1) * 2 + (m >> 2) for m in range(GROUP))


def pre_kernel(me_ref, noise_ref, w_ref, pre_ref, hid_ref):
    for m in range(GROUP):
        rows = pl.ds(pl.multiple_of((me_ref[0] ^ NOISE_MASK[m]) * PIX, PIX), PIX)
        pre = dot(noise_ref[m], w_ref[...], TN)
        pre_ref[rows, :] = pre
        hid_ref[rows, :] = (pre * jax.nn.sigmoid(pre)).astype(bf16)


def turn_kernel(near_ref, far_ref, o_ref):
    for m in range(GROUP):
        source = near_ref if m < 4 else far_ref
        for part, at in enumerate((SLOT_FIRST[m % 4], SLOT_SECOND[m % 4])):
            o_ref[128 * m : 128 * m + 128, 1024 * part : 1024 * part + 1024] = jnp.transpose(
                source[at]
            )


def share_kernel(me_ref, *refs):
    blocks, out, four, sem = refs[:-3], refs[-3], refs[-2], refs[-1]
    rows = out.shape[2]
    tail = pl.ds(blocks[0].shape[0] - rows, rows)
    for here in range(4):

        @pl.when(me_ref[1] == here)
        def _():
            for k in range(4):
                pltpu.make_async_copy(blocks[3 + k - here].at[tail, :], four.at[k], sem).start()

    pltpu.make_async_copy(four, four, sem).wait()
    for q in range(GROUP):
        out[q] = four[...]


def pixel_column():
    return lax.broadcasted_iota(jnp.int32, (PIX, 128), 0) & 15


def from_left(x, column):
    return jnp.where(column > 0, pltpu.roll(x, 1, 0), 0.0)


def from_right(x, column):
    return jnp.where(column < 15, pltpu.roll(x, PIX - 1, 0), 0.0)


def from_above(x):
    return jnp.concatenate([jnp.zeros((16, x.shape[1]), x.dtype), x[:-16]], axis=0)


def from_below(x):
    return jnp.concatenate([x[16:], jnp.zeros((16, x.shape[1]), x.dtype)], axis=0)


def block_row(tap, q, half):
    return ROWS_FIRST + tap * GIN + half * GOUT + q * 64


def forward_kernel(*refs):
    me_ref, near_hbm, far_hbm, color_ref = refs[:4]
    factor_hbm, gated_hbm, rgb_ref, wide_hbm = refs[-13:-9]
    parts, w_ref, sem, near_ref, far_ref, factor_ref, gated_ref, wide, sems = refs[-9:]
    blocks = refs[4:-13]
    near_copy = pltpu.make_async_copy(near_hbm, near_ref, sems.at[0])
    far_copy = pltpu.make_async_copy(far_hbm, far_ref, sems.at[1])
    chunk = w_ref.shape[0] // 4
    if len(blocks) == 1:
        copy = pltpu.make_async_copy(blocks[0], w_ref, sem)
        copy.start()
        near_copy.start()
        far_copy.start()
        copy.wait()
    else:
        for here in range(4):

            @pl.when(me_ref[1] == here)
            def _():
                for k in range(4):
                    pltpu.make_async_copy(
                        blocks[3 + k - here].at[pl.ds(0, chunk), :],
                        w_ref.at[pl.ds(k * chunk, chunk), :],
                        sem,
                    ).start()

        near_copy.start()
        far_copy.start()
        pltpu.make_async_copy(w_ref, w_ref, sem).wait()
    for m in range(GROUP):
        q = me_ref[0] ^ SLOT_MASK[m]
        for tap in range(TAPS):
            for half in range(2):
                at = m * 128 + half * 64
                row = pl.multiple_of(block_row(tap, q, half), 64)
                wide[at : at + 64, 128 * tap : 128 * tap + 128] = w_ref[pl.ds(row, 64), :]
    wide[:, 128 * TAPS :] = jnp.zeros((GIN, 128), bf16)
    wide_copy = pltpu.make_async_copy(wide, wide_hbm, sems.at[2])
    wide_copy.start()
    near_copy.wait()
    far_copy.wait()

    def outgoing(b):
        rows = pl.ds(pl.multiple_of(b * PIX, PIX), PIX)
        return (
            pltpu.make_async_copy(
                factor_ref.at[:, rows, :], factor_hbm.at[:, rows, :], sems.at[3 + b]
            ),
            pltpu.make_async_copy(
                gated_ref.at[:, rows, :], gated_hbm.at[:, rows, :], sems.at[3 + GROUP + b]
            ),
        )

    low_half = lax.broadcasted_iota(jnp.int32, (PIX, 128), 1) < 64
    column = pixel_column()
    color_high, color_low = split_two(color_ref[...])
    color = jnp.concatenate([color_high, color_low], axis=0)

    @pl.loop(0, 4)
    def _(pair):
        start = pl.multiple_of(pair * 512, 512)
        local = pl.multiple_of((pair & 1) * 512, 512)
        first = pair < 2
        left = []
        for m in range(GROUP):
            at = jnp.where(first, SLOT_FIRST[m % 4], SLOT_SECOND[m % 4])
            left.append((near_ref if m < 4 else far_ref)[at, pl.ds(local, 512), :])
        left = jnp.concatenate(left, axis=1)
        for k in range(5):
            y = dot(left, wide[:, 256 * k : 256 * k + 256])
            parts[2 * k] = y[:, :128]
            if k < 4:
                parts[2 * k + 1] = y[:, 128:]
        for one in range(2):
            rows = pl.ds(pl.multiple_of(start + one * PIX, PIX), PIX)
            here = slice(one * PIX, one * PIX + PIX)
            cols = []
            for a in range(3):
                y0, y1, y2 = (parts[3 * a + b, here, :] for b in range(3))
                cols.append((from_left(y0, column) + (y1 + y2), (y0 + y1) + from_right(y2, column)))
            for pi in range(2):
                gated = []
                for pj in range(2):
                    if pi == 0:
                        mixed = from_above(cols[0][pj]) + (cols[1][pj] + cols[2][pj])
                    else:
                        mixed = (cols[0][pj] + cols[1][pj]) + from_below(cols[2][pj])
                    turned = pltpu.roll(mixed, 64, 1)
                    gate = jax.nn.sigmoid(jnp.where(low_half, turned, mixed))
                    value = jnp.where(low_half, mixed, turned)
                    gated.append(value * gate)
                    factor_ref[2 * pi + pj, rows, :] = jnp.where(
                        low_half, gate, gated[-1] * (1.0 - gate)
                    )
                both = jnp.where(low_half, gated[0], gated[1])
                gated_ref[pi, rows, :] = both
                high, low = split_two(both)
                rgb = dot(color, jnp.concatenate([high, low], axis=1), NT)
                rgb_ref[2 * pair + one, 16 * pi : 16 * pi + 16, :] = rgb[:16] + rgb[16:]
            for copy in outgoing(2 * pair + one):
                copy.start()

    @pl.loop(0, GROUP)
    def _(b):
        for copy in outgoing(b):
            copy.wait()

    wide_copy.wait()


def tap_sums(parts, column):
    sums = []
    for a in range(3):
        line = []
        for pj in range(2):
            even, odd = parts[pj], parts[2 + pj]
            if a == 0:
                line.append(odd + from_below(even))
            elif a == 1:
                line.append(even + odd)
            else:
                line.append(from_above(odd) + even)
        sums.append(line[1] + from_right(line[0], column))
        sums.append(line[0] + line[1])
        sums.append(from_left(line[1], column) + line[0])
    return sums


def weight_grad_kernel(
    me_ref, dt_ref, factor_hbm, hid_hbm, color_ref, g_hbm, dm_hbm, last_hbm, first_hbm,
    moved, factor_ref, hid_ref, g_ref, dm_ref, in_sems, dm_sems, out_sems,
):
    column = pixel_column()

    def piece(b):
        return pl.ds(pl.multiple_of(b * PIX, PIX), PIX)

    def factor_copy(b):
        return pltpu.make_async_copy(
            factor_hbm.at[:, piece(b), :], factor_ref.at[:, piece(b), :], in_sems.at[b]
        )

    def dm_copy(b):
        return pltpu.make_async_copy(
            dm_ref.at[:, piece(b), :], dm_hbm.at[:, piece(b), :], dm_sems.at[b]
        )

    def taps_copy(a):
        start = 0 if a == 0 else ROWS_FIRST + 3 * a * GIN
        at = pl.ds(start, ROWS_FIRST + 3 * (a + 1) * GIN - start)
        return pltpu.make_async_copy(g_ref.at[at, :], g_hbm.at[at, :], out_sems.at[a])

    chunk = last_hbm.shape[0]
    low = pl.ds(0, chunk)
    high = pl.ds(g_ref.shape[0] - chunk, chunk)
    first_copy = pltpu.make_async_copy(g_ref.at[low, :], first_hbm, out_sems.at[3])
    last_copy = pltpu.make_async_copy(g_ref.at[high, :], last_hbm, out_sems.at[4])
    for b in range(GROUP):
        factor_copy(b).start()
    hid_copy = pltpu.make_async_copy(hid_hbm, hid_ref, in_sems.at[GROUP])
    hid_copy.start()
    g_ref[:ROWS_FIRST, :] = jnp.zeros((ROWS_FIRST, 128), f32)
    c_high, c_middle, c_low = (x.astype(f32) for x in split_three(color_ref[...]))
    colors = jnp.concatenate([c_high, c_middle, c_low, c_high, c_middle, c_high], axis=0)
    colors = colors.astype(bf16)

    @pl.loop(0, GROUP)
    def _(b):
        rows = piece(b)
        factor_copy(b).wait()
        for phase in range(4):
            pi, pj = phase // 2, phase % 2
            high, middle, low = (
                x.astype(f32) for x in split_three(dt_ref[b, 8 * phase : 8 * phase + 8, :])
            )
            left = jnp.concatenate([high, high, high, middle, middle, low], axis=0).astype(bf16)
            spread = dot(left, colors, TN)
            low = (spread * factor_ref[phase, rows, :]).astype(bf16)
            dm_ref[phase, rows, :] = low
            plain = low.astype(f32)
            side = (from_right if pj == 0 else from_left)(plain, column)
            lanes = slice(128 * pj, 128 * pj + 128)
            for k, value in enumerate((plain, side)):
                line = (from_below if pi == 0 else from_above)(value)
                moved[4 * pi + k, rows, lanes] = value.astype(bf16)
                moved[4 * pi + 2 + k, rows, lanes] = line.astype(bf16)
        dm_copy(b).start()

    hid_copy.wait()

    def column_sums(at):
        plain = dot(hid_ref[...], moved[at])
        side = dot(hid_ref[...], moved[at + 1])
        return (
            plain[:, 128:] + side[:, :128],
            plain[:, :128] + plain[:, 128:],
            side[:, 128:] + plain[:, :128],
        )

    def put(tap, value, add):
        for m in range(GROUP):
            for half in range(2):
                q = me_ref[0] ^ SLOT_MASK[m]
                at = pl.ds(pl.multiple_of(block_row(tap, q, half), 64), 64)
                piece = value[128 * m + 64 * half : 128 * m + 64 * half + 64]
                g_ref[at, :] = g_ref[at, :] + piece if add else piece

    for at, takes in ((0, ((1, False), (2, False))), (4, ((0, False), (1, True)))):
        for b, value in enumerate(column_sums(at)):
            for a, add in takes:
                put(3 * a + b, value, add)
    taps_copy(1).start()
    for at, a in ((2, 0), (6, 2)):
        for b, value in enumerate(column_sums(at)):
            put(3 * a + b, value, True)
        (first_copy if a == 0 else last_copy).start()
        taps_copy(a).start()
    for a in range(3):
        taps_copy(a).wait()
    first_copy.wait()
    last_copy.wait()

    @pl.loop(0, GROUP)
    def _(b):
        dm_copy(b).wait()


def hidden_grad_kernel(
    dm_ref, wide_ref, dt_ref, gated_ref, keep_ref, send_ref, rgb_ref, sums, color
):
    column = pixel_column()
    color[...] = jnp.zeros_like(color)

    @pl.loop(0, GROUP)
    def _(b):
        rows = pl.ds(pl.multiple_of(b * PIX, PIX), PIX)
        parts = [dm_ref[phase, rows, :].astype(f32) for phase in range(4)]
        for tap, total in enumerate(tap_sums(parts, column)):
            high, low = split_two(total)
            sums[:PIX, 128 * tap : 128 * tap + 128] = high
            sums[PIX:, 128 * tap : 128 * tap + 128] = low
        for k in range(4):
            out = dot(sums[...], wide_ref[256 * k : 256 * k + 256, : 128 * TAPS], NT)
            out = out[:PIX] + out[PIX:]
            put = keep_ref if k < 2 else send_ref
            put[2 * (k % 2), rows, :] = out[:, :128]
            put[2 * (k % 2) + 1, rows, :] = out[:, 128:]
        for pi in range(2):
            high, low = split_two(dt_ref[b, 16 * pi : 16 * pi + 16, :])
            g_high, g_low = split_two(gated_ref[pi, rows, :])
            left = jnp.concatenate([high, low], axis=0)
            out = dot(left, jnp.concatenate([g_high, g_low], axis=1))
            color[...] += out[:16, :128] + (out[:16, 128:] + out[16:, :128])

    low_half = lax.broadcasted_iota(jnp.int32, (8, 128), 1) < 64
    folded = color[:8, :] + pltpu.roll(color[8:, :], 64, 1)
    rgb_ref[...] = jnp.where(low_half, folded, 0.0)


def first_grad_kernel(me_ref, dh_ref, pre_ref, noise_ref, o_ref):
    o_ref[...] = jnp.zeros_like(o_ref)
    for m in range(GROUP):
        rows = pl.ds(pl.multiple_of((me_ref[0] ^ NOISE_MASK[m]) * PIX, PIX), PIX)
        pre = pre_ref[rows, :]
        gate = jax.nn.sigmoid(pre)
        slope = gate * (1.0 + pre * (1.0 - gate))
        o_ref[...] += dot(noise_ref[m], (slope * dh_ref[rows, :]).astype(bf16))


def row_normalized(row):
    return row * lax.rsqrt(jnp.sum(row * row, axis=1, keepdims=True) + norm_epsilon)


def row_times(row, matrix, dims):
    pieces = jnp.concatenate(
        [jnp.broadcast_to(x.astype(f32), (8, row.shape[1])) for x in split_three(row)], axis=0
    ).astype(bf16)
    out = dot(pieces, matrix, dims)
    return out[0:1] + out[8:9] + out[16:17]


INS = (3,) + CS[:3]
CRIT_AT = (0, 4096, 20480, 86016)


def window(length):
    rows = length // 128 if length % 128 == 0 else -(-(127 + length) // 128)
    return -(-rows // 8) * 8


def prepare_kernel(
    crit_length, frozen_length, small_ref, own_ref, u_ref,
    e1, e2, e3, e4, r1, r2, r3, r4, m1, m2, m3, m4, c1, c2, c3, c4,
    left_ref, sigma_ref, share_ref, crit, frozen, moved, rows_buf,
):
    devices = GROUP * small_ref.shape[1]
    crit_rows, frozen_rows = window(crit_length), window(frozen_length)
    crit[...] = jnp.zeros_like(crit)
    frozen[...] = jnp.zeros_like(frozen)
    live = jnp.zeros((1, 128), f32)
    for k in range(devices):
        block = small_ref[k % GROUP, k // GROUP].astype(f32)
        at = pl.ds((k * crit_length) // 128, crit_rows)
        crit[at, :] += block[:crit_rows]
        at = pl.ds((k * frozen_length) // 128, frozen_rows)
        frozen[at, :] += block[crit_rows : crit_rows + frozen_rows]
        live += block[crit_rows + frozen_rows : crit_rows + frozen_rows + 1]
    lane = lax.broadcasted_iota(jnp.int32, (1, 128), 1)
    real = jnp.sum(jnp.where((lane > 0) & (lane < SLOTS), live, 0.0), axis=1, keepdims=True)
    count = jnp.where(lane == 0, live, real) * float(IMAGE_TILES)
    share_ref[...] = jnp.broadcast_to(own_ref[...] / jnp.maximum(count, 1.0), share_ref.shape)

    def lanes_of(x):
        return lax.broadcasted_iota(jnp.int32, x.shape, 1)

    def shifted(a, b, lane_at):
        if lane_at == 0:
            return a
        turn = 128 - lane_at
        return jnp.where(lanes_of(a) < turn, pltpu.roll(a, turn, 1), pltpu.roll(b, turn, 1))

    def halves(x):
        low = lanes_of(x) < 64
        return jnp.where(low, x, 0.0), jnp.where(low, pltpu.roll(x, 64, 1), 0.0)

    def flush(ref, rows):
        ref[...] = rows_buf[: ref.shape[0], :].astype(bf16)
        rows_buf[:rows, :] = jnp.zeros((rows, 128), f32)

    total = frozen.shape[0] - 8
    moved[...] = shifted(frozen[:total, :], frozen[1 : total + 1, :], 8)
    rows_buf[...] = jnp.zeros_like(rows_buf)
    for ref, offset, rows, width in ((e1, 0, INS[0], CS[0]), (e2, 72, INS[1], CS[1])):
        for r in range(rows):
            a, lane_at = divmod(offset + r * width, 128)
            row = shifted(frozen[a : a + 1, :], frozen[a + 1 : a + 2, :], lane_at)
            rows_buf[r : r + 1, :] = jnp.where(lane < width, row, 0.0)
        flush(ref, 32)
    for i in range(8):
        a, lane_at = divmod(112 * i, 128)
        row = shifted(
            moved[pl.ds(8 + a, 5, stride=7), :], moved[pl.ds(9 + a, 5, stride=7), :], lane_at
        )
        rows_buf[pl.ds(i, 5, stride=8), :] = jnp.where(lanes_of(row) < 112, row, 0.0)
    flush(e3, 40)
    five = [moved[pl.ds(43 + k, 56, stride=5), :] for k in range(5)]
    pairs = (
        (five[0], shifted(five[2], five[3], 64)),
        (five[1], shifted(five[3], five[4], 64)),
        (halves(five[2])[0], halves(five[4])[1]),
    )
    e4[...] = jnp.zeros_like(e4)
    for b, (even, odd) in enumerate(pairs):
        rows_buf[pl.ds(0, 56, stride=2), :] = even
        rows_buf[pl.ds(1, 56, stride=2), :] = odd
        e4[:112, 128 * b : 128 * b + 128] = rows_buf[:112, :].astype(bf16)
    rows_buf[...] = jnp.zeros_like(rows_buf)
    even, odd = halves(moved[323:335, :])
    rows_buf[pl.ds(0, 12, stride=2), :] = even
    rows_buf[pl.ds(1, 12, stride=2), :] = odd
    flush(r1, 24)
    rows_buf[:40, :] = moved[335:375, :]
    flush(r2, 40)
    r3[...] = jnp.zeros_like(r3)
    r4[...] = jnp.zeros_like(r4)
    for b in range(2):
        r3[:112, 128 * b : 128 * b + 128] = moved[pl.ds(375 + b, 112, stride=2), :].astype(bf16)
    for b in range(4):
        r4[:320, 128 * b : 128 * b + 128] = moved[pl.ds(599 + b, 320, stride=4), :].astype(bf16)
    even, odd = halves(crit[:32, :])
    rows_buf[pl.ds(0, 32, stride=2), :] = even
    rows_buf[pl.ds(1, 32, stride=2), :] = odd
    flush(m1, 64)
    m2[...] = crit[32:160, :].astype(bf16)
    for b in range(2):
        m3[:, 128 * b : 128 * b + 128] = crit[pl.ds(160 + b, 256, stride=2), :].astype(bf16)
    for b in range(4):
        m4[:, 128 * b : 128 * b + 128] = crit[pl.ds(672 + b, 512, stride=4), :].astype(bf16)

    left_ref[...] = jnp.zeros_like(left_ref)
    sigma_ref[...] = jnp.ones_like(sigma_ref)
    for k, (m_ref, c_ref) in enumerate(((m1, c1), (m2, c2), (m3, c3), (m4, c4))):
        width = KP[k]
        matrix = m_ref[...]
        right = row_normalized(row_times(u_ref[k : k + 1, :width], matrix, NT))
        turned = row_times(right, matrix, NN)
        left = row_normalized(turned)
        left_ref[k : k + 1, :width] = left
        sigma = jnp.sum(left * turned, axis=1, keepdims=True)
        sigma_ref[k : k + 1, :] = jnp.broadcast_to(sigma, (1, 128))
        c_ref[...] = jnp.transpose(jnp.broadcast_to(right, (128, width)))


def wanted_code(scal_ref, slot):
    d = lax.broadcasted_iota(jnp.int32, (1, 1024), 1)

    def bit(k):
        return (d >> k) & 1

    i = bit(9) + 2 * bit(7) + 4 * bit(5) + 8 * bit(3) + 16 * bit(1)
    j = bit(8) + 2 * bit(6) + 4 * bit(4) + 8 * bit(2) + 16 * bit(0)
    down, across, flip, top, side = (scal_ref[slot, k] for k in range(5))
    row = i - down
    moved = j - across
    fine = (row >= 0) & (row < S) & (moved >= 0) & (moved < S)
    source = jnp.where(flip == 1, S - 1 - moved, moved)
    boxed = (i >= top) & (i < top + S // 2) & (j >= side) & (j < side + S // 2)
    return jnp.where(fine & jnp.logical_not(boxed), row * S + source, -1)


def three(x):
    return jnp.concatenate([v.astype(f32) for v in split_three(x)], axis=0).astype(bf16)


def fold(x):
    return x[0:8] + x[8:16] + x[16:24]


def fill_pick(pick, scal_ref, slot, phases):
    want = wanted_code(scal_ref, slot)

    @pl.loop(0, 8)
    def _(k):
        s = lax.broadcasted_iota(jnp.int32, (128, 1024), 0) + k * 128
        if phases:
            at = s & 255
            s = (2 * (at >> 4) + (s >> 9)) * S + 2 * (at & 15) + ((s >> 8) & 1)
        hit = jnp.where(s == want, 1.0, 0.0).astype(bf16)
        pick[pl.ds(pl.multiple_of(k * 128, 128), 128), :] = hit


def augmented(image, pick):
    seen = fold(dot(three(image), pick[...]))
    small = 0.25 * ((seen[:, :256] + seen[:, 256:512]) + (seen[:, 512:768] + seen[:, 768:]))
    return jnp.transpose(small).astype(bf16)


def last_pool(slots):
    row = lax.broadcasted_iota(jnp.int32, (16, 16 * slots), 0)
    col = lax.broadcasted_iota(jnp.int32, (16, 16 * slots), 1)
    pool = jnp.where((row // 4 == col // 16) & (row % 4 == col % 4), 0.25, 0.0)
    return jnp.concatenate([pool.astype(bf16)] * 3, axis=1)


def critic_levels(inputs, slots, extract, project, matrices, head_ref, sigma_ref):
    levels = []
    pool = last_pool(slots)
    for k in range(4):
        count = 16 if k == 3 else (slots * PIX) >> (2 * k)
        width = KP[k]
        pre = dot(inputs, extract[k][...])
        active = pre * jax.nn.sigmoid(pre)
        feat = dot(active.astype(bf16), project[k][...]).astype(bf16)
        raw = dot(feat, matrices[k][...])
        sigma = sigma_ref[k : k + 1, 0:1]
        scaled = raw / sigma
        slope = jnp.where(scaled >= 0, 1.0, leak_slope)
        leaky = scaled * slope
        head = head_ref[k : k + 1, :width]
        scale = lax.rsqrt(jnp.sum(head * head, axis=1, keepdims=True) + norm_epsilon)
        unit = head * scale
        logit = jnp.sum(leaky * unit, axis=1, keepdims=True)
        levels.append((pre, feat, raw, sigma, slope, leaky, head, scale, unit, logit))
        if k < 2:
            blocks = active.reshape(slots, 4, count // (4 * slots), CP[k])
            total = (blocks[:, 0] + blocks[:, 1]) + (blocks[:, 2] + blocks[:, 3])
            inputs = (0.25 * total).reshape(count // 4, CP[k]).astype(bf16)
        elif k == 2:
            inputs = dot(pool, three(active)).astype(bf16)
    return levels


def image_grad_kernel(
    scal_ref,
    share_ref,
    got_ref,
    head_ref,
    sigma_ref,
    e1, e2, e3, e4,
    r1, r2, r3, r4,
    m1, m2, m3, m4,
    dt_ref,
    map_ref,
    pick,
):
    extract, project, matrices = (e1, e2, e3, e4), (r1, r2, r3, r4), (m1, m2, m3, m4)
    fill_pick(pick, scal_ref, 0, True)
    color = got_ref[0]
    for k in range(1, GROUP):
        color = color + got_ref[k]
    color = jnp.tanh(color)
    fake = jnp.concatenate([color[8 * k : 8 * k + 8] for k in range(4)], axis=1)
    first_map = augmented(fake, pick)
    map_ref[...] = first_map
    levels = critic_levels(first_map, 1, extract, project, matrices, head_ref, sigma_ref)
    row = lax.broadcasted_iota(jnp.int32, (16, 16), 0)
    col = lax.broadcasted_iota(jnp.int32, (16, 16), 1)
    spread = jnp.where((col < 4) & (row % 4 == col), 0.25, 0.0)
    spread = jnp.concatenate([spread.astype(bf16)] * 3, axis=1)
    carry = None
    for k in (3, 2, 1, 0):
        pre, feat, raw, sigma, slope, leaky, head, scale, unit, logit = levels[k]
        dlogit = -share_ref[0:1, 0:1] * jax.nn.sigmoid(-logit)
        if k == 3:
            dlogit = jnp.where(lax.broadcasted_iota(jnp.int32, (16, 1), 0) < 4, dlogit, 0.0)
        dscaled = dlogit * unit * slope
        dfeat = dot((dscaled / sigma).astype(bf16), matrices[k][...], NT).astype(bf16)
        dactive = dot(dfeat, project[k][...], NT)
        if carry is not None:
            dactive = dactive + carry
        gate = jax.nn.sigmoid(pre)
        dpre = (gate * (1.0 + pre * (1.0 - gate)) * dactive).astype(bf16)
        dinput = dot(dpre, extract[k][...], NT)
        if k == 3:
            carry = dot(spread, three(dinput))
        elif k > 0:
            carry = jnp.concatenate([0.25 * dinput] * 4, axis=0)
    daug = 0.25 * jnp.transpose(dinput)
    daug = jnp.concatenate([daug] * 4, axis=1)
    dimage = fold(dot(three(daug), pick[...], NT))
    dtanh = dimage * (1.0 - fake * fake)
    for q in range(GROUP):
        for k in range(4):
            dt_ref[q, 8 * k : 8 * k + 8, :] = dtanh[:, 256 * k : 256 * k + 256]


def critic_kernel(
    scal_ref,
    share_ref,
    map_ref,
    real_ref,
    head_ref,
    left_ref,
    sigma_ref,
    e1, e2, e3, e4,
    r1, r2, r3, r4,
    m1, m2, m3, m4,
    c1, c2, c3, c4,
    color_ref,
    sent_ref,
    pick,
    first_map,
    corner,
    out_ref,
    flat_ref,
):
    extract, project = (e1, e2, e3, e4), (r1, r2, r3, r4)
    matrices, columns = (m1, m2, m3, m4), (c1, c2, c3, c4)
    first_map[:PIX, :] = map_ref[...]
    for slot in range(1, SLOTS):
        fill_pick(pick, scal_ref, slot, False)
        first_map[slot * PIX : slot * PIX + PIX, :] = augmented(real_ref[slot - 1], pick)
    levels = critic_levels(first_map[...], SLOTS, extract, project, matrices, head_ref, sigma_ref)
    loss_gen = jnp.zeros((1, 1), f32)
    loss_critic = jnp.zeros((1, 1), f32)
    out_ref[...] = jnp.zeros_like(out_ref)
    for k in range(4):
        pre, feat, raw, sigma, slope, leaky, head, scale, unit, logit = levels[k]
        count, width = logit.shape[0], KP[k]
        slot = lax.broadcasted_iota(jnp.int32, (count, 1), 0) // (count // SLOTS)
        share = share_ref[0:1, 0:1]
        for other in range(1, SLOTS):
            share = jnp.where(slot == other, share_ref[0:1, other : other + 1], share)
        sign = jnp.where(slot == 0, -1.0, 1.0)
        hinge = 1.0 - sign * logit
        loss_critic += jnp.sum(share * jnp.maximum(hinge, 0.0), axis=0, keepdims=True)
        dlogit = jnp.where(hinge > 0, -sign * share, 0.0)
        soft = jnp.maximum(-logit, 0.0) + jnp.log1p(jnp.exp(-jnp.abs(logit)))
        loss_gen += jnp.sum(jnp.where(slot == 0, share * soft, 0.0), axis=0, keepdims=True)
        dscaled = dlogit * unit * slope
        grad = dot(feat, (dscaled / sigma).astype(bf16), TN)
        dsigma = jnp.sum(jnp.sum(dscaled * raw, axis=1, keepdims=True), axis=0, keepdims=True)
        dsigma = -dsigma / (sigma * sigma)
        side = columns[k][...] * dsigma
        for b in range(width // 128):
            lanes = slice(128 * b, 128 * b + 128)
            piece = grad[:, lanes] + side * left_ref[k : k + 1, lanes]
            if k == 0:
                corner[...] = piece
                low = lax.broadcasted_iota(jnp.int32, (32, 128), 1) < 64
                even, odd = corner[pl.ds(0, 32, stride=2), :], corner[pl.ds(1, 32, stride=2), :]
                flat_ref[:32, :] = jnp.where(low, even, pltpu.roll(odd, 64, 1))
            else:
                stride = width // 128
                flat_ref[pl.ds(CRIT_AT[k] // 128 + b, width, stride=stride), :] = piece
        dunit = jnp.sum(leaky * dlogit, axis=0, keepdims=True)
        inner = jnp.sum(head * dunit, axis=1, keepdims=True)
        out_ref[k : k + 1, :width] = scale * dunit - head * (scale * scale * scale * inner)
    out_ref[4:5, 0:128] = jnp.broadcast_to(loss_gen, (1, 128))
    out_ref[4:5, 128:256] = jnp.broadcast_to(loss_critic, (1, 128))
    rows = sent_ref.shape[1] - 40
    if sent_ref.shape[0] == GROUP:
        groups = rows // 85
        for q in range(GROUP):
            for z in range(groups):
                at = (z * GROUP + q) * 85
                sent_ref[q, z * 85 : z * 85 + 85, :] = flat_ref[at : at + 85, :]
            sent_ref[q, groups * 85 : rows, :] = jnp.zeros((rows - groups * 85, 128), f32)
    else:
        sent_ref[0, :rows, :] = flat_ref[...]
    for q in range(sent_ref.shape[0]):
        for k in range(8):
            for b in range(4):
                at = rows + 4 * k + b
                sent_ref[q, at : at + 1, :] = out_ref[k : k + 1, 128 * b : 128 * b + 128]
        sent_ref[q, rows + 32 :, :] = color_ref[...]


def local(
    groups,
    noise_maps,
    dataset_lowres_images,
    dataset_highres_images,
    occupied_mask,
    shift_amounts,
    mirror_indicator,
    erase_box_corner,
    update_ordinal,
    fixed_backbone_params,
    singular_estimate_dirs,
    maker_weight_arrays,
    maker_mean_estimate,
    maker_variance_estimate,
    judge_weight_arrays,
    judge_mean_estimate,
    judge_variance_estimate,
    output_weight_rows,
    output_mean_estimate,
    output_variance_estimate,
):
    devices = groups * GROUP
    rows = maker_weight_arrays.shape[0] // 1024
    chunk = GROUP * rows
    z = lax.axis_index("z")
    q = (lax.axis_index("y") * 2 + lax.axis_index("x")) * 2 + lax.axis_index("c")
    me = jnp.stack([q, z]).astype(jnp.int32)

    def pad_rows(x):
        return jnp.pad(x, ((0, 0), (0, -x.shape[1] % 1024))).reshape(x.shape[0], -1, 128)

    def swap(x, axis):
        return lax.ppermute(x, axis, [(0, 1), (1, 0)])

    crit_length = judge_weight_arrays.shape[0]
    frozen_length = fixed_backbone_params.shape[0]
    member = z * GROUP + q

    def windowed(x):
        length = x.shape[0]
        rows_here = window(length)
        if length % 128 == 0:
            return jnp.pad(x.reshape(-1, 128), ((0, rows_here - length // 128), (0, 0)))
        empty = jnp.zeros((rows_here * 128,), bf16)
        start = lax.rem(member * length, 128)
        return lax.dynamic_update_slice(empty, x, (start,)).reshape(rows_here, 128)

    own = occupied_mask.astype(f32)
    small = jnp.concatenate(
        [
            windowed(judge_weight_arrays.astype(bf16)),
            windowed(fixed_backbone_params),
            jnp.pad(own.astype(bf16), ((0, 7), (0, 128 - SLOTS))),
        ]
    )

    def rows_of(flat):
        out, offset = [], 0
        for k in range(4):
            out.append(jnp.pad(flat[offset : offset + KS[k]], (0, 512 - KS[k])))
            offset += KS[k]
        return jnp.pad(jnp.stack(out), ((0, 4), (0, 0)))

    head_rows = rows_of(output_weight_rows)
    start_rows = rows_of(singular_estimate_dirs)
    own_row = jnp.pad(own, ((0, 0), (0, 128 - SLOTS)))
    color_all = output_weight_rows[960:].reshape(GOUT, 3)
    color = jnp.pad(lax.dynamic_slice(color_all, (q * 64, 0), (64, 3)).T, ((0, 5), (0, 0)))
    none = jnp.zeros_like(color)
    color_left = jnp.concatenate(
        [
            jnp.concatenate([color, none, color, none], axis=1),
            jnp.concatenate([none, color, none, color], axis=1),
        ],
        axis=0,
    )
    color_twice = jnp.concatenate([color, color], axis=1)
    small_images = dataset_lowres_images.astype(f32)
    large = dataset_highres_images.astype(f32).reshape(1, 3, S, 2, S, 2)
    large = jnp.mean(large, axis=(3, 5)).reshape(1, 3, S * S)
    reals = jnp.pad(jnp.concatenate([small_images, large]), ((0, 0), (0, 5), (0, 0)))
    scalars = jnp.concatenate(
        [shift_amounts[0], mirror_indicator[0][:, None], erase_box_corner[0]], axis=1
    )

    noise_all = jnp.concatenate([noise_maps, swap(noise_maps, "y")])

    packed = call(
        pack_kernel,
        shape((GROUP, rows, 128), bf16),
        maker_weight_arrays.reshape(8 * rows, 128),
        us=3,
        name="pack",
    )
    slices = lax.all_to_all(packed, PLANE, 0, 0, tiled=True).reshape(chunk, 128)
    slices, noise_all = lax.optimization_barrier((slices, noise_all))
    for axis in ("x", "c"):
        noise_all = jnp.concatenate([noise_all, swap(noise_all, axis)])
    first_block = slices[:ROWS_FIRST]

    def hop(x, y):
        down = lax.ppermute(x, "z", [(0, 1), (1, 2), (2, 3)])
        return down, lax.ppermute(y, "z", [(1, 0), (2, 1), (3, 2)])

    if groups == 4:
        sent = [lax.ppermute(first_block, "z", [(0, k)]) for k in (1, 2, 3)]
        riding = jnp.concatenate([slices, small])
        hop_one = hop(riding, riding)
        ready = (head_rows, start_rows, own_row, color_left, color_twice, reals, scalars, me)
        sent, hop_one, ready = lax.optimization_barrier((sent, hop_one, ready))
        head_rows, start_rows, own_row, color_left, color_twice, reals, scalars, me = ready
        first_weights = jnp.where(z == 0, first_block, sent[0] + sent[1] + sent[2])
        hop_two = hop(*hop_one)
    else:
        first_weights = lax.all_gather(first_block, "z", axis=0)[0]
        blocks = [lax.all_gather(slices, "z", axis=0, tiled=True)]

    pixels = GROUP * PIX
    pre, hid = call(
        pre_kernel,
        [shape((pixels, 128), f32), shape((pixels, 128), bf16)],
        me,
        noise_all,
        first_weights,
        smem=(0,),
        us=4,
        name="pre",
    )
    first, second = hid[: pixels // 2], hid[pixels // 2 :]
    first = jnp.stack([first, swap(first, "y")])
    second = jnp.stack([second, swap(second, "x")])
    if groups == 4:
        first, second, hop_two = lax.optimization_barrier((first, second, hop_two))
        hop_three = hop(*hop_two)
    first = jnp.concatenate([first, swap(first, "x")])
    second = jnp.concatenate([second, swap(second, "y")])
    if groups == 4:
        first, second, hop_three = lax.optimization_barrier((first, second, hop_three))
        blocks = [hop_three[0], hop_two[0], hop_one[0], riding, hop_one[1], hop_two[1], hop_three[1]]
        (small,) = call(
            share_kernel,
            [shape((GROUP, 4) + small.shape, bf16)],
            me,
            *blocks,
            smem=(0,),
            hbm=range(1, 8),
            scratch=[pltpu.VMEM((4,) + small.shape, bf16), pltpu.SemaphoreType.DMA],
            us=3,
            name="share",
        )
    else:
        small = lax.all_gather(small, "z", axis=0)
        small = jnp.broadcast_to(small, (GROUP,) + small.shape)
    near = jnp.concatenate([first, second])
    far = swap(near, "c")
    near, far, small = lax.optimization_barrier((near, far, small))
    small = lax.all_to_all(small, PLANE, 0, 0, tiled=True)
    factor, gated, rgb, wide = call(
        forward_kernel,
        [
            shape((4, pixels, 128), f32),
            shape((2, pixels, 128), f32),
            shape((GROUP, 32, PIX), f32),
            shape((GIN, 1280), bf16),
        ],
        me,
        near,
        far,
        color_left,
        *blocks,
        smem=(0,),
        hbm=(1, 2, *range(4, 4 + len(blocks))),
        out_hbm=(0, 1, 3),
        scratch=[
            pltpu.VMEM((TAPS + 1, 512, 128), f32),
            pltpu.VMEM((groups * chunk, 128), bf16),
            pltpu.SemaphoreType.DMA,
            pltpu.VMEM((GROUP, pixels // 2, 128), bf16),
            pltpu.VMEM((GROUP, pixels // 2, 128), bf16),
            pltpu.VMEM((4, pixels, 128), f32),
            pltpu.VMEM((2, pixels, 128), f32),
            pltpu.VMEM((GIN, 1280), bf16),
            pltpu.SemaphoreType.DMA((3 + 2 * GROUP,)),
        ],
        us=14,
        name="forward",
    )
    got = lax.all_to_all(rgb, PLANE, 0, 0, tiled=True)
    near, far, factor, small = lax.optimization_barrier((near, far, factor, small))
    squares = [shape((8, CP[0]), bf16)] + [shape((CP[k - 1], CP[k]), bf16) for k in (1, 2, 3)]
    squares += [shape((CP[k], KP[k]), bf16) for k in range(4)]
    squares += [shape((KP[k], KP[k]), bf16) for k in range(4)]
    squares += [shape((KP[k], 128), f32) for k in range(4)]
    squares += [shape((8, 512), f32), shape((8, 128), f32), shape((8, 128), f32)]
    crit_space = -(-((devices - 1) * crit_length // 128 + window(crit_length)) // 8) * 8
    frozen_space = -(-((devices - 1) * frozen_length // 128 + window(frozen_length)) // 8) * 8 + 8
    prepared = call(
        functools.partial(prepare_kernel, crit_length, frozen_length),
        squares,
        small,
        own_row,
        start_rows,
        scratch=[
            pltpu.VMEM((crit_space, 128), f32),
            pltpu.VMEM((frozen_space, 128), f32),
            pltpu.VMEM((frozen_space - 8, 128), f32),
            pltpu.VMEM((128, 128), f32),
        ],
        us=8,
        name="prepare",
    )
    frozen, matrices, right_cols = prepared[:8], prepared[8:12], prepared[12:16]
    left_rows, sigma_rows, share = prepared[16:]
    power_new = jnp.concatenate([left_rows[k, : KS[k]] for k in range(4)])
    dtanh, first_map = call(
        image_grad_kernel,
        [shape((GROUP, 32, PIX), f32), shape((PIX, 8), bf16)],
        scalars,
        share,
        got,
        head_rows,
        sigma_rows,
        *frozen,
        *matrices,
        smem=(0,),
        scratch=[pltpu.VMEM((1024, 1024), bf16)],
        us=8,
        name="image_grad",
    )

    near, far, dtanh = lax.optimization_barrier((near, far, dtanh))
    hid_turned = call(turn_kernel, shape((GIN, pixels), bf16), near, far, us=5, name="turn")
    dtanh_all = lax.all_to_all(dtanh, PLANE, 0, 0, tiled=True)
    grad, dmixed, last_chunk, first_chunk = call(
        weight_grad_kernel,
        [shape((ROWS_FIRST + TAPS * GIN, 128), f32), shape((4, pixels, 128), bf16)]
        + [shape((chunk, 128), f32)] * 2,
        me,
        dtanh_all,
        factor,
        hid_turned,
        color_twice,
        smem=(0,),
        hbm=(2, 3),
        out_hbm=(0, 1, 2, 3),
        scratch=[
            pltpu.VMEM((8, pixels, 256), bf16),
            pltpu.VMEM((4, pixels, 128), f32),
            pltpu.VMEM((GIN, pixels), bf16),
            pltpu.VMEM((ROWS_FIRST + TAPS * GIN, 128), f32),
            pltpu.VMEM((4, pixels, 128), bf16),
            pltpu.SemaphoreType.DMA((GROUP + 1,)),
            pltpu.SemaphoreType.DMA((GROUP,)),
            pltpu.SemaphoreType.DMA((5,)),
        ],
        us=20,
        name="weight_grad",
    )
    steps = []
    if groups == 4:

        def part(k):
            return lax.dynamic_slice_in_dim(grad, jnp.clip(k, 0, 3) * chunk, chunk, axis=0)

        def step(s, a, b):
            if s == 1:
                a, b = part(2 + z) + a, part(z - 2) + b
            down = lax.ppermute(a, "z", [(k, k + 1) for k in range(s + 1)])
            up = lax.ppermute(b, "z", [(3 - k, 2 - k) for k in range(s + 1)])
            return lax.optimization_barrier((down, up))

        first_a, first_b, first_map, dmixed = lax.optimization_barrier(
            (last_chunk, first_chunk, first_map, dmixed)
        )
        steps.append(step(0, first_a, first_b))
    keep, send, color_grad = call(
        hidden_grad_kernel,
        [shape((4, pixels, 128), f32), shape((4, pixels, 128), f32), shape((8, 128), f32)],
        dmixed,
        wide,
        dtanh_all,
        gated,
        scratch=[pltpu.VMEM((2 * PIX, TAPS * 128), bf16), pltpu.VMEM((16, 128), f32)],
        us=18,
        name="hidden_grad",
    )
    aligned = crit_length == 85 * 128
    sent_rows = -(-85 * groups // 8) * 8 if aligned else devices * crit_length // 128
    both = call(
        critic_kernel,
        shape((GROUP if aligned else 1, sent_rows + 40, 128), f32),
        scalars,
        share,
        first_map,
        reals,
        head_rows,
        left_rows,
        sigma_rows,
        *frozen,
        *matrices,
        *right_cols,
        color_grad,
        smem=(0,),
        scratch=[
            pltpu.VMEM((1024, 1024), bf16),
            pltpu.VMEM((SLOTS * PIX, 8), bf16),
            pltpu.VMEM((128, 128), f32),
            pltpu.VMEM((8, 512), f32),
            pltpu.VMEM((devices * crit_length // 128, 128), f32),
        ],
        us=12,
        name="critic",
    )
    if groups == 4:
        got, keep, send, both = lax.optimization_barrier((steps[0], keep, send, both))
        steps.append(step(1, *got))
    keep = keep + swap(send, "c")
    first, second = keep[:, : pixels // 2], keep[:, pixels // 2 :]
    first = first[:2] + swap(first[2:], "y")
    second = second[::2] + swap(second[1::2], "x")
    if not aligned:
        message = both[0, sent_rows:]
        both = both[0, :sent_rows].reshape(groups, GROUP, crit_length)
        both = pad_rows(jnp.swapaxes(both, 0, 1).reshape(GROUP, -1))
        both = jnp.concatenate([both, jnp.broadcast_to(message, (GROUP, 40, 128))], axis=1)
    crit_rows = both.shape[1] - 40
    if groups == 4:
        got, first, second, both = lax.optimization_barrier((steps[1], first, second, both))
        a, b = part(1 + z) + got[0], part(z - 1) + got[1]
        a, b, first, second, both = lax.optimization_barrier((a, b, first, second, both))
        steps.append(step(2, a, b))
    first = first[0] + swap(first[1], "x")
    second = second[0] + swap(second[1], "y")
    dhidden = jnp.concatenate([first, second])
    both = lax.all_to_all(both, PLANE, 0, 0, tiled=True)
    first_grad = call(
        first_grad_kernel,
        shape((ROWS_FIRST, 128), f32),
        me,
        dhidden,
        pre,
        noise_all,
        smem=(0,),
        us=4,
        name="first_grad",
    )
    summed = jnp.sum(both[:, : crit_rows + 32], axis=0)
    message = jnp.concatenate([summed[crit_rows:], both[:, crit_rows + 32 :].reshape(64, 128)])
    both = pad_rows(summed[:crit_rows].reshape(-1)[: groups * crit_length].reshape(groups, -1))
    crit_rows = both.shape[1]
    both = jnp.concatenate([both, jnp.broadcast_to(message, (groups, 96, 128))], axis=1)
    if groups == 4:
        got_first = [lax.ppermute(first_grad, "z", [(k, 0)]) for k in (1, 2, 3)]
        first_sum = first_grad + got_first[0] + got_first[1] + got_first[2]
        reduced = part(z) + steps[2][0] + steps[2][1]
    else:
        first_sum = lax.psum(first_grad, "z")
        reduced = lax.psum_scatter(grad, "z", scatter_dimension=0, tiled=True)
    first_sum = jnp.where(z == 0, first_sum, 0.0)
    reduced = jnp.concatenate([reduced[:ROWS_FIRST] + first_sum, reduced[ROWS_FIRST:]], axis=0)
    reduced = lax.all_to_all(reduced.reshape(GROUP, rows, 128), PLANE, 0, 0, tiled=True)
    if groups == 4:
        rolled = [both[z]]
        for k in (1, 2, 3):
            piece = lax.dynamic_index_in_dim(both, lax.rem(z + k, 4), 0, keepdims=False)
            rolled.append(lax.ppermute(piece, "z", [(i, (i + k) % 4) for i in range(4)]))
        rolled = jnp.stack(rolled)
        both = jnp.stack([rolled[lax.rem(z + 4 - i, 4)] for i in range(4)])
    else:
        both = lax.all_to_all(both, "z", 0, 0, tiled=True)
    both = jnp.sum(both, axis=0)
    crit_reduced = both[:crit_rows].reshape(-1)[:crit_length]
    message = both[crit_rows : crit_rows + 32].reshape(8, 512)
    color_grad = both[crit_rows + 32 :].reshape(GROUP, 8, 128)[:, :3, :64]
    head_reduced = jnp.concatenate(
        [message[k, : KS[k]] for k in range(4)]
        + [jnp.swapaxes(color_grad, 1, 2).reshape(-1)]
    )
    losses = jnp.stack([message[4, 0], message[4, 128]])

    fix = 1.0 - jnp.power(f32(beta_first), update_ordinal[0].astype(f32))
    flat = (8 * rows, 128)
    gen = call(
        adam_kernel,
        [shape(flat, f32)] * 3,
        fix.reshape(1),
        reduced,
        maker_weight_arrays.reshape(flat),
        maker_mean_estimate.reshape(flat),
        maker_variance_estimate.reshape(flat),
        smem=(0,),
        hbm=(1, 2, 3, 4),
        out_hbm=(0, 1, 2),
        scratch=[pltpu.VMEM((GROUP, rows, 128), f32)]
        + [pltpu.VMEM(flat, f32)] * 4
        + [pltpu.SemaphoreType.DMA((16,)), pltpu.SemaphoreType.DMA((12,))],
        us=6,
        name="adam",
    )
    gen = [x.reshape(-1) for x in gen]
    crit = adamw_update(
        judge_weight_arrays, judge_mean_estimate, judge_variance_estimate, crit_reduced, fix
    )
    head = adamw_update(
        output_weight_rows, output_mean_estimate, output_variance_estimate, head_reduced, fix
    )
    return (*gen, *crit, *head, losses, power_new)


def solution(mesh):
    groups = mesh.shape["dp"] * mesh.shape["scale"] // GROUP
    grid = Mesh(mesh.devices.reshape(groups, 2, 2, 2), EVERY)
    split = P(EVERY)
    return jax.shard_map(
        functools.partial(local, groups),
        mesh=grid,
        in_specs=(split,) * 7 + (P(), split, P()) + (split,) * 6 + (P(),) * 3,
        out_specs=(split,) * 6 + (P(),) * 5,
        check_vma=False,
    )
```
